128 devices in a mesh: gz: 16 (over x, y_lo, core), gy: 8 (over y_hi, z).
Axes of the slice: x: 4, y: 4 (y_hi: 2, y_lo: 2; y = y_hi * 2 + y_lo), z: 4, core: 2. Of those that a mesh axis runs over, the one named last changes fastest.
Arguments:
- e_field: float32 [3, 512, 128, 256], P(None, 'gz', 'gy'), may hold values from -6 to 6
- h_field: float32 [3, 512, 128, 256], P(None, 'gz', 'gy'), may hold values from -6 to 6
- e_coef: float32 [512, 128, 256], P('gz', 'gy'), may hold values from 0.14 to 0.55
- e_loss: float32 [512, 128, 256], P('gz', 'gy'), may hold values from 0 to 0.1
- port_cell: int32 [4096], P(('gz', 'gy')), may hold values from 0 to 131071
- port_node: int32 [4096], replicated, may hold values from 0 to 16383
- port_gain: float32 [4096], replicated, may hold values from 0.5 to 2
- diag_blocks: float32 [256, 64, 64], P(('gz', 'gy')), may hold values from -0.5 to 4.5, as said below
- inv_blocks: float32 [256, 64, 64], P(('gz', 'gy')), may hold values from -0.012 to 0.247, as said below
- off_blocks: float32 [256, 4, 64, 64], P(('gz', 'gy')), may hold values from -0.1875 to 0.1875
- off_cols: int32 [256, 4], P(('gz', 'gy')), may hold values from 0 to 255
- volts_init: float32 [16384], P(('gz', 'gy')), may hold values from -6 to 6
Outputs:
- e_final: float32 [3, 512, 128, 256], P(None, 'gz', 'gy')
- h_final: float32 [3, 512, 128, 256], P(None, 'gz', 'gy')
- node_volts: float32 [16384], P(('gz', 'gy'))
The draws below stay inside these ranges and needn't reach their ends.
Inputs may be any that keep to these rules, and one draw needn't show every extreme that they name: `diag_blocks`: 4 times the identity plus independent entries of spread 1/8. `inv_blocks`: 0.235 times the identity plus small independent entries. `port_cell`: ports may share a cell.
All inputs are finite; a program needn't handle non-finite values.
Results may differ from the reference program's by a relative error of at most 0.00019.
Values sent between devices are 32-bit elements; how exact they have to be, the bound alone decides.
No kernel may reach another device: no remote copies, remote signals or barrier semaphores. Data moves between devices by JAX's collectives and lax.ppermute only.
A program may use at most 64 MiB of HBM per device.

```python
import math
import jax
import jax.numpy as jnp
from jax import lax

NX = 256
CY = 16
CZ = 32
STEPS = 5
NEWTON = 2
BS = 64
OFF = 4
PORT_DEV = 32
NZ = 512
NY = 128
NBLK = 256
NODES = 16384
PORTS = 4096
N_GY = 8


def draw_diag_blocks(key, part):
    noise = jnp.clip(jax.random.normal(jax.random.fold_in(key, 11), (NBLK, BS, BS), jnp.float32), -4.0, 4.0)
    return 4.0 * jnp.eye(BS, dtype=jnp.float32)[None] + noise / 8.0


def draw_inv_blocks(key, part):
    noise = jnp.clip(jax.random.normal(jax.random.fold_in(key, 23), (NBLK, BS, BS), jnp.float32), -4.0, 4.0)
    return 0.235 * jnp.eye(BS, dtype=jnp.float32)[None] + noise * 0.003


def plant(result, own_key, low, top_value):
    longest = result.shape.index(max(result.shape))
    spots = []
    for shift in (0, 1):
        where = [jax.random.randint(jax.random.fold_in(own_key, axis), (), 0, length) for axis, length in enumerate(result.shape)]
        where[longest] = (where[longest] + shift) % result.shape[longest]
        spots.append(tuple(where))
    return result.at[spots[0]].set(low).at[spots[1]].set(top_value)


def shard_levels(own_key, shape, cuts, low, high):
    def one(dim, shards_of):
        draws = jax.random.uniform(jax.random.fold_in(jax.random.fold_in(own_key, 6), dim), (shards_of,), jnp.float32, low / len(cuts), high / len(cuts))
        return jnp.repeat(jnp.exp(draws), shape[dim] // shards_of).reshape((-1,) + (1,) * (len(shape) - dim - 1))

    level = one(*cuts[0])
    for cut in cuts[1:]:
        level = level * one(*cut)
    return level


def scatter_about(stream_key, dims, scale, reach, pieces=(), held_as=jnp.bfloat16):
    result = scale * jax.random.normal(stream_key, dims, jnp.float32)
    if pieces:
        result = result * shard_levels(stream_key, dims, pieces, -0.22, 0.18)
    return jnp.clip(result, -reach, reach).astype(held_as)


def setup_inputs(seed: int = 0) -> dict:
    streams_of = jax.random.split(jax.random.key(seed), 13)
    return {
        "e_field": scatter_about(streams_of[0], (3, NZ, NY, NX), 1.0, 6.0, ((1, 16), (2, 8)), jnp.float32),
        "h_field": scatter_about(streams_of[1], (3, NZ, NY, NX), 1.0, 6.0, ((1, 16), (2, 8)), jnp.float32),
        "e_coef": jnp.clip(jnp.exp(math.log(0.55) - 1.3682759 * jax.random.uniform(streams_of[2], (NZ, NY, NX), jnp.float32) ** shard_levels(streams_of[2], (NZ, NY, NX), ((0, 16), (1, 8)), -0.2, 0.2)), 0.14, 0.55),
        "e_loss": jnp.clip(0.1 * jax.random.uniform(streams_of[3], (NZ, NY, NX), jnp.float32) ** shard_levels(streams_of[3], (NZ, NY, NX), ((0, 16), (1, 8)), -0.2, 0.2), 0.0, 0.1),
        "port_cell": plant(jax.random.randint(streams_of[4], (PORTS,), 0, CZ * CY * NX), jax.random.fold_in(streams_of[4], 1), 0, (CZ * CY * NX) - 1).astype(jnp.int32),
        "port_node": plant(jax.random.randint(streams_of[5], (PORTS,), 0, NODES), jax.random.fold_in(streams_of[5], 1), 0, NODES - 1).astype(jnp.int32),
        "port_gain": jnp.clip(jnp.exp(jax.random.uniform(streams_of[6], (PORTS,), jnp.float32, math.log(0.5), math.log(2.0))), 0.5, 2.0),
        "diag_blocks": draw_diag_blocks(jax.random.fold_in(streams_of[12], 71), 0),
        "inv_blocks": draw_inv_blocks(jax.random.fold_in(streams_of[12], 71), 0),
        "off_blocks": scatter_about(streams_of[9], (NBLK, OFF, BS, BS), (4 * BS * OFF) ** -0.5, 0.1875, ((0, 128),), jnp.float32),
        "off_cols": plant(jax.random.randint(streams_of[10], (NBLK, OFF), 0, NBLK), jax.random.fold_in(streams_of[10], 1), 0, NBLK - 1).astype(jnp.int32),
        "volts_init": scatter_about(streams_of[11], (NODES,), 1.0, 6.0, ((0, 128),), jnp.float32),
    }


precise = lax.Precision.HIGHEST


def ahead(field, axis):
    size = field.shape[axis]
    kept = lax.slice_in_dim(field, 1, size, axis=axis)
    blank = jnp.zeros_like(lax.slice_in_dim(field, 0, 1, axis=axis))
    return jnp.concatenate([kept, blank], axis=axis)


def behind(field, axis):
    size = field.shape[axis]
    kept = lax.slice_in_dim(field, 0, size - 1, axis=axis)
    blank = jnp.zeros_like(lax.slice_in_dim(field, 0, 1, axis=axis))
    return jnp.concatenate([blank, kept], axis=axis)


def reference(e_field, h_field, e_coef, e_loss, port_cell, port_node, port_gain, diag_blocks, inv_blocks, off_blocks, off_cols, volts_init):
    device = jnp.arange(PORTS, dtype=jnp.int32) // PORT_DEV
    plane_z = (device // N_GY) * CZ + port_cell // (CY * NX)
    plane_y = (device % N_GY) * CY + (port_cell // NX) % CY
    plane_x = port_cell % NX
    global_cell = ((plane_z * NY + plane_y) * NX + plane_x).astype(jnp.int32)
    coef_flat = e_coef.reshape(-1)
    e_now = e_field
    h_now = h_field
    volts = volts_init
    samples = e_now[2].reshape(-1)[global_cell]
    for step_index in range(STEPS):
        e_x, e_y, e_z = e_now[0], e_now[1], e_now[2]
        curl_x = (ahead(e_z, 1) - e_z) - (ahead(e_y, 0) - e_y)
        curl_y = (ahead(e_x, 0) - e_x) - (ahead(e_z, 2) - e_z)
        curl_z = (ahead(e_y, 2) - e_y) - (ahead(e_x, 1) - e_x)
        h_now = h_now - 0.55 * jnp.stack([curl_x, curl_y, curl_z])
        h_x, h_y, h_z = h_now[0], h_now[1], h_now[2]
        back_x = (h_z - behind(h_z, 1)) - (h_y - behind(h_y, 0))
        back_y = (h_x - behind(h_x, 0)) - (h_z - behind(h_z, 2))
        back_z = (h_y - behind(h_y, 2)) - (h_x - behind(h_x, 1))
        e_now = (1.0 - e_loss) * e_now + e_coef * jnp.stack([back_x, back_y, back_z])
        current = port_gain * (samples - volts[port_node])
        new_z = e_now[2].reshape(-1).at[global_cell].add(-coef_flat[global_cell] * current)
        e_now = jnp.stack([e_now[0], e_now[1], new_z.reshape(NZ, NY, NX)])
        vstart = volts.reshape(NBLK, BS)
        picked = vstart[off_cols]
        offsum = jnp.einsum("jkab,jkb->ja", off_blocks, picked, precision=precise)
        inject = jax.ops.segment_sum(port_gain * samples, port_node, num_segments=NODES).reshape(NBLK, BS)
        target = 4.0 * vstart + inject - offsum
        iterate = vstart
        for newton_round in range(NEWTON):
            resid = jnp.einsum("jab,jb->ja", diag_blocks, iterate, precision=precise) + 0.5 * jnp.tanh(iterate) - target
            iterate = iterate - jnp.einsum("jab,jb->ja", inv_blocks, resid, precision=precise)
        volts = iterate.reshape(-1)
        samples = e_now[2].reshape(-1)[global_cell]
    return e_now, h_now, volts
```

```python
import functools

import jax
import jax.numpy as jnp
from jax import lax
from jax.experimental import pallas as pl
from jax.experimental.pallas import tpu as pltpu
from jax.sharding import PartitionSpec as P

STEPS = 5
NEWTON = 2
BS = 64
NB_DEV = 2
OFF = 4
PORT_DEV = 32
NODE_DEV = NB_DEV * BS
DEPTH = 5
CZ, CY, NX = 32, 16, 256
LAYERS = CZ + 2 * DEPTH
ROWS = LAYERS * CY
OWN_LO, OWN_HI = DEPTH * CY, (DEPTH + CZ) * CY
EDGE = DEPTH * CY
PACK = 8 * EDGE + CY
TALL = 48
ND = 128
REACH = 3 * PORT_DEV

time_step = 0.55
charge_scale = 4.0
diode_weight = 0.5

f32 = jnp.float32
VM = pl.BlockSpec(memory_space=pltpu.VMEM)
SM = pl.BlockSpec(memory_space=pltpu.SMEM)
HBM = pl.BlockSpec(memory_space=pltpu.HBM)
DMA = pltpu.SemaphoreType.DMA


def onchip(shape):
    return pltpu.VMEM(shape, f32)


def keep(value):
    return pltpu.with_memory_space_constraint(value, pltpu.VMEM)


def away(value):
    return pltpu.with_memory_space_constraint(value, pltpu.HBM)


def params():
    return pltpu.CompilerParams(vmem_limit_bytes=8 << 20)


def lanes_of(count, width):
    return lax.broadcasted_iota(jnp.int32, (count, width), 1)


def pick(rows, lane):
    hit = lanes_of(rows.shape[0], rows.shape[1]) == lane
    return jnp.sum(jnp.where(hit, rows, 0.0), axis=1, keepdims=True)


def spread(column, lane, width):
    hit = lanes_of(column.shape[0], width) == lane
    return jnp.where(hit, column, 0.0)


def write_outgoing(out, volts_row, inject_rows, table, first, rows_ref):
    parity = lax.broadcasted_iota(jnp.int32, out.shape, 0) % 2
    out[...] = jnp.where(parity == 0, jnp.broadcast_to(volts_row, out.shape), 0.0)
    rows_ref[...] = inject_rows
    for port in range(PORT_DEV):
        spot = pl.ds(table[first + port] + 1, 1)
        out[spot, :] = out[spot, :] + rows_ref[port : port + 1, :]


def write_edges(up, down, e_xy, e_z, h=None):
    upper = [(e_xy, (0,)), (e_xy, (1,)), (e_z, ())] + ([(h, (0,)), (h, (2,))] if h is not None else [])
    for slot, (source, part) in enumerate(upper):
        for layer in range(LAYERS):
            spot = layer * CY + CY - 1
            up[slot, layer : layer + 1, :] = source[part + (slice(spot, spot + 1), slice(None))]
        up[slot, LAYERS:TALL, :] = jnp.zeros((TALL - LAYERS, NX), f32)
    for slot, (source, part) in enumerate((upper[0], upper[2])):
        for layer in range(LAYERS):
            spot = layer * CY
            down[slot, layer : layer + 1, :] = source[part + (slice(spot, spot + 1), slice(None))]
        down[slot, LAYERS:TALL, :] = jnp.zeros((TALL - LAYERS, NX), f32)


def copier(sems):
    copies = []

    def copy(source, target):
        job = pltpu.make_async_copy(source, target, sems.at[len(copies)])
        job.start()
        copies.append(job)

    return copies, copy


def begin_kernel(
    table, e_in, h_in, coef_in, loss_in, cell_rows, columns, volts, diag, inv, off,
    up, down, out, m_off, m_diag, m_inv, e_z, picked, spread_rows, sems,
):
    copies, copy = copier(sems)
    copy(e_in.at[2], e_z)
    top = pl.ds(CZ * CY - EDGE, EDGE)
    bottom = pl.ds(0, EDGE)
    sources = [e_in.at[k] for k in range(3)] + [h_in.at[k] for k in range(3)] + [coef_in, loss_in]
    for slot, source in enumerate(sources):
        copy(source.at[top], up.at[pl.ds(slot * EDGE, EDGE)])
        copy(source.at[bottom], down.at[pl.ds(slot * EDGE, EDGE)])
    copy(cell_rows, up.at[pl.ds(8 * EDGE, CY)])
    copy(cell_rows, down.at[pl.ds(8 * EDGE, CY)])

    m_diag[...] = jnp.zeros_like(m_diag)
    m_inv[...] = jnp.zeros_like(m_inv)
    for j in range(NB_DEV):
        part = slice(j * BS, (j + 1) * BS)
        m_diag[part, part] = diag[j]
        m_inv[part, part] = inv[j].T
        for k in range(OFF):
            m_off[part, k * BS : (k + 1) * BS] = off[j, k]

    copies[0].wait()
    for port in range(PORT_DEV):
        picked[port : port + 1, :] = e_z[pl.ds(table[port], 1), :]
    gain = columns[0:PORT_DEV, 0:1]
    place = columns[0:PORT_DEV, 1:2].astype(jnp.int32)
    lane = columns[0:PORT_DEV, 2:3].astype(jnp.int32)
    sample = pick(picked[...], place)
    rows = spread(gain * sample, lane, NODE_DEV)
    write_outgoing(out, volts[...], rows, table, PORT_DEV, spread_rows)
    for job in copies[1:]:
        job.wait()


def begin(table, e_in, h_in, coef, loss, cell_rows, columns, volts, diag, inv, off):
    return pl.pallas_call(
        begin_kernel,
        name="begin",
        out_shape=(
            jax.ShapeDtypeStruct((PACK, NX), f32),
            jax.ShapeDtypeStruct((PACK, NX), f32),
            jax.ShapeDtypeStruct((2 * ND, NODE_DEV), f32),
            onchip((NODE_DEV, OFF * BS)),
            onchip((NODE_DEV, NODE_DEV)),
            onchip((NODE_DEV, NODE_DEV)),
        ),
        in_specs=[SM, HBM, HBM, HBM, HBM, HBM, VM, VM, VM, VM, VM],
        out_specs=(HBM, HBM, VM, VM, VM, VM),
        scratch_shapes=[
            pltpu.VMEM((CZ * CY, NX), f32),
            pltpu.VMEM((PORT_DEV, NX), f32),
            pltpu.VMEM((PORT_DEV, NODE_DEV), f32),
            DMA((19,)),
        ],
        compiler_params=params(),
    )(table, *map(away, (e_in, h_in, coef, loss, cell_rows)), columns, volts, diag, inv, off)


def halo_kernel(
    table, columns, lower, upper, e_in, h_in, coef_in, loss_in,
    e_xy, e_z, h, media, up, down, sample, coef, picked, sems,
):
    copies, copy = copier(sems)
    targets = [
        e_xy.at[0], e_xy.at[1], e_z, h.at[0], h.at[1], h.at[2], media.at[0], media.at[1],
    ]
    sources = [e_in.at[k] for k in range(3)] + [h_in.at[k] for k in range(3)] + [coef_in, loss_in]
    own = pl.ds(OWN_LO, CZ * CY)
    for slot, (source, target) in enumerate(zip(sources, targets)):
        part = pl.ds(slot * EDGE, EDGE)
        copy(source, target.at[own])
        copy(lower.at[part], target.at[pl.ds(0, EDGE)])
        copy(upper.at[part], target.at[pl.ds(OWN_HI, EDGE)])
    for job in copies:
        job.wait()

    @pl.loop(0, LAYERS)
    def _(layer):
        part = pl.ds(pl.multiple_of(layer * CY, CY), CY)
        media[1, part, :] = 1.0 - media[1, part, :]

    place = columns[:, 1:2].astype(jnp.int32)
    for port in range(REACH):
        picked[port : port + 1, :] = e_z[pl.ds(table[port], 1), :]
    sample[...] = pick(picked[...], place)
    for port in range(REACH):
        picked[port : port + 1, :] = media[0, pl.ds(table[port], 1), :]
    coef[...] = pick(picked[...], place)
    write_edges(up, down, e_xy, e_z, h)


def halo(table, columns, lower, upper, e_in, h_in, coef, loss):
    return pl.pallas_call(
        halo_kernel,
        name="halo",
        out_shape=(
            onchip((2, ROWS, NX)),
            onchip((ROWS, NX)),
            onchip((3, ROWS, NX)),
            onchip((2, ROWS, NX)),
            jax.ShapeDtypeStruct((5, TALL, NX), f32),
            jax.ShapeDtypeStruct((2, TALL, NX), f32),
            onchip((REACH, 1)),
            onchip((REACH, 1)),
        ),
        in_specs=[SM, VM] + [HBM] * 6,
        out_specs=(VM,) * 8,
        scratch_shapes=[pltpu.VMEM((REACH, NX), f32), DMA((24,))],
        compiler_params=params(),
    )(table, columns, *map(away, (lower, upper, e_in, h_in, coef, loss)))


def field_kernel(step, first, bounds, front, back, near, media, edge_in, e_xy, e_z, h, to_xy, to_z, to_h, edge):
    base = 3 if first else 0
    low_z, low_y = bounds[0], bounds[1]
    lane = lanes_of(CY, NX)
    row = lax.broadcasted_iota(jnp.int32, (CY, NX), 0)
    last_lane, first_lane = lane == NX - 1, lane == 0
    last_row, first_row = row == CY - 1, row == 0

    def next_x(value):
        return jnp.where(last_lane, 0.0, pltpu.roll(value, NX - 1, 1))

    def prior_x(value):
        return jnp.where(first_lane, 0.0, pltpu.roll(value, 1, 1))

    def next_y(value, beyond):
        return jnp.where(last_row, beyond, pltpu.roll(value, CY - 1, 0))

    def prior_y(value, beyond):
        return jnp.where(first_row, beyond, pltpu.roll(value, 1, 0))

    span = pl.ds(0, LAYERS)
    out_x, out_y, out_z = front[0, span, :], front[1, span, :], front[2, span, :]
    out_y_above = front[1, pl.ds(1, LAYERS), :]
    tall_lane = lanes_of(LAYERS, NX)
    out_y_next = jnp.where(tall_lane == NX - 1, 0.0, pltpu.roll(out_y, NX - 1, 1))
    near_x, near_z = near[0, span, :], near[1, span, :]
    edge_x, edge_z = edge_in[base, span, :], edge_in[base + 1, span, :]
    edge[0, span, :] = edge_x - low_y * ((near_z - out_z) - (out_y_above - out_y))
    edge[1, span, :] = edge_z - low_y * ((out_y_next - out_y) - (near_x - out_x))

    def magnetic(layer):
        here = pl.ds(pl.multiple_of(layer * CY, CY), CY)
        above = pl.ds(pl.multiple_of(layer * CY + CY, CY), CY)
        e_x, e_y, e_zz = e_xy[0, here, :], e_xy[1, here, :], e_z[here, :]
        rate = jnp.where(layer < DEPTH, low_z, time_step)
        curl_x = (next_y(e_zz, back[1, pl.ds(layer, 1), :]) - e_zz) - (e_xy[1, above, :] - e_y)
        curl_y = (e_xy[0, above, :] - e_x) - (next_x(e_zz) - e_zz)
        curl_z = (next_x(e_y) - e_y) - (next_y(e_x, back[0, pl.ds(layer, 1), :]) - e_x)
        h_x = h[0, here, :] - rate * curl_x
        h_y = h[1, here, :] - rate * curl_y
        h_z = h[2, here, :] - rate * curl_z
        to_h[0, here, :] = h_x
        to_h[1, here, :] = h_y
        to_h[2, here, :] = h_z
        return here, e_x, e_y, e_zz, h_x, h_y, h_z

    magnetic(step - 1)

    @pl.loop(step, LAYERS - step)
    def _(layer):
        here, e_x, e_y, e_zz, h_x, h_y, h_z = magnetic(layer)
        below = pl.ds(pl.multiple_of(layer * CY - CY, CY), CY)
        coef, kept = media[0, here, :], media[1, here, :]
        back_x = (h_z - prior_y(h_z, edge[1, pl.ds(layer, 1), :])) - (h_y - to_h[1, below, :])
        back_y = (h_x - to_h[0, below, :]) - (h_z - prior_x(h_z))
        back_z = (h_y - prior_x(h_y)) - (h_x - prior_y(h_x, edge[0, pl.ds(layer, 1), :]))
        to_xy[0, here, :] = kept * e_x + coef * back_x
        to_xy[1, here, :] = kept * e_y + coef * back_y
        to_z[here, :] = kept * e_zz + coef * back_z


def field(step, bounds, front, back, near, media, edge, e_xy, e_z, h):
    first = step == 1
    return pl.pallas_call(
        functools.partial(field_kernel, step, first),
        name="field",
        out_shape=(
            onchip((2, ROWS, NX)), onchip((ROWS, NX)), onchip((3, ROWS, NX)), onchip((2, TALL, NX)),
        ),
        in_specs=[SM] + [VM] * 8,
        out_specs=(VM,) * 4,
        compiler_params=params(),
    )(
        bounds, front, back, near, keep(media), front if first else keep(edge),
        keep(e_xy), keep(e_z), keep(h),
    )


NODES_AT, ACTIVE_AT, OFF_AT, SWAP_AT = REACH, 2 * REACH, 3 * REACH, 3 * REACH + NB_DEV * OFF


def solve(arrived, table, volts, m_off, m_diag, m_inv):
    lane = lanes_of(1, NODE_DEV)
    halves = []
    for j in range(NB_DEV):
        pieces = []
        for half in range(OFF // 2):
            total = None
            for side in range(2):
                spot = j * OFF + half * 2 + side
                row = arrived[pl.ds(table[OFF_AT + spot], 1), :]
                row = jnp.where(table[SWAP_AT + spot] == side, row, pltpu.roll(row, BS, 1))
                row = jnp.where((lane < BS) == (side == 0), row, 0.0)
                total = row if total is None else total + row
            pieces.append(jnp.broadcast_to(total, (BS, NODE_DEV)))
        halves.append(pieces)
    first = jnp.concatenate([halves[0][0], halves[1][0]], axis=0)
    second = jnp.concatenate([halves[0][1], halves[1][1]], axis=0)
    product = m_off[:, 0:NODE_DEV] * first + m_off[:, NODE_DEV : 2 * NODE_DEV] * second
    offsum = jnp.sum(product, axis=1, keepdims=True)
    parity = lax.broadcasted_iota(jnp.int32, arrived.shape, 0) % 2
    inject = jnp.sum(jnp.where(parity == 1, arrived[...], 0.0), axis=0, keepdims=True)
    start = volts[...]
    target = charge_scale * start + inject
    diagonal = lax.broadcasted_iota(jnp.int32, (NODE_DEV, NODE_DEV), 0) == lanes_of(NODE_DEV, NODE_DEV)
    iterate = start
    for newton_round in range(NEWTON):
        local = diode_weight * jnp.tanh(iterate) - target
        terms = m_diag[...] * iterate + jnp.where(diagonal, local, 0.0)
        resid = jnp.sum(terms, axis=1, keepdims=True) + offsum
        iterate = iterate - jnp.sum(m_inv[...] * resid, axis=0, keepdims=True)
    return iterate


def apply_ports(table, arrived, columns, sample, coef, e_z, picked, deltas):
    for port in range(REACH):
        picked[port : port + 1, 0:NODE_DEV] = arrived[pl.ds(table[NODES_AT + port], 1), :]
    gain = columns[:, 0:1]
    place = columns[:, 1:2].astype(jnp.int32)
    lane = columns[:, 2:3].astype(jnp.int32)
    near = pick(picked[:, 0:NODE_DEV], lane)
    current = gain * (sample[...] - near)
    deltas[...] = spread(-coef[...] * current, place, NX)

    def add(port):
        spot = pl.ds(table[port], 1)
        e_z[spot, :] = e_z[spot, :] + deltas[port : port + 1, :]

    for port in range(PORT_DEV):
        add(port)
    for port in range(PORT_DEV, REACH):
        pl.when(table[ACTIVE_AT + port] > 0)(functools.partial(add, port))
    return gain, place, lane


def ports_kernel(
    table, arrived, columns, sample, coef, e_xy, e_in, e_z, up, down, picked, deltas,
):
    e_z[...] = e_in[...]
    apply_ports(table, arrived, columns, sample, coef, e_z, picked, deltas)
    write_edges(up, down, e_xy, e_z)


def ports(table, arrived, columns, sample, coef, e_xy, e_z):
    return pl.pallas_call(
        ports_kernel,
        name="ports",
        out_shape=(
            onchip((ROWS, NX)),
            jax.ShapeDtypeStruct((3, TALL, NX), f32),
            jax.ShapeDtypeStruct((2, TALL, NX), f32),
        ),
        in_specs=[SM] + [VM] * 6,
        out_specs=(VM,) * 3,
        scratch_shapes=[pltpu.VMEM((REACH, NX), f32), pltpu.VMEM((REACH, NX), f32)],
        compiler_params=params(),
    )(table, arrived, columns, keep(sample), keep(coef), keep(e_xy), keep(e_z))


def circuit_kernel(
    table, arrived, columns, volts, m_off, m_diag, m_inv, e_z,
    out, volts_out, sample_out, picked, spread_rows,
):
    for port in range(REACH):
        picked[port : port + 1, :] = e_z[pl.ds(table[port], 1), :]
    taken = pick(picked[...], columns[:, 1:2].astype(jnp.int32))
    sample_out[...] = taken
    solved = solve(arrived, table, volts, m_off, m_diag, m_inv)
    volts_out[...] = solved
    own = slice(0, PORT_DEV)
    lane = columns[own, 2:3].astype(jnp.int32)
    rows = spread(columns[own, 0:1] * taken[own], lane, NODE_DEV)
    write_outgoing(out, solved, rows, table, NODES_AT, spread_rows)


def circuit(table, arrived, columns, volts, mats, e_z):
    return pl.pallas_call(
        circuit_kernel,
        name="circuit",
        out_shape=(
            onchip(arrived.shape),
            onchip((1, NODE_DEV)),
            onchip((REACH, 1)),
        ),
        in_specs=[SM] + [VM] * 7,
        out_specs=(VM,) * 3,
        scratch_shapes=[pltpu.VMEM((REACH, NX), f32), pltpu.VMEM((PORT_DEV, NODE_DEV), f32)],
        compiler_params=params(),
    )(table, arrived, columns, volts, *[keep(mat) for mat in mats], keep(e_z))


def finish_kernel(
    table, arrived, columns, sample, coef, volts, m_off, m_diag, m_inv, e_xy, e_in, h,
    e_out, h_out, volts_out, e_z, picked, deltas, sems,
):
    own = pl.ds(OWN_LO, CZ * CY)
    copies, copy = copier(sems)
    for k in range(3):
        copy(h.at[k, own], h_out.at[k])
    for k in range(2):
        copy(e_xy.at[k, own], e_out.at[k])
    e_z[...] = e_in[...]
    apply_ports(table, arrived, columns, sample, coef, e_z, picked, deltas)
    copy(e_z.at[own], e_out.at[2])
    volts_out[...] = solve(arrived, table, volts, m_off, m_diag, m_inv)
    for job in copies:
        job.wait()


def finish(table, arrived, columns, sample, coef, volts, mats, e_xy, e_z, h):
    return pl.pallas_call(
        finish_kernel,
        name="finish",
        out_shape=(
            jax.ShapeDtypeStruct((3, CZ * CY, NX), f32),
            jax.ShapeDtypeStruct((3, CZ * CY, NX), f32),
            jax.ShapeDtypeStruct((1, NODE_DEV), f32),
        ),
        in_specs=[SM] + [VM] * 11,
        out_specs=(HBM, HBM, VM),
        scratch_shapes=[
            pltpu.VMEM((ROWS, NX), f32),
            pltpu.VMEM((REACH, NX), f32),
            pltpu.VMEM((REACH, NX), f32),
            DMA((6,)),
        ],
        compiler_params=params(),
    )(
        table, arrived, columns, keep(sample), keep(coef), volts,
        *[keep(mat) for mat in mats], keep(e_xy), keep(e_z), keep(h),
    )


def shifted(value, axis, steps):
    count = lax.axis_size(axis)
    first, last = (max(0, -steps), min(count, count - steps))
    return lax.ppermute(value, axis, [(source, source + steps) for source in range(first, last)])


def exchange(value):
    return lax.all_to_all(value, ("gz", "gy"), 0, 0, tiled=True)


def body(
    e_field,
    h_field,
    e_coef,
    e_loss,
    port_cell,
    port_node,
    port_gain,
    diag_blocks,
    inv_blocks,
    off_blocks,
    off_cols,
    volts_init,
):
    gz, gy = lax.axis_index("gz"), lax.axis_index("gy")
    n_gz, n_gy = lax.axis_size("gz"), lax.axis_size("gy")
    device = gz * n_gy + gy
    count = n_gz * n_gy * PORT_DEV

    def of_device(table, which):
        start = jnp.clip(which, 0, n_gz * n_gy - 1) * PORT_DEV
        return lax.dynamic_slice_in_dim(table, start, PORT_DEV)

    trio = (device, device - n_gy, device + n_gy)
    nodes = jnp.concatenate([of_device(port_node, which) for which in trio])
    gains = jnp.concatenate([of_device(port_gain, which) for which in trio])
    node_row = 2 * (nodes // NODE_DEV)

    def columns_of(gain, cells, node):
        table = jnp.stack([gain, (cells % NX).astype(f32), (node % NODE_DEV).astype(f32)], axis=1)
        return table

    own = slice(0, PORT_DEV)
    cell_rows = jnp.pad(port_cell.astype(f32)[None], ((0, CY - 1), (0, NX - PORT_DEV)))
    flat = (CZ * CY, NX)
    grids = [array.reshape(array.shape[:-3] + flat) for array in (e_field, h_field, e_coef, e_loss)]
    volts = volts_init.reshape(1, NODE_DEV)
    up, down, out, *mats = begin(
        jnp.concatenate([port_cell // NX, node_row[own]]),
        *grids,
        cell_rows,
        columns_of(gains[own], port_cell, nodes[own]),
        volts,
        diag_blocks,
        inv_blocks,
        off_blocks,
    )
    lower = shifted(up, "gz", 1)
    upper = shifted(down, "gz", -1)
    arrived = exchange(out)
    lower, upper, arrived = lax.optimization_barrier((lower, upper, arrived))

    spot = 8 * EDGE
    cells = jnp.concatenate(
        [
            port_cell,
            lower[spot, 0:PORT_DEV].astype(jnp.int32),
            upper[spot, 0:PORT_DEV].astype(jnp.int32),
        ]
    )
    group = jnp.arange(REACH, dtype=jnp.int32) // PORT_DEV
    offset = jnp.where(group == 0, 0, jnp.where(group == 1, -CZ, CZ))
    layer = cells // (CY * NX) + offset + DEPTH
    exists = (group == 0) | ((group == 1) & (gz > 0)) | ((group == 2) & (gz < n_gz - 1))
    valid = exists & (layer >= 0) & (layer < LAYERS)
    cell_row = jnp.clip(layer, 0, LAYERS - 1) * CY + (cells // NX) % CY
    active = valid.astype(jnp.int32)
    columns = columns_of(jnp.where(valid, gains, 0.0), cells, nodes)
    flat_cols = off_cols.reshape(-1)
    table = jnp.concatenate(
        [cell_row, node_row, active, 2 * (flat_cols // NB_DEV), flat_cols % NB_DEV]
    )
    bounds = jnp.stack(
        [jnp.where(gz > 0, time_step, 0.0), jnp.where(gy > 0, time_step, 0.0)]
    ).astype(f32)

    e_xy, e_z, h, media, up, down, sample, coef = halo(table, columns, lower, upper, *grids)
    edge = None
    for step in range(1, STEPS + 1):
        front = shifted(up, "gy", 1)
        back = shifted(down, "gy", -1)
        if step > 1:
            out, volts, sample = circuit(table, arrived, columns, volts, mats, e_z)
            out, front, back = lax.optimization_barrier((out, front, back))
            arrived = exchange(out)
            arrived, e_z = lax.optimization_barrier((arrived, e_z))
        e_xy, e_z, h, edge = field(step, bounds, front, back, down, media, edge, e_xy, e_z, h)
        shared = (table, arrived, columns, sample, coef)
        if step < STEPS:
            e_z, up, down = ports(*shared, e_xy, e_z)
        else:
            e_end, h_end, volts = finish(*shared, volts, mats, e_xy, e_z, h)
    return e_end.reshape(e_field.shape), h_end.reshape(h_field.shape), volts.reshape(-1)


def solution(mesh):
    placed = (
        P(None, "gz", "gy", None),
        P(None, "gz", "gy", None),
        P("gz", "gy", None),
        P("gz", "gy", None),
        P(("gz", "gy")),
        P(),
        P(),
        P(("gz", "gy"), None, None),
        P(("gz", "gy"), None, None),
        P(("gz", "gy"), None, None, None),
        P(("gz", "gy"), None),
        P(("gz", "gy")),
    )
    return jax.shard_map(
        body,
        mesh=mesh,
        in_specs=placed,
        out_specs=(P(None, "gz", "gy", None), P(None, "gz", "gy", None), P(("gz", "gy"))),
        check_vma=False,
    )
```

```python
import functools

import jax
import jax.numpy as jnp
from jax import lax
from jax.experimental import pallas as pl
from jax.experimental.pallas import tpu as pltpu
from jax.sharding import PartitionSpec as P

STEPS = 5
NEWTON = 2
BS = 64
NB_DEV = 2
OFF = 4
PORT_DEV = 32
ND = 128
NODE_DEV = NB_DEV * BS
DEPTH = 5
CZ, CY, NX = 32, 16, 256
LAYERS = CZ + 2 * DEPTH
PAD = 8
TALL = CY + 2 * PAD
PARTS = 8
STRIP = PARTS * DEPTH
SIDES = ((0, 0), (-1, 0), (1, 0), (0, -1), (-1, -1), (1, -1), (0, 1), (-1, 1), (1, 1))
REACH = len(SIDES) * PORT_DEV
NODES_AT, COUNT_AT, OFF_AT = REACH, 2 * REACH, 2 * REACH + 1
SWAP_AT = OFF_AT + NB_DEV * OFF

time_step = 0.55
charge_scale = 4.0
diode_weight = 0.5

f32 = jnp.float32
VM = pl.BlockSpec(memory_space=pltpu.VMEM)
SM = pl.BlockSpec(memory_space=pltpu.SMEM)
HBM = pl.BlockSpec(memory_space=pltpu.HBM)
DMA = pltpu.SemaphoreType.DMA
CUBE = (LAYERS, TALL, NX)


def onchip(shape):
    return pltpu.VMEM(shape, f32)


def keep(value):
    return pltpu.with_memory_space_constraint(value, pltpu.VMEM)


def away(value):
    return pltpu.with_memory_space_constraint(value, pltpu.HBM)


def params():
    return pltpu.CompilerParams(vmem_limit_bytes=12 << 20)


def lanes_of(count, width):
    return lax.broadcasted_iota(jnp.int32, (count, width), 1)


def pick(rows, lane):
    hit = lanes_of(rows.shape[0], rows.shape[1]) == lane
    return jnp.sum(jnp.where(hit, rows, 0.0), axis=1, keepdims=True)


def spread(column, lane, width):
    hit = lanes_of(column.shape[0], width) == lane
    return jnp.where(hit, column, 0.0)


def columns_at(columns, part):
    block = columns[part, :]
    return block[:, 0:1], block[:, 1:2].astype(jnp.int32), block[:, 2:3].astype(jnp.int32)


def write_outgoing(out, volts_row, inject_rows, table, first, rows_ref):
    parity = lax.broadcasted_iota(jnp.int32, out.shape, 0) % 2
    out[...] = jnp.where(parity == 0, jnp.broadcast_to(volts_row, out.shape), 0.0)
    rows_ref[...] = inject_rows
    for port in range(PORT_DEV):
        spot = pl.ds(table[first + port] + 1, 1)
        out[spot, :] = out[spot, :] + rows_ref[port : port + 1, :]


def copier(sems):
    copies = []

    def copy(source, target):
        job = pltpu.make_async_copy(source, target, sems.at[len(copies)])
        job.start()
        copies.append(job)

    return copies, copy


def strip_of(block, rows):
    return jnp.concatenate([block(part)[rows] for part in range(PARTS)], axis=0)


def begin_kernel(
    table, e_in, h_in, coef_in, loss_in, cell_rows, columns, volts, diag, inv, off,
    up, down, front, back, out, m_off, m_diag, m_inv, fields, picked, spread_rows, sems,
):
    copies, copy = copier(sems)
    sources = [e_in.at[k] for k in range(3)] + [h_in.at[k] for k in range(3)] + [coef_in, loss_in]
    for part in (2, 0, 1, 3, 4, 5, 6, 7):
        copy(sources[part], fields.at[part])
    for part, source in enumerate(sources):
        to = pl.ds(part * DEPTH, DEPTH)
        copy(source.at[pl.ds(CZ - DEPTH, DEPTH)], up.at[to])
        copy(source.at[pl.ds(0, DEPTH)], down.at[to])
    copy(cell_rows, up.at[PARTS * DEPTH])
    copy(cell_rows, down.at[PARTS * DEPTH])

    m_diag[...] = jnp.zeros_like(m_diag)
    m_inv[...] = jnp.zeros_like(m_inv)
    for j in range(NB_DEV):
        part = slice(j * BS, (j + 1) * BS)
        m_diag[part, part] = diag[j]
        m_inv[part, part] = inv[j].T
        for k in range(OFF):
            m_off[part, k * BS : (k + 1) * BS] = off[j, k]

    copies[0].wait()
    for port in range(PORT_DEV):
        spot = table[port]
        picked[port : port + 1, :] = fields[2, spot // CY, pl.ds(spot % CY, 1), :]
    gain, place, lane = columns_at(columns, slice(0, PORT_DEV))
    sample = pick(picked[...], place)
    rows = spread(gain * sample, lane, NODE_DEV)
    write_outgoing(out, volts[...], rows, table, PORT_DEV, spread_rows)
    for job in copies[1:8]:
        job.wait()

    @pl.loop(0, CZ)
    def _(layer):
        to = pl.ds(pl.multiple_of(layer * STRIP, 8), STRIP)
        front[to, :] = strip_of(lambda part: fields[part, layer, 8:CY, :], slice(8 - DEPTH, 8))
        back[to, :] = strip_of(lambda part: fields[part, layer, 0:8, :], slice(0, DEPTH))

    front[CZ * STRIP :, :] = cell_rows[0:8, :]
    back[CZ * STRIP :, :] = cell_rows[0:8, :]
    for job in copies[8:]:
        job.wait()


def begin(table, e_in, h_in, coef, loss, cell_rows, columns, volts, diag, inv, off):
    return pl.pallas_call(
        begin_kernel,
        name="begin",
        out_shape=(
            jax.ShapeDtypeStruct((PARTS * DEPTH + 1, CY, NX), f32),
            jax.ShapeDtypeStruct((PARTS * DEPTH + 1, CY, NX), f32),
            jax.ShapeDtypeStruct((CZ * STRIP + 8, NX), f32),
            jax.ShapeDtypeStruct((CZ * STRIP + 8, NX), f32),
            jax.ShapeDtypeStruct((2 * ND, NODE_DEV), f32),
            onchip((NODE_DEV, OFF * BS)),
            onchip((NODE_DEV, NODE_DEV)),
            onchip((NODE_DEV, NODE_DEV)),
        ),
        in_specs=[SM, HBM, HBM, HBM, HBM, VM, VM, VM, VM, VM, VM],
        out_specs=(HBM, HBM, VM, VM, VM, VM, VM, VM),
        scratch_shapes=[
            pltpu.VMEM((PARTS, CZ, CY, NX), f32),
            pltpu.VMEM((PORT_DEV, NX), f32),
            pltpu.VMEM((PORT_DEV, NODE_DEV), f32),
            DMA((26,)),
        ],
        compiler_params=params(),
    )(table, *map(away, (e_in, h_in, coef, loss)), cell_rows, columns, volts, diag, inv, off)


def corners_kernel(lower, upper, front, back):
    for side, source in enumerate((lower, upper)):
        for layer in range(DEPTH):
            to = pl.ds((side * DEPTH + layer) * STRIP, STRIP)
            front[to, :] = strip_of(
                lambda part: source[part * DEPTH + layer, 8:CY, :], slice(8 - DEPTH, 8)
            )
            back[to, :] = strip_of(
                lambda part: source[part * DEPTH + layer, 0:8, :], slice(0, DEPTH)
            )
    row = lax.broadcasted_iota(jnp.int32, (8, NX), 0)
    last = PARTS * DEPTH
    cells = jnp.where(row == 0, lower[last, 0:8, :], pltpu.roll(upper[last, 0:8, :], 1, 0))
    front[2 * DEPTH * STRIP :, :] = cells
    back[2 * DEPTH * STRIP :, :] = cells


def corners(lower, upper):
    shape = jax.ShapeDtypeStruct((2 * DEPTH * STRIP + 8, NX), f32)
    return pl.pallas_call(
        corners_kernel,
        name="corners",
        out_shape=(shape, shape),
        in_specs=[VM, VM],
        out_specs=(VM, VM),
        compiler_params=params(),
    )(lower, upper)


def halo_kernel(
    spots, active, node_row, columns, lower, upper, before, after, before_ends, after_ends,
    e_in, h_in, coef_in, loss_in,
    e_xy, e_z, h, media, found, columns_out, sample, coef, picked, sems,
):
    copies, copy = copier(sems)
    targets = [
        e_xy.at[0], e_xy.at[1], e_z, h.at[0], h.at[1], h.at[2], media.at[0], media.at[1],
    ]
    sources = [e_in.at[k] for k in range(3)] + [h_in.at[k] for k in range(3)] + [coef_in, loss_in]
    middle = pl.ds(PAD, CY)
    for part, (source, target) in enumerate(zip(sources, targets)):
        given = pl.ds(part * DEPTH, DEPTH)
        copy(source, target.at[pl.ds(DEPTH, CZ), middle])
        copy(lower.at[given], target.at[pl.ds(0, DEPTH), middle])
        copy(upper.at[given], target.at[pl.ds(DEPTH + CZ, DEPTH), middle])

    blank = jnp.zeros((8 - DEPTH, NX), f32)

    def unpack(ahead, behind, at, layer):
        given = pl.ds(pl.multiple_of(at * STRIP, 8), STRIP)
        low, high = ahead[given, :], behind[given, :]
        for part, target in enumerate(targets):
            rows = slice(part * DEPTH, (part + 1) * DEPTH)
            target[layer, 0:PAD, :] = jnp.concatenate([blank, low[rows]], axis=0)
            target[layer, PAD + CY : TALL, :] = jnp.concatenate([high[rows], blank], axis=0)

    @pl.loop(0, CZ)
    def _(layer):
        unpack(before, after, layer, layer + DEPTH)

    @pl.loop(0, 2 * DEPTH)
    def _(end):
        unpack(before_ends, after_ends, end, jnp.where(end < DEPTH, end, end + CZ))

    @pl.loop(0, REACH)
    def _(port):
        found[port] = PAD
        found[NODES_AT + port] = 0

    columns_out[...] = jnp.zeros_like(columns_out)

    def place_port(port, count):
        @pl.when(active[port] > 0)
        def _():
            found[count] = spots[port]
            found[NODES_AT + count] = node_row[port]
            columns_out[pl.ds(count, 1), :] = columns[pl.ds(port, 1), :]

        return count + active[port]

    count = lax.fori_loop(0, REACH, place_port, 0)
    groups = (count + PORT_DEV - 1) // PORT_DEV
    found[COUNT_AT] = groups
    for item in range(2 * NB_DEV * OFF):
        found[OFF_AT + item] = node_row[REACH + item]

    for job in copies:
        job.wait()

    @pl.loop(0, LAYERS)
    def _(layer):
        media[1, layer] = 1.0 - media[1, layer]

    @pl.loop(0, groups)
    def _(group):
        part = pl.ds(pl.multiple_of(group * PORT_DEV, PORT_DEV), PORT_DEV)
        _, place, _ = columns_at(columns_out, part)
        sample[part, :] = gather_cells(e_z, found, group, place, picked)
        coef[part, :] = gather_cells(media.at[0], found, group, place, picked)


def gather_cells(source, found, group, place, picked):
    for port in range(PORT_DEV):
        spot = found[group * PORT_DEV + port]
        picked[port : port + 1, :] = source[spot // TALL, pl.ds(spot % TALL, 1), :]
    return pick(picked[...], place)


def halo(spots, active, node_row, columns, lower, upper, sides, e_in, h_in, coef, loss):
    return pl.pallas_call(
        halo_kernel,
        name="halo",
        out_shape=(
            onchip((2,) + CUBE),
            onchip(CUBE),
            onchip((3,) + CUBE),
            onchip((2,) + CUBE),
            jax.ShapeDtypeStruct((SWAP_AT + NB_DEV * OFF,), jnp.int32),
            onchip(columns.shape),
            onchip((REACH, 1)),
            onchip((REACH, 1)),
        ),
        in_specs=[SM, SM, SM, VM, HBM, HBM, VM, VM, VM, VM] + [HBM] * 4,
        out_specs=(VM, VM, VM, VM, SM, VM, VM, VM),
        scratch_shapes=[pltpu.VMEM((PORT_DEV, NX), f32), DMA((24,))],
        compiler_params=params(),
    )(
        spots, active, node_row, columns, away(lower), away(upper), *sides,
        *map(away, (e_in, h_in, coef, loss)),
    )


def field_kernel(step, bounds, media, e_xy, e_z, h, to_xy, to_z, to_h):
    low_z, low_y = bounds[0], bounds[1]
    lane = lanes_of(TALL, NX)
    last_lane, first_lane = lane == NX - 1, lane == 0
    row = lax.broadcasted_iota(jnp.int32, (TALL, NX), 0)
    rate_rows = jnp.where(row < PAD, low_y, time_step)

    def next_x(value):
        return jnp.where(last_lane, 0.0, pltpu.roll(value, NX - 1, 1))

    def prior_x(value):
        return jnp.where(first_lane, 0.0, pltpu.roll(value, 1, 1))

    def next_y(value):
        return pltpu.roll(value, TALL - 1, 0)

    def prior_y(value):
        return pltpu.roll(value, 1, 0)

    def magnetic(layer):
        e_x, e_y, e_zz = e_xy[0, layer], e_xy[1, layer], e_z[layer]
        rate = rate_rows * jnp.where(layer < DEPTH, low_z, 1.0)
        curl_x = (next_y(e_zz) - e_zz) - (e_xy[1, layer + 1] - e_y)
        curl_y = (e_xy[0, layer + 1] - e_x) - (next_x(e_zz) - e_zz)
        curl_z = (next_x(e_y) - e_y) - (next_y(e_x) - e_x)
        return (h[0, layer] - rate * curl_x, h[1, layer] - rate * curl_y, h[2, layer] - rate * curl_z)

    def electric(layer):
        h_x, h_y, h_z = to_h[0, layer], to_h[1, layer], to_h[2, layer]
        coef, kept = media[0, layer], media[1, layer]
        back_x = (h_z - prior_y(h_z)) - (h_y - to_h[1, layer - 1])
        back_y = (h_x - to_h[0, layer - 1]) - (h_z - prior_x(h_z))
        back_z = (h_y - prior_x(h_y)) - (h_x - prior_y(h_x))
        return (
            kept * e_xy[0, layer] + coef * back_x,
            kept * e_xy[1, layer] + coef * back_y,
            kept * e_z[layer] + coef * back_z,
        )

    def put_h(layer, values):
        to_h[0, layer], to_h[1, layer], to_h[2, layer] = values

    def put_e(layer, values):
        to_xy[0, layer], to_xy[1, layer], to_z[layer] = values

    put_h(step - 1, magnetic(step - 1))
    put_h(step, magnetic(step))
    last = LAYERS - step - 1

    @pl.loop(step, last)
    def _(layer):
        electric_values = electric(layer)
        magnetic_values = magnetic(layer + 1)
        put_e(layer, electric_values)
        put_h(layer + 1, magnetic_values)

    put_e(last, electric(last))


def field(step, bounds, media, e_xy, e_z, h):
    return pl.pallas_call(
        functools.partial(field_kernel, step),
        name="field",
        out_shape=(onchip((2,) + CUBE), onchip(CUBE), onchip((3,) + CUBE)),
        in_specs=[SM] + [VM] * 4,
        out_specs=(VM,) * 3,
        compiler_params=params(),
    )(bounds, keep(media), keep(e_xy), keep(e_z), keep(h))


def solve(arrived, table, volts, m_off, m_diag, m_inv):
    lane = lanes_of(1, NODE_DEV)
    halves = []
    for j in range(NB_DEV):
        pieces = []
        for half in range(OFF // 2):
            total = None
            for side in range(2):
                spot = j * OFF + half * 2 + side
                row = arrived[pl.ds(table[OFF_AT + spot], 1), :]
                row = jnp.where(table[SWAP_AT + spot] == side, row, pltpu.roll(row, BS, 1))
                row = jnp.where((lane < BS) == (side == 0), row, 0.0)
                total = row if total is None else total + row
            pieces.append(jnp.broadcast_to(total, (BS, NODE_DEV)))
        halves.append(pieces)
    first = jnp.concatenate([halves[0][0], halves[1][0]], axis=0)
    second = jnp.concatenate([halves[0][1], halves[1][1]], axis=0)
    product = m_off[:, 0:NODE_DEV] * first + m_off[:, NODE_DEV : 2 * NODE_DEV] * second
    offsum = jnp.sum(product, axis=1, keepdims=True)
    parity = lax.broadcasted_iota(jnp.int32, arrived.shape, 0) % 2
    inject = jnp.sum(jnp.where(parity == 1, arrived[...], 0.0), axis=0, keepdims=True)
    start = volts[...]
    target = charge_scale * start + inject
    diagonal = lax.broadcasted_iota(jnp.int32, (NODE_DEV, NODE_DEV), 0) == lanes_of(NODE_DEV, NODE_DEV)
    iterate = start
    for newton_round in range(NEWTON):
        local = diode_weight * jnp.tanh(iterate) - target
        terms = m_diag[...] * iterate + jnp.where(diagonal, local, 0.0)
        resid = jnp.sum(terms, axis=1, keepdims=True) + offsum
        iterate = iterate - jnp.sum(m_inv[...] * resid, axis=0, keepdims=True)
    return iterate


def apply_ports(table, arrived, columns, sample, coef, e_z, near_rows, deltas):
    @pl.loop(0, table[COUNT_AT])
    def _(group):
        first = group * PORT_DEV
        part = pl.ds(pl.multiple_of(first, PORT_DEV), PORT_DEV)
        for port in range(PORT_DEV):
            near_rows[port : port + 1, :] = arrived[pl.ds(table[NODES_AT + first + port], 1), :]
        gain, place, lane = columns_at(columns, part)
        current = gain * (sample[part, :] - pick(near_rows[...], lane))
        deltas[...] = spread(-coef[part, :] * current, place, NX)
        for port in range(PORT_DEV):
            spot = table[first + port]
            layer, row = spot // TALL, pl.ds(spot % TALL, 1)
            e_z[layer, row, :] = e_z[layer, row, :] + deltas[port : port + 1, :]


def circuit_kernel(
    table, arrived, columns, sample, coef, volts, m_off, m_diag, m_inv, e_in,
    e_z, out, volts_out, sample_out, near_rows, deltas, picked, spread_rows,
):
    e_z[...] = e_in[...]
    apply_ports(table, arrived, columns, sample, coef, e_z, near_rows, deltas)

    @pl.loop(0, table[COUNT_AT])
    def _(group):
        part = pl.ds(pl.multiple_of(group * PORT_DEV, PORT_DEV), PORT_DEV)
        _, place, _ = columns_at(columns, part)
        sample_out[part, :] = gather_cells(e_z, table, group, place, picked)

    solved = solve(arrived, table, volts, m_off, m_diag, m_inv)
    volts_out[...] = solved
    own = slice(0, PORT_DEV)
    gain, _, lane = columns_at(columns, own)
    rows = spread(gain * sample_out[own, :], lane, NODE_DEV)
    write_outgoing(out, solved, rows, table, NODES_AT, spread_rows)


def circuit(table, arrived, columns, sample, coef, volts, mats, e_z):
    return pl.pallas_call(
        circuit_kernel,
        name="circuit",
        out_shape=(
            onchip(CUBE),
            onchip(arrived.shape),
            onchip((1, NODE_DEV)),
            onchip((REACH, 1)),
        ),
        in_specs=[SM] + [VM] * 9,
        out_specs=(VM,) * 4,
        scratch_shapes=[
            pltpu.VMEM((PORT_DEV, NODE_DEV), f32),
            pltpu.VMEM((PORT_DEV, NX), f32),
            pltpu.VMEM((PORT_DEV, NX), f32),
            pltpu.VMEM((PORT_DEV, NODE_DEV), f32),
        ],
        compiler_params=params(),
    )(
        table, arrived, keep(columns), keep(sample), keep(coef), volts,
        *[keep(mat) for mat in mats], keep(e_z),
    )


def finish_kernel(
    table, arrived, columns, sample, coef, volts, m_off, m_diag, m_inv, e_xy, e_in, h,
    e_out, h_out, volts_out, e_z, near_rows, deltas, sems,
):
    copies, copy = copier(sems)
    layers, rows = pl.ds(DEPTH, CZ), pl.ds(PAD, CY)
    for k in range(3):
        copy(h.at[k, layers, rows], h_out.at[k])
    for k in range(2):
        copy(e_xy.at[k, layers, rows], e_out.at[k])
    e_z[...] = e_in[...]
    apply_ports(table, arrived, columns, sample, coef, e_z, near_rows, deltas)
    copy(e_z.at[layers, rows], e_out.at[2])
    volts_out[...] = solve(arrived, table, volts, m_off, m_diag, m_inv)
    for job in copies:
        job.wait()


def finish(table, arrived, columns, sample, coef, volts, mats, e_xy, e_z, h):
    return pl.pallas_call(
        finish_kernel,
        name="finish",
        out_shape=(
            jax.ShapeDtypeStruct((3, CZ, CY, NX), f32),
            jax.ShapeDtypeStruct((3, CZ, CY, NX), f32),
            jax.ShapeDtypeStruct((1, NODE_DEV), f32),
        ),
        in_specs=[SM] + [VM] * 11,
        out_specs=(HBM, HBM, VM),
        scratch_shapes=[
            pltpu.VMEM(CUBE, f32),
            pltpu.VMEM((PORT_DEV, NODE_DEV), f32),
            pltpu.VMEM((PORT_DEV, NX), f32),
            DMA((6,)),
        ],
        compiler_params=params(),
    )(
        table, arrived, keep(columns), keep(sample), keep(coef), volts,
        *[keep(mat) for mat in mats], keep(e_xy), keep(e_z), keep(h),
    )


def shifted(value, axis, steps):
    count = lax.axis_size(axis)
    first, last = (max(0, -steps), min(count, count - steps))
    return lax.ppermute(value, axis, [(source, source + steps) for source in range(first, last)])


def exchange(value):
    return lax.all_to_all(value, ("gz", "gy"), 0, 0, tiled=True)


def body(
    e_field,
    h_field,
    e_coef,
    e_loss,
    port_cell,
    port_node,
    port_gain,
    diag_blocks,
    inv_blocks,
    off_blocks,
    off_cols,
    volts_init,
):
    gz, gy = lax.axis_index("gz"), lax.axis_index("gy")
    n_gz, n_gy = lax.axis_size("gz"), lax.axis_size("gy")
    device = gz * n_gy + gy
    own = slice(0, PORT_DEV)

    def columns_of(gain, cells, node):
        return jnp.stack([gain, (cells % NX).astype(f32), (node % NODE_DEV).astype(f32)], axis=1)

    own_node = lax.dynamic_slice_in_dim(port_node, device * PORT_DEV, PORT_DEV)
    own_gain = lax.dynamic_slice_in_dim(port_gain, device * PORT_DEV, PORT_DEV)
    cell_rows = jnp.pad(port_cell.astype(f32)[None], ((0, CY - 1), (0, NX - PORT_DEV)))
    grids = (e_field, h_field, e_coef, e_loss)
    volts = volts_init.reshape(1, NODE_DEV)
    up, down, front, back, out, *mats = begin(
        jnp.concatenate([port_cell // NX, 2 * (own_node // NODE_DEV)]),
        *grids,
        cell_rows,
        columns_of(own_gain, port_cell, own_node),
        volts,
        diag_blocks,
        inv_blocks,
        off_blocks,
    )
    before = shifted(front, "gy", 1)
    after = shifted(back, "gy", -1)
    lower = shifted(up, "gz", 1)
    upper = shifted(down, "gz", -1)
    arrived = exchange(out)
    front_ends, back_ends = corners(lower, upper)
    before_ends = shifted(front_ends, "gy", 1)
    after_ends = shifted(back_ends, "gy", -1)
    sides = (before, after, before_ends, after_ends)

    def cells_in(value, row):
        return value[row, own].astype(jnp.int32)

    last, end = CZ * STRIP, 2 * DEPTH * STRIP
    cells = jnp.stack(
        [
            port_cell,
            lower[PARTS * DEPTH, 0, own].astype(jnp.int32),
            upper[PARTS * DEPTH, 0, own].astype(jnp.int32),
            cells_in(before, last),
            cells_in(before_ends, end),
            cells_in(before_ends, end + 1),
            cells_in(after, last),
            cells_in(after_ends, end),
            cells_in(after_ends, end + 1),
        ]
    )
    shift_z = jnp.array([side[0] for side in SIDES], jnp.int32)[:, None]
    shift_y = jnp.array([side[1] for side in SIDES], jnp.int32)[:, None]
    at_z, at_y = gz + shift_z, gy + shift_y
    exists = (at_z >= 0) & (at_z < n_gz) & (at_y >= 0) & (at_y < n_gy)
    ids = jnp.where(exists, at_z * n_gy + at_y, 0)[:, 0]
    nodes = port_node.reshape(-1, PORT_DEV)[ids].reshape(-1)
    gains = port_gain.reshape(-1, PORT_DEV)[ids].reshape(-1)
    layer = cells // (CY * NX) + shift_z * CZ + DEPTH
    row = (cells // NX) % CY + shift_y * CY + PAD
    inside = (layer >= 1) & (layer < LAYERS - 1) & (row >= PAD - DEPTH + 1) & (row < PAD + CY + DEPTH - 1)
    valid = exists & inside
    spots = jnp.where(valid, layer * TALL + row, PAD).reshape(-1)
    active = valid.astype(jnp.int32).reshape(-1)
    columns = columns_of(gains, cells.reshape(-1), nodes)
    flat_cols = off_cols.reshape(-1)
    node_row = jnp.concatenate(
        [2 * (nodes // NODE_DEV), 2 * (flat_cols // NB_DEV), flat_cols % NB_DEV]
    )
    bounds = jnp.stack([jnp.where(gz > 0, 1.0, 0.0), jnp.where(gy > 0, time_step, 0.0)]).astype(f32)

    e_xy, e_z, h, media, table, columns, sample, coef = halo(
        spots, active, node_row, columns, lower, upper, sides, *grids
    )
    for step in range(1, STEPS + 1):
        if step > 1:
            arrived = exchange(out)
            arrived, e_z = lax.optimization_barrier((arrived, e_z))
        e_xy, e_z, h = field(step, bounds, media, e_xy, e_z, h)
        shared = (table, arrived, columns, sample, coef, volts, mats)
        if step < STEPS:
            e_z, out, volts, sample = circuit(*shared, e_z)
        else:
            e_end, h_end, volts = finish(*shared, e_xy, e_z, h)
    return e_end, h_end, volts.reshape(-1)


def solution(mesh):
    placed = (
        P(None, "gz", "gy", None),
        P(None, "gz", "gy", None),
        P("gz", "gy", None),
        P("gz", "gy", None),
        P(("gz", "gy")),
        P(),
        P(),
        P(("gz", "gy"), None, None),
        P(("gz", "gy"), None, None),
        P(("gz", "gy"), None, None, None),
        P(("gz", "gy"), None),
        P(("gz", "gy")),
    )
    return jax.shard_map(
        body,
        mesh=mesh,
        in_specs=placed,
        out_specs=(P(None, "gz", "gy", None), P(None, "gz", "gy", None), P(("gz", "gy"))),
        check_vma=False,
    )
```

```python
import functools

import jax
import jax.numpy as jnp
from jax import lax
from jax.experimental import pallas as pl
from jax.experimental.pallas import tpu as pltpu
from jax.sharding import PartitionSpec as P

STEPS = 5
NEWTON = 2
BS = 64
NB_DEV = 2
OFF = 4
PORT_DEV = 32
ND = 128
NODE_DEV = NB_DEV * BS
DEPTH = 5
CZ, CY, NX = 32, 16, 256
LAYERS = CZ + 2 * DEPTH
PAD = 8
TALL = CY + 2 * PAD
PARTS = 8
STRIP = PARTS * DEPTH
SIDES = ((0, 0), (-1, 0), (1, 0), (0, -1), (-1, -1), (1, -1), (0, 1), (-1, 1), (1, 1))
REACH = len(SIDES) * PORT_DEV
NODES_AT, COUNT_AT, OFF_AT = REACH, 2 * REACH, 2 * REACH + 1
SWAP_AT = OFF_AT + NB_DEV * OFF

time_step = 0.55
charge_scale = 4.0
diode_weight = 0.5

f32 = jnp.float32
VM = pl.BlockSpec(memory_space=pltpu.VMEM)
SM = pl.BlockSpec(memory_space=pltpu.SMEM)
HBM = pl.BlockSpec(memory_space=pltpu.HBM)
DMA = pltpu.SemaphoreType.DMA
CUBE = (LAYERS, TALL, NX)


def onchip(shape):
    return pltpu.VMEM(shape, f32)


def keep(value):
    return pltpu.with_memory_space_constraint(value, pltpu.VMEM)


def away(value):
    return pltpu.with_memory_space_constraint(value, pltpu.HBM)


def params():
    return pltpu.CompilerParams(vmem_limit_bytes=12 << 20)


def lanes_of(count, width):
    return lax.broadcasted_iota(jnp.int32, (count, width), 1)


def pick(rows, lane):
    hit = lanes_of(rows.shape[0], rows.shape[1]) == lane
    return jnp.sum(jnp.where(hit, rows, 0.0), axis=1, keepdims=True)


def spread(column, lane, width):
    hit = lanes_of(column.shape[0], width) == lane
    return jnp.where(hit, column, 0.0)


def columns_at(columns, part):
    block = columns[part, :]
    return block[:, 0:1], block[:, 1:2].astype(jnp.int32), block[:, 2:3].astype(jnp.int32)


def row_kind(shape, stride):
    return lax.broadcasted_iota(jnp.int32, shape, 0) % stride


def add_rows(out, stride, devices, rows_ref):
    for port, device in enumerate(devices):
        spot = pl.ds(device * stride + 1, 1)
        out[spot, :] = out[spot, :] + rows_ref[port : port + 1, :]


def copier(sems):
    copies = []

    def copy(source, target):
        job = pltpu.make_async_copy(source, target, sems.at[len(copies)])
        job.start()
        copies.append(job)

    return copies, copy


def begin_kernel(
    n_gy, cells, nodes, gains, e_in, h_in, coef_in, loss_in, cell_row, volts,
    up, down, front, back, out, fields, picked, hits, rows_ref, sems,
):
    copies, copy = copier(sems)
    sources = [e_in.at[k] for k in range(3)] + [h_in.at[k] for k in range(3)] + [coef_in, loss_in]
    for part in (2, 0, 1, 3, 4, 5, 6, 7):
        copy(sources[part], fields.at[part])
    for part, source in enumerate(sources):
        to = pl.ds(part * DEPTH, DEPTH)
        copy(source.at[pl.ds(CZ - DEPTH, DEPTH)], up.at[to])
        copy(source.at[pl.ds(0, DEPTH)], down.at[to])

    first = (lax.axis_index("gz") * n_gy + lax.axis_index("gy")) * PORT_DEV
    wide, narrow = lanes_of(1, NX), lanes_of(1, NODE_DEV)
    own_nodes = [nodes[first + port] for port in range(PORT_DEV)]
    for port, node in enumerate(own_nodes):
        hits[port : port + 1, :] = jnp.where(narrow == node % NODE_DEV, 1.0, 0.0)
    kind = row_kind(out.shape, 4)
    rows_ref[0:1, :] = jnp.zeros((1, NODE_DEV), f32)
    rows_ref[0:1, 0:PORT_DEV] = cell_row[...].astype(f32)
    out[...] = jnp.where(kind == 0, volts[...], jnp.where(kind == 2, rows_ref[0:1, :], 0.0))

    copies[0].wait()
    for port in range(PORT_DEV):
        cell = cells[port]
        line = cell // NX
        value = fields[2, line // CY, pl.ds(line % CY, 1), :] * gains[first + port]
        picked[port : port + 1, :] = jnp.where(wide == cell % NX, value, 0.0)
    rows_ref[...] = hits[...] * jnp.sum(picked[...], axis=1, keepdims=True)
    add_rows(out, 4, [node // NODE_DEV for node in own_nodes], rows_ref)
    for job in copies[1:8]:
        job.wait()

    @pl.loop(0, CZ)
    def _(layer):
        for part in range(PARTS):
            to = slice(part * DEPTH, (part + 1) * DEPTH)
            front[layer, to, :] = fields[part, layer, CY - DEPTH : CY, :]
            back[layer, to, :] = fields[part, layer, 0:DEPTH, :]

    for job in copies[8:]:
        job.wait()


def begin(n_gy, cells, nodes, gains, e_in, h_in, coef, loss, volts):
    thick = jax.ShapeDtypeStruct((PARTS * DEPTH, CY, NX), f32)
    strips = jax.ShapeDtypeStruct((CZ, STRIP, NX), f32)
    return pl.pallas_call(
        functools.partial(begin_kernel, n_gy),
        name="begin",
        out_shape=(thick, thick, strips, strips, jax.ShapeDtypeStruct((4 * ND, NODE_DEV), f32)),
        in_specs=[SM, SM, SM, HBM, HBM, HBM, HBM, VM, VM],
        out_specs=(HBM, HBM, VM, VM, VM),
        scratch_shapes=[
            pltpu.VMEM((PARTS, CZ, CY, NX), f32),
            pltpu.VMEM((PORT_DEV, NX), f32),
            pltpu.VMEM((PORT_DEV, NODE_DEV), f32),
            pltpu.VMEM((PORT_DEV, NODE_DEV), f32),
            DMA((24,)),
        ],
        compiler_params=params(),
    )(cells, nodes, gains, *map(away, (e_in, h_in, coef, loss)), cells.reshape(1, -1), volts)


def matrices_kernel(diag, inv, off, m_off, m_diag, m_inv):
    m_diag[...] = jnp.zeros_like(m_diag)
    m_inv[...] = jnp.zeros_like(m_inv)
    for j in range(NB_DEV):
        part = slice(j * BS, (j + 1) * BS)
        m_diag[part, part] = diag[j]
        m_inv[part, part] = inv[j].T
        for k in range(OFF):
            m_off[part, k * BS : (k + 1) * BS] = off[j, k]


def matrices(diag, inv, off):
    square = onchip((NODE_DEV, NODE_DEV))
    return pl.pallas_call(
        matrices_kernel,
        name="matrices",
        out_shape=(onchip((NODE_DEV, OFF * BS)), square, square),
        in_specs=[VM, VM, VM],
        out_specs=(VM, VM, VM),
        compiler_params=params(),
    )(diag, inv, off)


def corners_kernel(lower, upper, front, back):
    for side, source in enumerate((lower, upper)):
        for layer in range(DEPTH):
            for part in range(PARTS):
                to = slice(part * DEPTH, (part + 1) * DEPTH)
                given = part * DEPTH + layer
                front[side * DEPTH + layer, to, :] = source[given, CY - DEPTH : CY, :]
                back[side * DEPTH + layer, to, :] = source[given, 0:DEPTH, :]


def corners(lower, upper):
    shape = jax.ShapeDtypeStruct((2 * DEPTH, STRIP, NX), f32)
    return pl.pallas_call(
        corners_kernel,
        name="corners",
        out_shape=(shape, shape),
        in_specs=[VM, VM],
        out_specs=(VM, VM),
        compiler_params=params(),
    )(lower, upper)


def plan_kernel(spots, active, node_at, columns, found, columns_out):
    @pl.loop(0, REACH)
    def _(port):
        found[port] = PAD
        found[NODES_AT + port] = 0

    columns_out[...] = jnp.zeros_like(columns_out)

    def place_port(port, count):
        @pl.when(active[port] > 0)
        def _():
            found[count] = spots[port]
            found[NODES_AT + count] = node_at[port]
            columns_out[pl.ds(count, 1), :] = columns[pl.ds(port, 1), :]

        return count + active[port]

    count = lax.fori_loop(0, REACH, place_port, 0)
    found[COUNT_AT] = (count + PORT_DEV - 1) // PORT_DEV
    for item in range(2 * NB_DEV * OFF):
        found[OFF_AT + item] = node_at[REACH + item]


def plan(spots, active, node_at, columns):
    return pl.pallas_call(
        plan_kernel,
        name="plan",
        out_shape=(
            jax.ShapeDtypeStruct((SWAP_AT + NB_DEV * OFF,), jnp.int32),
            jax.ShapeDtypeStruct(columns.shape, f32),
        ),
        in_specs=[SM, SM, SM, VM],
        out_specs=(SM, VM),
        compiler_params=params(),
    )(spots, active, node_at, columns)


def halo_kernel(
    found, columns, lower, upper, before, after, before_ends, after_ends,
    e_in, h_in, coef_in, loss_in, e_xy, e_z, h, media, sample, coef, picked, sems,
):
    copies, copy = copier(sems)
    targets = [
        e_xy.at[0], e_xy.at[1], e_z, h.at[0], h.at[1], h.at[2], media.at[0], media.at[1],
    ]
    sources = [e_in.at[k] for k in range(3)] + [h_in.at[k] for k in range(3)] + [coef_in, loss_in]
    middle = pl.ds(PAD, CY)
    for part, (source, target) in enumerate(zip(sources, targets)):
        given = pl.ds(part * DEPTH, DEPTH)
        copy(source, target.at[pl.ds(DEPTH, CZ), middle])
        copy(lower.at[given], target.at[pl.ds(0, DEPTH), middle])
        copy(upper.at[given], target.at[pl.ds(DEPTH + CZ, DEPTH), middle])

    def unpack(ahead, behind, at, layer):
        for part, target in enumerate(targets):
            rows = slice(part * DEPTH, (part + 1) * DEPTH)
            target[layer, PAD - DEPTH : PAD, :] = ahead[at, rows, :]
            target[layer, PAD + CY : PAD + CY + DEPTH, :] = behind[at, rows, :]

    @pl.loop(0, CZ)
    def _(layer):
        unpack(before, after, layer, layer + DEPTH)

    @pl.loop(0, 2 * DEPTH)
    def _(end):
        unpack(before_ends, after_ends, end, jnp.where(end < DEPTH, end, end + CZ))

    for job in copies:
        job.wait()

    @pl.loop(0, LAYERS)
    def _(layer):
        media[1, layer] = 1.0 - media[1, layer]

    @pl.loop(0, found[COUNT_AT])
    def _(group):
        part = pl.ds(pl.multiple_of(group * PORT_DEV, PORT_DEV), PORT_DEV)
        _, place, _ = columns_at(columns, part)
        sample[part, :] = gather_cells(e_z, found, group, place, picked)
        coef[part, :] = gather_cells(media.at[0], found, group, place, picked)


def gather_cells(source, found, group, place, picked):
    for port in range(PORT_DEV):
        spot = found[group * PORT_DEV + port]
        picked[port : port + 1, :] = source[spot // TALL, pl.ds(spot % TALL, 1), :]
    return pick(picked[...], place)


def halo(found, columns, lower, upper, sides, e_in, h_in, coef, loss):
    return pl.pallas_call(
        halo_kernel,
        name="halo",
        out_shape=(
            onchip((2,) + CUBE),
            onchip(CUBE),
            onchip((3,) + CUBE),
            onchip((2,) + CUBE),
            onchip((REACH, 1)),
            onchip((REACH, 1)),
        ),
        in_specs=[SM, VM, HBM, HBM, VM, VM, VM, VM] + [HBM] * 4,
        out_specs=(VM,) * 6,
        scratch_shapes=[pltpu.VMEM((PORT_DEV, NX), f32), DMA((24,))],
        compiler_params=params(),
    )(found, columns, away(lower), away(upper), *sides, *map(away, (e_in, h_in, coef, loss)))


def field_kernel(step, bounds, media, e_xy, e_z, h, to_xy, to_z, to_h):
    low_z, low_y = bounds[0], bounds[1]
    lane = lanes_of(TALL, NX)
    last_lane, first_lane = lane == NX - 1, lane == 0
    row = lax.broadcasted_iota(jnp.int32, (TALL, NX), 0)
    rate_rows = jnp.where(row < PAD, low_y, time_step)

    def next_x(value):
        return jnp.where(last_lane, 0.0, pltpu.roll(value, NX - 1, 1))

    def prior_x(value):
        return jnp.where(first_lane, 0.0, pltpu.roll(value, 1, 1))

    def next_y(value):
        return pltpu.roll(value, TALL - 1, 0)

    def prior_y(value):
        return pltpu.roll(value, 1, 0)

    def magnetic(layer):
        e_x, e_y, e_zz = e_xy[0, layer], e_xy[1, layer], e_z[layer]
        rate = rate_rows * jnp.where(layer < DEPTH, low_z, 1.0)
        curl_x = (next_y(e_zz) - e_zz) - (e_xy[1, layer + 1] - e_y)
        curl_y = (e_xy[0, layer + 1] - e_x) - (next_x(e_zz) - e_zz)
        curl_z = (next_x(e_y) - e_y) - (next_y(e_x) - e_x)
        return (h[0, layer] - rate * curl_x, h[1, layer] - rate * curl_y, h[2, layer] - rate * curl_z)

    def electric(layer):
        h_x, h_y, h_z = to_h[0, layer], to_h[1, layer], to_h[2, layer]
        coef, kept = media[0, layer], media[1, layer]
        back_x = (h_z - prior_y(h_z)) - (h_y - to_h[1, layer - 1])
        back_y = (h_x - to_h[0, layer - 1]) - (h_z - prior_x(h_z))
        back_z = (h_y - prior_x(h_y)) - (h_x - prior_y(h_x))
        return (
            kept * e_xy[0, layer] + coef * back_x,
            kept * e_xy[1, layer] + coef * back_y,
            kept * e_z[layer] + coef * back_z,
        )

    def put_h(layer, values):
        to_h[0, layer], to_h[1, layer], to_h[2, layer] = values

    def put_e(layer, values):
        to_xy[0, layer], to_xy[1, layer], to_z[layer] = values

    put_h(step - 1, magnetic(step - 1))
    put_h(step, magnetic(step))
    last = LAYERS - step - 1

    @pl.loop(step, last)
    def _(layer):
        electric_values = electric(layer)
        magnetic_values = magnetic(layer + 1)
        put_e(layer, electric_values)
        put_h(layer + 1, magnetic_values)

    put_e(last, electric(last))


def field(step, bounds, media, e_xy, e_z, h):
    return pl.pallas_call(
        functools.partial(field_kernel, step),
        name="field",
        out_shape=(onchip((2,) + CUBE), onchip(CUBE), onchip((3,) + CUBE)),
        in_specs=[SM] + [VM] * 4,
        out_specs=(VM,) * 3,
        compiler_params=params(),
    )(bounds, keep(media), keep(e_xy), keep(e_z), keep(h))


def solve(stride, arrived, table, volts, m_off, m_diag, m_inv):
    lane = lanes_of(1, NODE_DEV)
    halves = []
    for j in range(NB_DEV):
        pieces = []
        for half in range(OFF // 2):
            total = None
            for side in range(2):
                spot = j * OFF + half * 2 + side
                row = arrived[pl.ds(table[OFF_AT + spot] * stride, 1), :]
                row = jnp.where(table[SWAP_AT + spot] == side, row, pltpu.roll(row, BS, 1))
                row = jnp.where((lane < BS) == (side == 0), row, 0.0)
                total = row if total is None else total + row
            pieces.append(jnp.broadcast_to(total, (BS, NODE_DEV)))
        halves.append(pieces)
    first = jnp.concatenate([halves[0][0], halves[1][0]], axis=0)
    second = jnp.concatenate([halves[0][1], halves[1][1]], axis=0)
    product = m_off[:, 0:NODE_DEV] * first + m_off[:, NODE_DEV : 2 * NODE_DEV] * second
    offsum = jnp.sum(product, axis=1, keepdims=True)
    kind = row_kind(arrived.shape, stride)
    inject = jnp.sum(jnp.where(kind == 1, arrived[...], 0.0), axis=0, keepdims=True)
    start = volts[...]
    target = charge_scale * start + inject
    diagonal = lax.broadcasted_iota(jnp.int32, (NODE_DEV, NODE_DEV), 0) == lanes_of(NODE_DEV, NODE_DEV)
    iterate = start
    for newton_round in range(NEWTON):
        local = diode_weight * jnp.tanh(iterate) - target
        terms = m_diag[...] * iterate + jnp.where(diagonal, local, 0.0)
        resid = jnp.sum(terms, axis=1, keepdims=True) + offsum
        iterate = iterate - jnp.sum(m_inv[...] * resid, axis=0, keepdims=True)
    return iterate


def apply_ports(stride, table, arrived, columns, sample, coef, e_z, near_rows, deltas):
    @pl.loop(0, table[COUNT_AT])
    def _(group):
        first = group * PORT_DEV
        part = pl.ds(pl.multiple_of(first, PORT_DEV), PORT_DEV)
        for port in range(PORT_DEV):
            near_at = table[NODES_AT + first + port] * stride
            near_rows[port : port + 1, :] = arrived[pl.ds(near_at, 1), :]
        gain, place, lane = columns_at(columns, part)
        current = gain * (sample[part, :] - pick(near_rows[...], lane))
        deltas[...] = spread(-coef[part, :] * current, place, NX)
        for port in range(PORT_DEV):
            spot = table[first + port]
            layer, row = spot // TALL, pl.ds(spot % TALL, 1)
            e_z[layer, row, :] = e_z[layer, row, :] + deltas[port : port + 1, :]


def circuit_kernel(
    stride, table, arrived, columns, sample, coef, volts, m_off, m_diag, m_inv, e_in,
    e_z, out, volts_out, sample_out, near_rows, deltas, picked, spread_rows,
):
    e_z[...] = e_in[...]
    apply_ports(stride, table, arrived, columns, sample, coef, e_z, near_rows, deltas)

    @pl.loop(0, table[COUNT_AT])
    def _(group):
        part = pl.ds(pl.multiple_of(group * PORT_DEV, PORT_DEV), PORT_DEV)
        _, place, _ = columns_at(columns, part)
        sample_out[part, :] = gather_cells(e_z, table, group, place, picked)

    solved = solve(stride, arrived, table, volts, m_off, m_diag, m_inv)
    volts_out[...] = solved
    own = slice(0, PORT_DEV)
    gain, _, lane = columns_at(columns, own)
    spread_rows[...] = spread(gain * sample_out[own, :], lane, NODE_DEV)
    out[...] = jnp.where(row_kind(out.shape, 2) == 0, solved, 0.0)
    add_rows(out, 2, [table[NODES_AT + port] for port in range(PORT_DEV)], spread_rows)


def circuit(table, arrived, columns, sample, coef, volts, mats, e_z):
    return pl.pallas_call(
        functools.partial(circuit_kernel, arrived.shape[0] // ND),
        name="circuit",
        out_shape=(
            onchip(CUBE),
            onchip((2 * ND, NODE_DEV)),
            onchip((1, NODE_DEV)),
            onchip((REACH, 1)),
        ),
        in_specs=[SM] + [VM] * 9,
        out_specs=(VM,) * 4,
        scratch_shapes=[
            pltpu.VMEM((PORT_DEV, NODE_DEV), f32),
            pltpu.VMEM((PORT_DEV, NX), f32),
            pltpu.VMEM((PORT_DEV, NX), f32),
            pltpu.VMEM((PORT_DEV, NODE_DEV), f32),
        ],
        compiler_params=params(),
    )(
        table, arrived, columns, keep(sample), keep(coef), volts,
        *[keep(mat) for mat in mats], keep(e_z),
    )


def finish_kernel(
    stride, table, arrived, columns, sample, coef, volts, m_off, m_diag, m_inv, e_xy, e_in, h,
    e_out, h_out, volts_out, e_z, near_rows, deltas, sems,
):
    copies, copy = copier(sems)
    layers, rows = pl.ds(DEPTH, CZ), pl.ds(PAD, CY)
    for k in range(3):
        copy(h.at[k, layers, rows], h_out.at[k])
    for k in range(2):
        copy(e_xy.at[k, layers, rows], e_out.at[k])
    e_z[...] = e_in[...]
    apply_ports(stride, table, arrived, columns, sample, coef, e_z, near_rows, deltas)
    copy(e_z.at[layers, rows], e_out.at[2])
    volts_out[...] = solve(stride, arrived, table, volts, m_off, m_diag, m_inv)
    for job in copies:
        job.wait()


def finish(table, arrived, columns, sample, coef, volts, mats, e_xy, e_z, h):
    return pl.pallas_call(
        functools.partial(finish_kernel, arrived.shape[0] // ND),
        name="finish",
        out_shape=(
            jax.ShapeDtypeStruct((3, CZ, CY, NX), f32),
            jax.ShapeDtypeStruct((3, CZ, CY, NX), f32),
            jax.ShapeDtypeStruct((1, NODE_DEV), f32),
        ),
        in_specs=[SM] + [VM] * 11,
        out_specs=(HBM, HBM, VM),
        scratch_shapes=[
            pltpu.VMEM(CUBE, f32),
            pltpu.VMEM((PORT_DEV, NODE_DEV), f32),
            pltpu.VMEM((PORT_DEV, NX), f32),
            DMA((6,)),
        ],
        compiler_params=params(),
    )(
        table, arrived, columns, keep(sample), keep(coef), volts,
        *[keep(mat) for mat in mats], keep(e_xy), keep(e_z), keep(h),
    )


def shifted(value, axis, steps):
    count = lax.axis_size(axis)
    first, last = (max(0, -steps), min(count, count - steps))
    return lax.ppermute(value, axis, [(source, source + steps) for source in range(first, last)])


def exchange(value):
    return lax.all_to_all(value, ("gz", "gy"), 0, 0, tiled=True)


def body(
    e_field,
    h_field,
    e_coef,
    e_loss,
    port_cell,
    port_node,
    port_gain,
    diag_blocks,
    inv_blocks,
    off_blocks,
    off_cols,
    volts_init,
):
    gz, gy = lax.axis_index("gz"), lax.axis_index("gy")
    n_gz, n_gy = lax.axis_size("gz"), lax.axis_size("gy")
    grids = (e_field, h_field, e_coef, e_loss)
    volts = volts_init.reshape(1, NODE_DEV)
    up, down, front, back, out = begin(n_gy, port_cell, port_node, port_gain, *grids, volts)
    before = shifted(front, "gy", 1)
    after = shifted(back, "gy", -1)
    lower = shifted(up, "gz", 1)
    upper = shifted(down, "gz", -1)
    arrived = exchange(out)
    front_ends, back_ends = corners(lower, upper)
    before_ends = shifted(front_ends, "gy", 1)
    after_ends = shifted(back_ends, "gy", -1)
    sides = (before, after, before_ends, after_ends)
    mats = matrices(diag_blocks, inv_blocks, off_blocks)

    shift_z = jnp.array([side[0] for side in SIDES], jnp.int32)[:, None]
    shift_y = jnp.array([side[1] for side in SIDES], jnp.int32)[:, None]
    at_z, at_y = gz + shift_z, gy + shift_y
    exists = (at_z >= 0) & (at_z < n_gz) & (at_y >= 0) & (at_y < n_gy)
    ids = jnp.where(exists, at_z * n_gy + at_y, 0)[:, 0]
    cells = arrived[4 * ids + 2][:, 0:PORT_DEV].astype(jnp.int32)
    nodes = port_node.reshape(-1, PORT_DEV)[ids].reshape(-1)
    gains = port_gain.reshape(-1, PORT_DEV)[ids].reshape(-1)
    layer = cells // (CY * NX) + shift_z * CZ + DEPTH
    row = (cells // NX) % CY + shift_y * CY + PAD
    inside = (layer >= 1) & (layer < LAYERS - 1) & (row >= PAD - DEPTH + 1) & (row < PAD + CY + DEPTH - 1)
    valid = exists & inside
    spots = jnp.where(valid, layer * TALL + row, PAD).reshape(-1)
    columns = jnp.stack(
        [gains, (cells % NX).astype(f32).reshape(-1), (nodes % NODE_DEV).astype(f32)], axis=1
    )
    flat_cols = off_cols.reshape(-1)
    node_at = jnp.concatenate([nodes // NODE_DEV, flat_cols // NB_DEV, flat_cols % NB_DEV])
    table, columns = plan(spots, valid.astype(jnp.int32).reshape(-1), node_at, columns)
    bounds = jnp.stack([jnp.where(gz > 0, 1.0, 0.0), jnp.where(gy > 0, time_step, 0.0)]).astype(f32)

    e_xy, e_z, h, media, sample, coef = halo(table, columns, lower, upper, sides, *grids)
    for step in range(1, STEPS + 1):
        if step > 1:
            arrived = exchange(out)
            arrived, e_z = lax.optimization_barrier((arrived, e_z))
        e_xy, e_z, h = field(step, bounds, media, e_xy, e_z, h)
        shared = (table, arrived, columns, sample, coef, volts, mats)
        if step < STEPS:
            e_z, out, volts, sample = circuit(*shared, e_z)
        else:
            e_end, h_end, volts = finish(*shared, e_xy, e_z, h)
    return e_end, h_end, volts.reshape(-1)


def solution(mesh):
    placed = (
        P(None, "gz", "gy", None),
        P(None, "gz", "gy", None),
        P("gz", "gy", None),
        P("gz", "gy", None),
        P(("gz", "gy")),
        P(),
        P(),
        P(("gz", "gy"), None, None),
        P(("gz", "gy"), None, None),
        P(("gz", "gy"), None, None, None),
        P(("gz", "gy"), None),
        P(("gz", "gy")),
    )
    return jax.shard_map(
        body,
        mesh=mesh,
        in_specs=placed,
        out_specs=(P(None, "gz", "gy", None), P(None, "gz", "gy", None), P(("gz", "gy"))),
        check_vma=False,
    )
```

```python
import functools

import jax
import jax.numpy as jnp
from jax import lax
from jax.experimental import pallas as pl
from jax.experimental.pallas import tpu as pltpu
from jax.sharding import PartitionSpec as P

STEPS = 5
NEWTON = 2
BS = 64
NB_DEV = 2
OFF = 4
PORT_DEV = 32
ND = 128
NODE_DEV = NB_DEV * BS
DEPTH = 5
CZ, CY, NX = 32, 16, 256
LAYERS = CZ + 2 * DEPTH
PAD = 8
TALL = CY + 2 * PAD
PARTS = 8
STRIP = PARTS * DEPTH
SIDES = ((0, 0), (-1, 0), (1, 0), (0, -1), (-1, -1), (1, -1), (0, 1), (-1, 1), (1, 1))
REACH = len(SIDES) * PORT_DEV
NODES_AT, COUNT_AT, OFF_AT = REACH, 2 * REACH, 2 * REACH + 1
SWAP_AT = OFF_AT + NB_DEV * OFF

time_step = 0.55
charge_scale = 4.0
diode_weight = 0.5

f32 = jnp.float32
VM = pl.BlockSpec(memory_space=pltpu.VMEM)
SM = pl.BlockSpec(memory_space=pltpu.SMEM)
HBM = pl.BlockSpec(memory_space=pltpu.HBM)
ANY = pl.BlockSpec(memory_space=pl.ANY)
DMA = pltpu.SemaphoreType.DMA
CUBE = (LAYERS, TALL, NX)


def onchip(shape):
    return pltpu.VMEM(shape, f32)


def keep(value):
    return pltpu.with_memory_space_constraint(value, pltpu.VMEM)


def away(value):
    return pltpu.with_memory_space_constraint(value, pltpu.HBM)


def params():
    return pltpu.CompilerParams(vmem_limit_bytes=12 << 20)


def lanes_of(count, width):
    return lax.broadcasted_iota(jnp.int32, (count, width), 1)


def pick(rows, lane):
    hit = lanes_of(rows.shape[0], rows.shape[1]) == lane
    return jnp.sum(jnp.where(hit, rows, 0.0), axis=1, keepdims=True)


def spread(column, lane, width):
    hit = lanes_of(column.shape[0], width) == lane
    return jnp.where(hit, column, 0.0)


def columns_at(columns, part):
    block = columns[part, :]
    return block[:, 0:1], block[:, 1:2].astype(jnp.int32), block[:, 2:3].astype(jnp.int32)


def row_kind(shape, stride):
    return lax.broadcasted_iota(jnp.int32, shape, 0) % stride


def add_rows(out, stride, devices, rows_ref):
    for port, device in enumerate(devices):
        spot = pl.ds(device * stride + 1, 1)
        out[spot, :] = out[spot, :] + rows_ref[port : port + 1, :]


def copier(sems):
    copies = []

    def copy(source, target):
        job = pltpu.make_async_copy(source, target, sems.at[len(copies)])
        job.start()
        copies.append(job)

    return copies, copy


def sources_of(e_in, h_in, coef_in, loss_in):
    return [e_in.at[k] for k in range(3)] + [h_in.at[k] for k in range(3)] + [coef_in, loss_in]


def strip_kernel(top, e_in, h_in, coef_in, loss_in, after, strip, fields, sems):
    copies, copy = copier(sems)
    rows = pl.ds(CY - 8 if top else 0, 8)
    for part, source in enumerate(sources_of(e_in, h_in, coef_in, loss_in)):
        copy(source.at[:, rows], fields.at[part])
    for job in copies:
        job.wait()
    given = slice(8 - DEPTH, 8) if top else slice(0, DEPTH)

    @pl.loop(0, CZ)
    def _(layer):
        for part in range(PARTS):
            strip[layer, part * DEPTH : (part + 1) * DEPTH, :] = fields[part, layer, given, :]


def strip_of(top, grids, after):
    return pl.pallas_call(
        functools.partial(strip_kernel, top),
        name="strip",
        out_shape=jax.ShapeDtypeStruct((CZ, STRIP, NX), f32),
        in_specs=[HBM] * 4 + [ANY],
        out_specs=VM,
        scratch_shapes=[pltpu.VMEM((PARTS, CZ, 8, NX), f32), DMA((PARTS,))],
        compiler_params=params(),
    )(*map(away, grids), after)


def slab_kernel(top, e_in, h_in, coef_in, loss_in, after, slab, sems):
    copies, copy = copier(sems)
    layers = pl.ds(CZ - DEPTH if top else 0, DEPTH)
    for part, source in enumerate(sources_of(e_in, h_in, coef_in, loss_in)):
        copy(source.at[layers], slab.at[pl.ds(part * DEPTH, DEPTH)])
    for job in copies:
        job.wait()


def slab_of(top, grids, after):
    return pl.pallas_call(
        functools.partial(slab_kernel, top),
        name="slab",
        out_shape=jax.ShapeDtypeStruct((PARTS * DEPTH, CY, NX), f32),
        in_specs=[HBM] * 4 + [ANY],
        out_specs=VM,
        scratch_shapes=[DMA((PARTS,))],
        compiler_params=params(),
    )(*map(away, grids), after)


def begin_kernel(
    n_gy, cells, nodes, gains, e_in, cell_row, volts, after, out, e_z, picked, hits, rows_ref, sem,
):
    load = pltpu.make_async_copy(e_in.at[2], e_z, sem)
    load.start()
    first = (lax.axis_index("gz") * n_gy + lax.axis_index("gy")) * PORT_DEV
    wide, narrow = lanes_of(1, NX), lanes_of(1, NODE_DEV)
    own_nodes = [nodes[first + port] for port in range(PORT_DEV)]
    for port, node in enumerate(own_nodes):
        hits[port : port + 1, :] = jnp.where(narrow == node % NODE_DEV, 1.0, 0.0)
    kind = row_kind(out.shape, 4)
    rows_ref[0:1, :] = jnp.zeros((1, NODE_DEV), f32)
    rows_ref[0:1, 0:PORT_DEV] = cell_row[...].astype(f32)
    out[...] = jnp.where(kind == 0, volts[...], jnp.where(kind == 2, rows_ref[0:1, :], 0.0))

    load.wait()
    for port in range(PORT_DEV):
        cell = cells[port]
        line = cell // NX
        value = e_z[line // CY, pl.ds(line % CY, 1), :] * gains[first + port]
        picked[port : port + 1, :] = jnp.where(wide == cell % NX, value, 0.0)
    rows_ref[...] = hits[...] * jnp.sum(picked[...], axis=1, keepdims=True)
    add_rows(out, 4, [node // NODE_DEV for node in own_nodes], rows_ref)


def begin(n_gy, cells, nodes, gains, e_in, volts, after):
    return pl.pallas_call(
        functools.partial(begin_kernel, n_gy),
        name="begin",
        out_shape=jax.ShapeDtypeStruct((4 * ND, NODE_DEV), f32),
        in_specs=[SM, SM, SM, HBM, VM, VM, ANY],
        out_specs=VM,
        scratch_shapes=[
            pltpu.VMEM((CZ, CY, NX), f32),
            pltpu.VMEM((PORT_DEV, NX), f32),
            pltpu.VMEM((PORT_DEV, NODE_DEV), f32),
            pltpu.VMEM((PORT_DEV, NODE_DEV), f32),
            DMA,
        ],
        compiler_params=params(),
    )(cells, nodes, gains, away(e_in), cells.reshape(1, -1), volts, after)


def matrices_kernel(diag, inv, off, m_off, m_diag, m_inv):
    m_diag[...] = jnp.zeros_like(m_diag)
    m_inv[...] = jnp.zeros_like(m_inv)
    for j in range(NB_DEV):
        part = slice(j * BS, (j + 1) * BS)
        m_diag[part, part] = diag[j]
        m_inv[part, part] = inv[j].T
        for k in range(OFF):
            m_off[part, k * BS : (k + 1) * BS] = off[j, k]


def matrices(diag, inv, off):
    square = onchip((NODE_DEV, NODE_DEV))
    return pl.pallas_call(
        matrices_kernel,
        name="matrices",
        out_shape=(onchip((NODE_DEV, OFF * BS)), square, square),
        in_specs=[VM, VM, VM],
        out_specs=(VM, VM, VM),
        compiler_params=params(),
    )(diag, inv, off)


def corners_kernel(lower, upper, front, back):
    for side, source in enumerate((lower, upper)):
        for layer in range(DEPTH):
            for part in range(PARTS):
                to = slice(part * DEPTH, (part + 1) * DEPTH)
                given = part * DEPTH + layer
                front[side * DEPTH + layer, to, :] = source[given, CY - DEPTH : CY, :]
                back[side * DEPTH + layer, to, :] = source[given, 0:DEPTH, :]


def corners(lower, upper):
    shape = jax.ShapeDtypeStruct((2 * DEPTH, STRIP, NX), f32)
    return pl.pallas_call(
        corners_kernel,
        name="corners",
        out_shape=(shape, shape),
        in_specs=[VM, VM],
        out_specs=(VM, VM),
        compiler_params=params(),
    )(lower, upper)


def plan_kernel(spots, active, node_at, columns, found, columns_out):
    @pl.loop(0, REACH)
    def _(port):
        found[port] = PAD
        found[NODES_AT + port] = 0

    columns_out[...] = jnp.zeros_like(columns_out)

    def place_port(port, count):
        @pl.when(active[port] > 0)
        def _():
            found[count] = spots[port]
            found[NODES_AT + count] = node_at[port]
            columns_out[pl.ds(count, 1), :] = columns[pl.ds(port, 1), :]

        return count + active[port]

    count = lax.fori_loop(0, REACH, place_port, 0)
    found[COUNT_AT] = (count + PORT_DEV - 1) // PORT_DEV
    for item in range(2 * NB_DEV * OFF):
        found[OFF_AT + item] = node_at[REACH + item]


def plan(spots, active, node_at, columns):
    return pl.pallas_call(
        plan_kernel,
        name="plan",
        out_shape=(
            jax.ShapeDtypeStruct((SWAP_AT + NB_DEV * OFF,), jnp.int32),
            jax.ShapeDtypeStruct(columns.shape, f32),
        ),
        in_specs=[SM, SM, SM, VM],
        out_specs=(SM, VM),
        compiler_params=params(),
    )(spots, active, node_at, columns)


def halo_kernel(
    found, columns, lower, upper, before, after, before_ends, after_ends,
    e_in, h_in, coef_in, loss_in, e_xy, e_z, h, media, sample, coef, picked, sems,
):
    copies, copy = copier(sems)
    targets = [
        e_xy.at[0], e_xy.at[1], e_z, h.at[0], h.at[1], h.at[2], media.at[0], media.at[1],
    ]
    sources = [e_in.at[k] for k in range(3)] + [h_in.at[k] for k in range(3)] + [coef_in, loss_in]
    middle = pl.ds(PAD, CY)
    for part, (source, target) in enumerate(zip(sources, targets)):
        given = pl.ds(part * DEPTH, DEPTH)
        copy(source, target.at[pl.ds(DEPTH, CZ), middle])
        copy(lower.at[given], target.at[pl.ds(0, DEPTH), middle])
        copy(upper.at[given], target.at[pl.ds(DEPTH + CZ, DEPTH), middle])

    def unpack(ahead, behind, at, layer):
        for part, target in enumerate(targets):
            rows = slice(part * DEPTH, (part + 1) * DEPTH)
            target[layer, PAD - DEPTH : PAD, :] = ahead[at, rows, :]
            target[layer, PAD + CY : PAD + CY + DEPTH, :] = behind[at, rows, :]

    @pl.loop(0, CZ)
    def _(layer):
        unpack(before, after, layer, layer + DEPTH)

    @pl.loop(0, 2 * DEPTH)
    def _(end):
        unpack(before_ends, after_ends, end, jnp.where(end < DEPTH, end, end + CZ))

    for job in copies:
        job.wait()

    @pl.loop(0, LAYERS)
    def _(layer):
        media[1, layer] = 1.0 - media[1, layer]

    @pl.loop(0, found[COUNT_AT])
    def _(group):
        part = pl.ds(pl.multiple_of(group * PORT_DEV, PORT_DEV), PORT_DEV)
        _, place, _ = columns_at(columns, part)
        sample[part, :] = gather_cells(e_z, found, group, place, picked)
        coef[part, :] = gather_cells(media.at[0], found, group, place, picked)


def gather_cells(source, found, group, place, picked):
    for port in range(PORT_DEV):
        spot = found[group * PORT_DEV + port]
        picked[port : port + 1, :] = source[spot // TALL, pl.ds(spot % TALL, 1), :]
    return pick(picked[...], place)


def halo(found, columns, lower, upper, sides, e_in, h_in, coef, loss):
    return pl.pallas_call(
        halo_kernel,
        name="halo",
        out_shape=(
            onchip((2,) + CUBE),
            onchip(CUBE),
            onchip((3,) + CUBE),
            onchip((2,) + CUBE),
            onchip((REACH, 1)),
            onchip((REACH, 1)),
        ),
        in_specs=[SM, VM, HBM, HBM, VM, VM, VM, VM] + [HBM] * 4,
        out_specs=(VM,) * 6,
        scratch_shapes=[pltpu.VMEM((PORT_DEV, NX), f32), DMA((24,))],
        compiler_params=params(),
    )(found, columns, away(lower), away(upper), *sides, *map(away, (e_in, h_in, coef, loss)))


def field_kernel(step, bounds, media, e_xy, e_z, h, to_xy, to_z, to_h):
    low_z, low_y = bounds[0], bounds[1]
    lane = lanes_of(TALL, NX)
    last_lane, first_lane = lane == NX - 1, lane == 0
    row = lax.broadcasted_iota(jnp.int32, (TALL, NX), 0)
    rate_rows = jnp.where(row < PAD, low_y, time_step)

    def next_x(value):
        return jnp.where(last_lane, 0.0, pltpu.roll(value, NX - 1, 1))

    def prior_x(value):
        return jnp.where(first_lane, 0.0, pltpu.roll(value, 1, 1))

    def next_y(value):
        return pltpu.roll(value, TALL - 1, 0)

    def prior_y(value):
        return pltpu.roll(value, 1, 0)

    def magnetic(layer):
        e_x, e_y, e_zz = e_xy[0, layer], e_xy[1, layer], e_z[layer]
        rate = rate_rows * jnp.where(layer < DEPTH, low_z, 1.0)
        curl_x = (next_y(e_zz) - e_zz) - (e_xy[1, layer + 1] - e_y)
        curl_y = (e_xy[0, layer + 1] - e_x) - (next_x(e_zz) - e_zz)
        curl_z = (next_x(e_y) - e_y) - (next_y(e_x) - e_x)
        return (h[0, layer] - rate * curl_x, h[1, layer] - rate * curl_y, h[2, layer] - rate * curl_z)

    def electric(layer):
        h_x, h_y, h_z = to_h[0, layer], to_h[1, layer], to_h[2, layer]
        coef, kept = media[0, layer], media[1, layer]
        back_x = (h_z - prior_y(h_z)) - (h_y - to_h[1, layer - 1])
        back_y = (h_x - to_h[0, layer - 1]) - (h_z - prior_x(h_z))
        back_z = (h_y - prior_x(h_y)) - (h_x - prior_y(h_x))
        return (
            kept * e_xy[0, layer] + coef * back_x,
            kept * e_xy[1, layer] + coef * back_y,
            kept * e_z[layer] + coef * back_z,
        )

    def put_h(layer, values):
        to_h[0, layer], to_h[1, layer], to_h[2, layer] = values

    def put_e(layer, values):
        to_xy[0, layer], to_xy[1, layer], to_z[layer] = values

    put_h(step - 1, magnetic(step - 1))
    put_h(step, magnetic(step))
    last = LAYERS - step - 1

    @pl.loop(step, last)
    def _(layer):
        electric_values = electric(layer)
        magnetic_values = magnetic(layer + 1)
        put_e(layer, electric_values)
        put_h(layer + 1, magnetic_values)

    put_e(last, electric(last))


def field(step, bounds, media, e_xy, e_z, h):
    return pl.pallas_call(
        functools.partial(field_kernel, step),
        name="field",
        out_shape=(onchip((2,) + CUBE), onchip(CUBE), onchip((3,) + CUBE)),
        in_specs=[SM] + [VM] * 4,
        out_specs=(VM,) * 3,
        compiler_params=params(),
    )(bounds, keep(media), keep(e_xy), keep(e_z), keep(h))


def solve(stride, arrived, table, volts, m_off, m_diag, m_inv):
    lane = lanes_of(1, NODE_DEV)
    halves = []
    for j in range(NB_DEV):
        pieces = []
        for half in range(OFF // 2):
            total = None
            for side in range(2):
                spot = j * OFF + half * 2 + side
                row = arrived[pl.ds(table[OFF_AT + spot] * stride, 1), :]
                row = jnp.where(table[SWAP_AT + spot] == side, row, pltpu.roll(row, BS, 1))
                row = jnp.where((lane < BS) == (side == 0), row, 0.0)
                total = row if total is None else total + row
            pieces.append(jnp.broadcast_to(total, (BS, NODE_DEV)))
        halves.append(pieces)
    first = jnp.concatenate([halves[0][0], halves[1][0]], axis=0)
    second = jnp.concatenate([halves[0][1], halves[1][1]], axis=0)
    product = m_off[:, 0:NODE_DEV] * first + m_off[:, NODE_DEV : 2 * NODE_DEV] * second
    offsum = jnp.sum(product, axis=1, keepdims=True)
    kind = row_kind(arrived.shape, stride)
    inject = jnp.sum(jnp.where(kind == 1, arrived[...], 0.0), axis=0, keepdims=True)
    start = volts[...]
    target = charge_scale * start + inject
    diagonal = lax.broadcasted_iota(jnp.int32, (NODE_DEV, NODE_DEV), 0) == lanes_of(NODE_DEV, NODE_DEV)
    iterate = start
    for newton_round in range(NEWTON):
        local = diode_weight * jnp.tanh(iterate) - target
        terms = m_diag[...] * iterate + jnp.where(diagonal, local, 0.0)
        resid = jnp.sum(terms, axis=1, keepdims=True) + offsum
        iterate = iterate - jnp.sum(m_inv[...] * resid, axis=0, keepdims=True)
    return iterate


def apply_ports(stride, table, arrived, columns, sample, coef, e_z, near_rows, deltas):
    @pl.loop(0, table[COUNT_AT])
    def _(group):
        first = group * PORT_DEV
        part = pl.ds(pl.multiple_of(first, PORT_DEV), PORT_DEV)
        for port in range(PORT_DEV):
            near_at = table[NODES_AT + first + port] * stride
            near_rows[port : port + 1, :] = arrived[pl.ds(near_at, 1), :]
        gain, place, lane = columns_at(columns, part)
        current = gain * (sample[part, :] - pick(near_rows[...], lane))
        deltas[...] = spread(-coef[part, :] * current, place, NX)
        for port in range(PORT_DEV):
            spot = table[first + port]
            layer, row = spot // TALL, pl.ds(spot % TALL, 1)
            e_z[layer, row, :] = e_z[layer, row, :] + deltas[port : port + 1, :]


def circuit_kernel(
    stride, table, arrived, columns, sample, coef, volts, m_off, m_diag, m_inv, e_in,
    e_z, out, volts_out, sample_out, near_rows, deltas, picked, spread_rows,
):
    e_z[...] = e_in[...]
    apply_ports(stride, table, arrived, columns, sample, coef, e_z, near_rows, deltas)

    @pl.loop(0, table[COUNT_AT])
    def _(group):
        part = pl.ds(pl.multiple_of(group * PORT_DEV, PORT_DEV), PORT_DEV)
        _, place, _ = columns_at(columns, part)
        sample_out[part, :] = gather_cells(e_z, table, group, place, picked)

    solved = solve(stride, arrived, table, volts, m_off, m_diag, m_inv)
    volts_out[...] = solved
    own = slice(0, PORT_DEV)
    gain, _, lane = columns_at(columns, own)
    spread_rows[...] = spread(gain * sample_out[own, :], lane, NODE_DEV)
    out[...] = jnp.where(row_kind(out.shape, 2) == 0, solved, 0.0)
    add_rows(out, 2, [table[NODES_AT + port] for port in range(PORT_DEV)], spread_rows)


def circuit(table, arrived, columns, sample, coef, volts, mats, e_z):
    return pl.pallas_call(
        functools.partial(circuit_kernel, arrived.shape[0] // ND),
        name="circuit",
        out_shape=(
            onchip(CUBE),
            onchip((2 * ND, NODE_DEV)),
            onchip((1, NODE_DEV)),
            onchip((REACH, 1)),
        ),
        in_specs=[SM] + [VM] * 9,
        out_specs=(VM,) * 4,
        scratch_shapes=[
            pltpu.VMEM((PORT_DEV, NODE_DEV), f32),
            pltpu.VMEM((PORT_DEV, NX), f32),
            pltpu.VMEM((PORT_DEV, NX), f32),
            pltpu.VMEM((PORT_DEV, NODE_DEV), f32),
        ],
        compiler_params=params(),
    )(
        table, arrived, columns, keep(sample), keep(coef), volts,
        *[keep(mat) for mat in mats], keep(e_z),
    )


def finish_kernel(
    stride, table, arrived, columns, sample, coef, volts, m_off, m_diag, m_inv, e_xy, e_in, h,
    e_out, h_out, volts_out, e_z, near_rows, deltas, sems,
):
    copies, copy = copier(sems)
    layers, rows = pl.ds(DEPTH, CZ), pl.ds(PAD, CY)
    for k in range(3):
        copy(h.at[k, layers, rows], h_out.at[k])
    for k in range(2):
        copy(e_xy.at[k, layers, rows], e_out.at[k])
    e_z[...] = e_in[...]
    apply_ports(stride, table, arrived, columns, sample, coef, e_z, near_rows, deltas)
    copy(e_z.at[layers, rows], e_out.at[2])
    volts_out[...] = solve(stride, arrived, table, volts, m_off, m_diag, m_inv)
    for job in copies:
        job.wait()


def finish(table, arrived, columns, sample, coef, volts, mats, e_xy, e_z, h):
    return pl.pallas_call(
        functools.partial(finish_kernel, arrived.shape[0] // ND),
        name="finish",
        out_shape=(
            jax.ShapeDtypeStruct((3, CZ, CY, NX), f32),
            jax.ShapeDtypeStruct((3, CZ, CY, NX), f32),
            jax.ShapeDtypeStruct((1, NODE_DEV), f32),
        ),
        in_specs=[SM] + [VM] * 11,
        out_specs=(HBM, HBM, VM),
        scratch_shapes=[
            pltpu.VMEM(CUBE, f32),
            pltpu.VMEM((PORT_DEV, NODE_DEV), f32),
            pltpu.VMEM((PORT_DEV, NX), f32),
            DMA((6,)),
        ],
        compiler_params=params(),
    )(
        table, arrived, columns, keep(sample), keep(coef), volts,
        *[keep(mat) for mat in mats], keep(e_xy), keep(e_z), keep(h),
    )


def shifted(value, axis, steps):
    count = lax.axis_size(axis)
    first, last = (max(0, -steps), min(count, count - steps))
    return lax.ppermute(value, axis, [(source, source + steps) for source in range(first, last)])


def exchange(value):
    return lax.all_to_all(value, ("gz", "gy"), 0, 0, tiled=True)


def body(
    e_field,
    h_field,
    e_coef,
    e_loss,
    port_cell,
    port_node,
    port_gain,
    diag_blocks,
    inv_blocks,
    off_blocks,
    off_cols,
    volts_init,
):
    gz, gy = lax.axis_index("gz"), lax.axis_index("gy")
    n_gz, n_gy = lax.axis_size("gz"), lax.axis_size("gy")
    grids = (e_field, h_field, e_coef, e_loss)
    volts = volts_init.reshape(1, NODE_DEV)
    front = strip_of(True, grids, volts)
    before = shifted(front, "gy", 1)
    back = strip_of(False, grids, front)
    after = shifted(back, "gy", -1)
    up = slab_of(True, grids, back)
    lower = shifted(up, "gz", 1)
    down = slab_of(False, grids, up)
    upper = shifted(down, "gz", -1)
    out = begin(n_gy, port_cell, port_node, port_gain, e_field, volts, down)
    arrived = exchange(out)
    front_ends, back_ends = corners(lower, upper)
    before_ends = shifted(front_ends, "gy", 1)
    after_ends = shifted(back_ends, "gy", -1)
    sides = (before, after, before_ends, after_ends)
    mats = matrices(diag_blocks, inv_blocks, off_blocks)

    shift_z = jnp.array([side[0] for side in SIDES], jnp.int32)[:, None]
    shift_y = jnp.array([side[1] for side in SIDES], jnp.int32)[:, None]
    at_z, at_y = gz + shift_z, gy + shift_y
    exists = (at_z >= 0) & (at_z < n_gz) & (at_y >= 0) & (at_y < n_gy)
    ids = jnp.where(exists, at_z * n_gy + at_y, 0)[:, 0]
    cells = arrived[4 * ids + 2][:, 0:PORT_DEV].astype(jnp.int32)
    nodes = port_node.reshape(-1, PORT_DEV)[ids].reshape(-1)
    gains = port_gain.reshape(-1, PORT_DEV)[ids].reshape(-1)
    layer = cells // (CY * NX) + shift_z * CZ + DEPTH
    row = (cells // NX) % CY + shift_y * CY + PAD
    inside = (layer >= 1) & (layer < LAYERS - 1) & (row >= PAD - DEPTH + 1) & (row < PAD + CY + DEPTH - 1)
    valid = exists & inside
    spots = jnp.where(valid, layer * TALL + row, PAD).reshape(-1)
    columns = jnp.stack(
        [gains, (cells % NX).astype(f32).reshape(-1), (nodes % NODE_DEV).astype(f32)], axis=1
    )
    flat_cols = off_cols.reshape(-1)
    node_at = jnp.concatenate([nodes // NODE_DEV, flat_cols // NB_DEV, flat_cols % NB_DEV])
    table, columns = plan(spots, valid.astype(jnp.int32).reshape(-1), node_at, columns)
    bounds = jnp.stack([jnp.where(gz > 0, 1.0, 0.0), jnp.where(gy > 0, time_step, 0.0)]).astype(f32)

    e_xy, e_z, h, media, sample, coef = halo(table, columns, lower, upper, sides, *grids)
    for step in range(1, STEPS + 1):
        if step > 1:
            arrived = exchange(out)
            arrived, e_z = lax.optimization_barrier((arrived, e_z))
        e_xy, e_z, h = field(step, bounds, media, e_xy, e_z, h)
        shared = (table, arrived, columns, sample, coef, volts, mats)
        if step < STEPS:
            e_z, out, volts, sample = circuit(*shared, e_z)
        else:
            e_end, h_end, volts = finish(*shared, e_xy, e_z, h)
    return e_end, h_end, volts.reshape(-1)


def solution(mesh):
    placed = (
        P(None, "gz", "gy", None),
        P(None, "gz", "gy", None),
        P("gz", "gy", None),
        P("gz", "gy", None),
        P(("gz", "gy")),
        P(),
        P(),
        P(("gz", "gy"), None, None),
        P(("gz", "gy"), None, None),
        P(("gz", "gy"), None, None, None),
        P(("gz", "gy"), None),
        P(("gz", "gy")),
    )
    return jax.shard_map(
        body,
        mesh=mesh,
        in_specs=placed,
        out_specs=(P(None, "gz", "gy", None), P(None, "gz", "gy", None), P(("gz", "gy"))),
        check_vma=False,
    )
```

```python
import functools

import jax
import jax.numpy as jnp
from jax import lax
from jax.experimental import pallas as pl
from jax.experimental.pallas import tpu as pltpu
from jax.sharding import PartitionSpec as P

STEPS = 5
NEWTON = 2
BS = 64
NB_DEV = 2
OFF = 4
PORT_DEV = 32
ND = 128
NODE_DEV = NB_DEV * BS
DEPTH = 5
CZ, CY, NX = 32, 16, 256
LAYERS = CZ + 2 * DEPTH
PAD = 8
TALL = CY + 2 * PAD
PARTS = 8
STRIP = PARTS * DEPTH
SIDES = ((0, 0), (-1, 0), (1, 0), (0, -1), (-1, -1), (1, -1), (0, 1), (-1, 1), (1, 1))
REACH = len(SIDES) * PORT_DEV
SPOTS, NODES, COUNT = 0, 1, 7

time_step = 0.55
charge_scale = 4.0
diode_weight = 0.5

f32 = jnp.float32
VM = pl.BlockSpec(memory_space=pltpu.VMEM)
SM = pl.BlockSpec(memory_space=pltpu.SMEM)
HBM = pl.BlockSpec(memory_space=pltpu.HBM)
ANY = pl.BlockSpec(memory_space=pl.ANY)
DMA = pltpu.SemaphoreType.DMA
CUBE = (LAYERS, TALL, NX)


def onchip(shape):
    return pltpu.VMEM(shape, f32)


def keep(value):
    return pltpu.with_memory_space_constraint(value, pltpu.VMEM)


def away(value):
    return pltpu.with_memory_space_constraint(value, pltpu.HBM)


def params():
    return pltpu.CompilerParams(vmem_limit_bytes=12 << 20)


def lanes_of(count, width):
    return lax.broadcasted_iota(jnp.int32, (count, width), 1)


def pick(rows, lane):
    hit = lanes_of(rows.shape[0], rows.shape[1]) == lane
    return jnp.sum(jnp.where(hit, rows, 0.0), axis=1, keepdims=True)


def spread(column, lane, width):
    hit = lanes_of(column.shape[0], width) == lane
    return jnp.where(hit, column, 0.0)


def columns_at(columns, part):
    block = columns[part, :]
    return block[:, 2:3], block[:, 3:4].astype(jnp.int32), block[:, 4:5].astype(jnp.int32)


def row_kind(shape, stride):
    return lax.broadcasted_iota(jnp.int32, shape, 0) % stride


def add_rows(out, stride, devices, rows_ref):
    for port, device in enumerate(devices):
        spot = pl.ds(device * stride + 1, 1)
        out[spot, :] = out[spot, :] + rows_ref[port : port + 1, :]


def copier(sems):
    copies = []

    def copy(source, target):
        job = pltpu.make_async_copy(source, target, sems.at[len(copies)])
        job.start()
        copies.append(job)

    return copies, copy


def sources_of(e_in, h_in, coef_in, loss_in):
    return [e_in.at[k] for k in range(3)] + [h_in.at[k] for k in range(3)] + [coef_in, loss_in]


def strip_kernel(top, e_in, h_in, coef_in, loss_in, after, strip, fields, sems):
    copies, copy = copier(sems)
    rows = pl.ds(CY - 8 if top else 0, 8)
    for part, source in enumerate(sources_of(e_in, h_in, coef_in, loss_in)):
        copy(source.at[:, rows], fields.at[part])
    for job in copies:
        job.wait()
    given = slice(8 - DEPTH, 8) if top else slice(0, DEPTH)

    @pl.loop(0, CZ)
    def _(layer):
        for part in range(PARTS):
            strip[layer, part * DEPTH : (part + 1) * DEPTH, :] = fields[part, layer, given, :]


def strip_of(top, grids, after):
    return pl.pallas_call(
        functools.partial(strip_kernel, top),
        name="strip",
        out_shape=jax.ShapeDtypeStruct((CZ, STRIP, NX), f32),
        in_specs=[HBM] * 4 + [ANY],
        out_specs=VM,
        scratch_shapes=[pltpu.VMEM((PARTS, CZ, 8, NX), f32), DMA((PARTS,))],
        compiler_params=params(),
    )(*map(away, grids), after)


def slab_kernel(top, e_in, h_in, coef_in, loss_in, after, slab, sems):
    copies, copy = copier(sems)
    layers = pl.ds(CZ - DEPTH if top else 0, DEPTH)
    for part, source in enumerate(sources_of(e_in, h_in, coef_in, loss_in)):
        copy(source.at[layers], slab.at[pl.ds(part * DEPTH, DEPTH)])
    for job in copies:
        job.wait()


def slab_of(top, grids, after):
    return pl.pallas_call(
        functools.partial(slab_kernel, top),
        name="slab",
        out_shape=jax.ShapeDtypeStruct((PARTS * DEPTH, CY, NX), f32),
        in_specs=[HBM] * 4 + [ANY],
        out_specs=VM,
        scratch_shapes=[DMA((PARTS,))],
        compiler_params=params(),
    )(*map(away, grids), after)


def begin_kernel(
    n_gy, cells, nodes, gains, e_in, cell_row, volts, after, out, e_z, picked, hits, rows_ref, sem,
):
    load = pltpu.make_async_copy(e_in.at[2], e_z, sem)
    load.start()
    first = (lax.axis_index("gz") * n_gy + lax.axis_index("gy")) * PORT_DEV
    wide, narrow = lanes_of(1, NX), lanes_of(1, NODE_DEV)
    own_nodes = [nodes[first + port] for port in range(PORT_DEV)]
    for port, node in enumerate(own_nodes):
        hits[port : port + 1, :] = jnp.where(narrow == node % NODE_DEV, 1.0, 0.0)
    kind = row_kind(out.shape, 4)
    rows_ref[0:1, :] = jnp.zeros((1, NODE_DEV), f32)
    rows_ref[0:1, 0:PORT_DEV] = cell_row[...].astype(f32)
    out[...] = jnp.where(kind == 0, volts[...], jnp.where(kind == 2, rows_ref[0:1, :], 0.0))

    load.wait()
    for port in range(PORT_DEV):
        cell = cells[port]
        line = cell // NX
        value = e_z[line // CY, pl.ds(line % CY, 1), :] * gains[first + port]
        picked[port : port + 1, :] = jnp.where(wide == cell % NX, value, 0.0)
    rows_ref[...] = hits[...] * jnp.sum(picked[...], axis=1, keepdims=True)
    add_rows(out, 4, [node // NODE_DEV for node in own_nodes], rows_ref)


def begin(n_gy, cells, nodes, gains, e_in, volts, after):
    return pl.pallas_call(
        functools.partial(begin_kernel, n_gy),
        name="begin",
        out_shape=jax.ShapeDtypeStruct((4 * ND, NODE_DEV), f32),
        in_specs=[SM, SM, SM, HBM, VM, VM, ANY],
        out_specs=VM,
        scratch_shapes=[
            pltpu.VMEM((CZ, CY, NX), f32),
            pltpu.VMEM((PORT_DEV, NX), f32),
            pltpu.VMEM((PORT_DEV, NODE_DEV), f32),
            pltpu.VMEM((PORT_DEV, NODE_DEV), f32),
            DMA,
        ],
        compiler_params=params(),
    )(cells, nodes, gains, away(e_in), cells.reshape(1, -1), volts, after)


def matrices_kernel(diag, inv, off, m_off, m_diag, m_inv):
    m_diag[...] = jnp.zeros_like(m_diag)
    m_inv[...] = jnp.zeros_like(m_inv)
    for j in range(NB_DEV):
        part = slice(j * BS, (j + 1) * BS)
        m_diag[part, part] = diag[j]
        m_inv[part, part] = inv[j].T
        for k in range(OFF):
            m_off[part, k * BS : (k + 1) * BS] = off[j, k]


def matrices(diag, inv, off):
    square = onchip((NODE_DEV, NODE_DEV))
    return pl.pallas_call(
        matrices_kernel,
        name="matrices",
        out_shape=(onchip((NODE_DEV, OFF * BS)), square, square),
        in_specs=[VM, VM, VM],
        out_specs=(VM, VM, VM),
        compiler_params=params(),
    )(diag, inv, off)


def corners_kernel(lower, upper, after, front, back):
    for side, source in enumerate((lower, upper)):
        for layer in range(DEPTH):
            for part in range(PARTS):
                to = slice(part * DEPTH, (part + 1) * DEPTH)
                given = part * DEPTH + layer
                front[side * DEPTH + layer, to, :] = source[given, CY - DEPTH : CY, :]
                back[side * DEPTH + layer, to, :] = source[given, 0:DEPTH, :]


def corners(lower, upper, after):
    shape = jax.ShapeDtypeStruct((2 * DEPTH, STRIP, NX), f32)
    return pl.pallas_call(
        corners_kernel,
        name="corners",
        out_shape=(shape, shape),
        in_specs=[VM, VM, ANY],
        out_specs=(VM, VM),
        compiler_params=params(),
    )(lower, upper, after)


def plan_kernel(n_gz, n_gy, arrived, nodes, gains, found, columns, facts):
    gz, gy = lax.axis_index("gz"), lax.axis_index("gy")
    lane = lanes_of(1, NODE_DEV)
    width = NODE_DEV // PORT_DEV
    facts[...] = jnp.zeros_like(facts)
    for group, (side_z, side_y) in enumerate(SIDES):
        at_z, at_y = gz + side_z, gy + side_y
        exists = (at_z >= 0) & (at_z < n_gz) & (at_y >= 0) & (at_y < n_gy)
        device = jnp.where(exists, at_z * n_gy + at_y, 0)
        slot = group % width
        turn = (slot - device % width + width) % width * PORT_DEV
        row = pl.ds(device // width, 1)
        node, gain = pltpu.roll(nodes[row, :], turn, 1), pltpu.roll(gains[row, :], turn, 1)
        cell = pltpu.roll(arrived[pl.ds(4 * device + 2, 1), :], slot * PORT_DEV, 1).astype(jnp.int32)
        layer = cell // (CY * NX) + (side_z * CZ + DEPTH)
        line = (cell // NX) % CY + (side_y * CY + PAD)
        valid = (layer >= 1) & (layer < LAYERS - 1)
        valid &= (line > PAD - DEPTH) & (line < PAD + CY + DEPTH - 1)
        valid &= (lane // PORT_DEV == slot) & (jnp.where(exists, 1, 0) > 0)
        values = (layer * TALL + line, node // NODE_DEV, gain, cell % NX, node % NODE_DEV, 1)
        part = slice(group // width * NODE_DEV, (group // width + 1) * NODE_DEV)
        for kind, value in enumerate(values):
            fact = jnp.where(valid, jnp.asarray(value).astype(f32), 0.0)
            facts[kind : kind + 1, part] = facts[kind : kind + 1, part] + fact

    used = facts[5:6, :]
    total = used.shape[1]
    upper = lax.broadcasted_iota(jnp.int32, (total, total), 0) <= lanes_of(total, total)
    ones = jnp.broadcast_to(used, (8, total))
    order = jnp.dot(ones, upper.astype(f32), preferred_element_type=f32)[0:1, :] - 1.0
    spot = lax.broadcasted_iota(jnp.int32, (REACH, total), 0)
    chosen = jnp.where((spot == order.astype(jnp.int32)) & (used > 0.0), 1.0, 0.0)
    across = (((1,), (1,)), ((), ()))
    columns[...] = lax.dot_general(
        chosen, facts[...], across, precision=lax.Precision.HIGHEST, preferred_element_type=f32
    )
    rows = lax.dot_general(
        facts[...], chosen, across, precision=lax.Precision.HIGHEST, preferred_element_type=f32
    )
    count = jnp.sum(used, axis=1, keepdims=True)
    groups = ((count + (PORT_DEV - 1)) / PORT_DEV).astype(jnp.int32)
    kind = lax.broadcasted_iota(jnp.int32, rows.shape, 0)
    unused = (kind == 0) & (lanes_of(8, REACH) >= count.astype(jnp.int32))
    whole = jnp.where(unused, PAD, (rows + 0.5).astype(jnp.int32))
    found[...] = jnp.where(kind == 7, groups, whole)


def plan(n_gz, n_gy, arrived, nodes, gains):
    lanes = -(-REACH // NODE_DEV) * NODE_DEV
    return pl.pallas_call(
        functools.partial(plan_kernel, n_gz, n_gy),
        name="plan",
        out_shape=(
            jax.ShapeDtypeStruct((8, REACH), jnp.int32),
            jax.ShapeDtypeStruct((REACH, 8), f32),
        ),
        in_specs=[VM, VM, VM],
        out_specs=(VM, VM),
        scratch_shapes=[pltpu.VMEM((8, lanes), f32)],
        compiler_params=params(),
    )(arrived, nodes.reshape(-1, NODE_DEV), gains.reshape(-1, NODE_DEV))


def halo_kernel(
    found, columns, lower, upper, before, after, before_ends, after_ends,
    e_in, h_in, coef_in, loss_in, e_xy, e_z, h, media, sample, coef, picked, sems,
):
    copies, copy = copier(sems)
    targets = [
        e_xy.at[0], e_xy.at[1], e_z, h.at[0], h.at[1], h.at[2], media.at[0], media.at[1],
    ]
    sources = [e_in.at[k] for k in range(3)] + [h_in.at[k] for k in range(3)] + [coef_in, loss_in]
    middle = pl.ds(PAD, CY)
    for part, (source, target) in enumerate(zip(sources, targets)):
        given = pl.ds(part * DEPTH, DEPTH)
        copy(source, target.at[pl.ds(DEPTH, CZ), middle])
        copy(lower.at[given], target.at[pl.ds(0, DEPTH), middle])
        copy(upper.at[given], target.at[pl.ds(DEPTH + CZ, DEPTH), middle])

    def unpack(ahead, behind, at, layer):
        for part, target in enumerate(targets):
            rows = slice(part * DEPTH, (part + 1) * DEPTH)
            target[layer, PAD - DEPTH : PAD, :] = ahead[at, rows, :]
            target[layer, PAD + CY : PAD + CY + DEPTH, :] = behind[at, rows, :]

    @pl.loop(0, CZ)
    def _(layer):
        unpack(before, after, layer, layer + DEPTH)

    @pl.loop(0, 2 * DEPTH)
    def _(end):
        unpack(before_ends, after_ends, end, jnp.where(end < DEPTH, end, end + CZ))

    for job in copies:
        job.wait()

    @pl.loop(0, LAYERS)
    def _(layer):
        media[1, layer] = 1.0 - media[1, layer]

    @pl.loop(0, found[COUNT, 0])
    def _(group):
        part = pl.ds(pl.multiple_of(group * PORT_DEV, PORT_DEV), PORT_DEV)
        _, place, _ = columns_at(columns, part)
        sample[part, :] = gather_cells(e_z, found, group, place, picked)
        coef[part, :] = gather_cells(media.at[0], found, group, place, picked)


def gather_cells(source, found, group, place, picked):
    for port in range(PORT_DEV):
        spot = found[SPOTS, group * PORT_DEV + port]
        picked[port : port + 1, :] = source[spot // TALL, pl.ds(spot % TALL, 1), :]
    return pick(picked[...], place)


def halo(found, columns, lower, upper, sides, e_in, h_in, coef, loss):
    return pl.pallas_call(
        halo_kernel,
        name="halo",
        out_shape=(
            onchip((2,) + CUBE),
            onchip(CUBE),
            onchip((3,) + CUBE),
            onchip((2,) + CUBE),
            onchip((REACH, 1)),
            onchip((REACH, 1)),
        ),
        in_specs=[SM, VM, HBM, HBM, VM, VM, VM, VM] + [HBM] * 4,
        out_specs=(VM,) * 6,
        scratch_shapes=[pltpu.VMEM((PORT_DEV, NX), f32), DMA((24,))],
        compiler_params=params(),
    )(found, columns, away(lower), away(upper), *sides, *map(away, (e_in, h_in, coef, loss)))


def field_kernel(step, media, e_xy, e_z, h, to_xy, to_z, to_h):
    low_z = jnp.where(lax.axis_index("gz") > 0, 1.0, 0.0)
    low_y = jnp.where(lax.axis_index("gy") > 0, time_step, 0.0)
    lane = lanes_of(TALL, NX)
    last_lane, first_lane = lane == NX - 1, lane == 0
    row = lax.broadcasted_iota(jnp.int32, (TALL, NX), 0)
    rate_rows = jnp.where(row < PAD, low_y, time_step)

    def next_x(value):
        return jnp.where(last_lane, 0.0, pltpu.roll(value, NX - 1, 1))

    def prior_x(value):
        return jnp.where(first_lane, 0.0, pltpu.roll(value, 1, 1))

    def next_y(value):
        return pltpu.roll(value, TALL - 1, 0)

    def prior_y(value):
        return pltpu.roll(value, 1, 0)

    def magnetic(layer):
        e_x, e_y, e_zz = e_xy[0, layer], e_xy[1, layer], e_z[layer]
        rate = rate_rows * jnp.where(layer < DEPTH, low_z, 1.0)
        curl_x = (next_y(e_zz) - e_zz) - (e_xy[1, layer + 1] - e_y)
        curl_y = (e_xy[0, layer + 1] - e_x) - (next_x(e_zz) - e_zz)
        curl_z = (next_x(e_y) - e_y) - (next_y(e_x) - e_x)
        return (h[0, layer] - rate * curl_x, h[1, layer] - rate * curl_y, h[2, layer] - rate * curl_z)

    def electric(layer):
        h_x, h_y, h_z = to_h[0, layer], to_h[1, layer], to_h[2, layer]
        coef, kept = media[0, layer], media[1, layer]
        back_x = (h_z - prior_y(h_z)) - (h_y - to_h[1, layer - 1])
        back_y = (h_x - to_h[0, layer - 1]) - (h_z - prior_x(h_z))
        back_z = (h_y - prior_x(h_y)) - (h_x - prior_y(h_x))
        return (
            kept * e_xy[0, layer] + coef * back_x,
            kept * e_xy[1, layer] + coef * back_y,
            kept * e_z[layer] + coef * back_z,
        )

    def put_h(layer, values):
        to_h[0, layer], to_h[1, layer], to_h[2, layer] = values

    def put_e(layer, values):
        to_xy[0, layer], to_xy[1, layer], to_z[layer] = values

    put_h(step - 1, magnetic(step - 1))
    put_h(step, magnetic(step))
    last = LAYERS - step - 1

    @pl.loop(step, last)
    def _(layer):
        electric_values = electric(layer)
        magnetic_values = magnetic(layer + 1)
        put_e(layer, electric_values)
        put_h(layer + 1, magnetic_values)

    put_e(last, electric(last))


def field(step, media, e_xy, e_z, h):
    return pl.pallas_call(
        functools.partial(field_kernel, step),
        name="field",
        out_shape=(onchip((2,) + CUBE), onchip(CUBE), onchip((3,) + CUBE)),
        in_specs=[VM] * 4,
        out_specs=(VM,) * 3,
        compiler_params=params(),
    )(keep(media), keep(e_xy), keep(e_z), keep(h))


def solve(stride, arrived, off_cols, volts, m_off, m_diag, m_inv):
    lane = lanes_of(1, NODE_DEV)
    halves = []
    for j in range(NB_DEV):
        pieces = []
        for half in range(OFF // 2):
            total = None
            for side in range(2):
                column = off_cols[j, half * 2 + side]
                row = arrived[pl.ds(column // NB_DEV * stride, 1), :]
                row = jnp.where(column % NB_DEV == side, row, pltpu.roll(row, BS, 1))
                row = jnp.where((lane < BS) == (side == 0), row, 0.0)
                total = row if total is None else total + row
            pieces.append(jnp.broadcast_to(total, (BS, NODE_DEV)))
        halves.append(pieces)
    first = jnp.concatenate([halves[0][0], halves[1][0]], axis=0)
    second = jnp.concatenate([halves[0][1], halves[1][1]], axis=0)
    product = m_off[:, 0:NODE_DEV] * first + m_off[:, NODE_DEV : 2 * NODE_DEV] * second
    offsum = jnp.sum(product, axis=1, keepdims=True)
    kind = row_kind(arrived.shape, stride)
    inject = jnp.sum(jnp.where(kind == 1, arrived[...], 0.0), axis=0, keepdims=True)
    start = volts[...]
    target = charge_scale * start + inject
    diagonal = lax.broadcasted_iota(jnp.int32, (NODE_DEV, NODE_DEV), 0) == lanes_of(NODE_DEV, NODE_DEV)
    iterate = start
    for newton_round in range(NEWTON):
        local = diode_weight * jnp.tanh(iterate) - target
        terms = m_diag[...] * iterate + jnp.where(diagonal, local, 0.0)
        resid = jnp.sum(terms, axis=1, keepdims=True) + offsum
        iterate = iterate - jnp.sum(m_inv[...] * resid, axis=0, keepdims=True)
    return iterate


def apply_ports(stride, table, arrived, columns, sample, coef, e_z, near_rows, deltas):
    @pl.loop(0, table[COUNT, 0])
    def _(group):
        first = group * PORT_DEV
        part = pl.ds(pl.multiple_of(first, PORT_DEV), PORT_DEV)
        for port in range(PORT_DEV):
            near_at = table[NODES, first + port] * stride
            near_rows[port : port + 1, :] = arrived[pl.ds(near_at, 1), :]
        gain, place, lane = columns_at(columns, part)
        current = gain * (sample[part, :] - pick(near_rows[...], lane))
        deltas[...] = spread(-coef[part, :] * current, place, NX)
        for port in range(PORT_DEV):
            spot = table[SPOTS, first + port]
            layer, row = spot // TALL, pl.ds(spot % TALL, 1)
            e_z[layer, row, :] = e_z[layer, row, :] + deltas[port : port + 1, :]


def circuit_kernel(
    stride, table, off_cols, arrived, columns, sample, coef, volts, m_off, m_diag, m_inv, e_in,
    e_z, out, volts_out, sample_out, near_rows, deltas, picked, spread_rows,
):
    e_z[...] = e_in[...]
    apply_ports(stride, table, arrived, columns, sample, coef, e_z, near_rows, deltas)

    @pl.loop(0, table[COUNT, 0])
    def _(group):
        part = pl.ds(pl.multiple_of(group * PORT_DEV, PORT_DEV), PORT_DEV)
        _, place, _ = columns_at(columns, part)
        sample_out[part, :] = gather_cells(e_z, table, group, place, picked)

    solved = solve(stride, arrived, off_cols, volts, m_off, m_diag, m_inv)
    volts_out[...] = solved
    own = slice(0, PORT_DEV)
    gain, _, lane = columns_at(columns, own)
    spread_rows[...] = spread(gain * sample_out[own, :], lane, NODE_DEV)
    out[...] = jnp.where(row_kind(out.shape, 2) == 0, solved, 0.0)
    add_rows(out, 2, [table[NODES, port] for port in range(PORT_DEV)], spread_rows)


def circuit(table, off_cols, arrived, columns, sample, coef, volts, mats, e_z):
    return pl.pallas_call(
        functools.partial(circuit_kernel, arrived.shape[0] // ND),
        name="circuit",
        out_shape=(
            onchip(CUBE),
            onchip((2 * ND, NODE_DEV)),
            onchip((1, NODE_DEV)),
            onchip((REACH, 1)),
        ),
        in_specs=[SM, SM] + [VM] * 9,
        out_specs=(VM,) * 4,
        scratch_shapes=[
            pltpu.VMEM((PORT_DEV, NODE_DEV), f32),
            pltpu.VMEM((PORT_DEV, NX), f32),
            pltpu.VMEM((PORT_DEV, NX), f32),
            pltpu.VMEM((PORT_DEV, NODE_DEV), f32),
        ],
        compiler_params=params(),
    )(
        table, off_cols, arrived, columns, keep(sample), keep(coef), volts,
        *[keep(mat) for mat in mats], keep(e_z),
    )


def finish_kernel(
    stride, table, off_cols, arrived, columns, sample, coef, volts, m_off, m_diag, m_inv, e_xy, e_in, h,
    e_out, h_out, volts_out, e_z, near_rows, deltas, sems,
):
    copies, copy = copier(sems)
    layers, rows = pl.ds(DEPTH, CZ), pl.ds(PAD, CY)
    for k in range(3):
        copy(h.at[k, layers, rows], h_out.at[k])
    for k in range(2):
        copy(e_xy.at[k, layers, rows], e_out.at[k])
    e_z[...] = e_in[...]
    apply_ports(stride, table, arrived, columns, sample, coef, e_z, near_rows, deltas)
    copy(e_z.at[layers, rows], e_out.at[2])
    volts_out[...] = solve(stride, arrived, off_cols, volts, m_off, m_diag, m_inv)
    for job in copies:
        job.wait()


def finish(table, off_cols, arrived, columns, sample, coef, volts, mats, e_xy, e_z, h):
    return pl.pallas_call(
        functools.partial(finish_kernel, arrived.shape[0] // ND),
        name="finish",
        out_shape=(
            jax.ShapeDtypeStruct((3, CZ, CY, NX), f32),
            jax.ShapeDtypeStruct((3, CZ, CY, NX), f32),
            jax.ShapeDtypeStruct((1, NODE_DEV), f32),
        ),
        in_specs=[SM, SM] + [VM] * 11,
        out_specs=(HBM, HBM, VM),
        scratch_shapes=[
            pltpu.VMEM(CUBE, f32),
            pltpu.VMEM((PORT_DEV, NODE_DEV), f32),
            pltpu.VMEM((PORT_DEV, NX), f32),
            DMA((6,)),
        ],
        compiler_params=params(),
    )(
        table, off_cols, arrived, columns, keep(sample), keep(coef), volts,
        *[keep(mat) for mat in mats], keep(e_xy), keep(e_z), keep(h),
    )


def shifted(value, axis, steps):
    count = lax.axis_size(axis)
    first, last = (max(0, -steps), min(count, count - steps))
    return lax.ppermute(value, axis, [(source, source + steps) for source in range(first, last)])


def exchange(value):
    return lax.all_to_all(value, ("gz", "gy"), 0, 0, tiled=True)


def body(
    e_field,
    h_field,
    e_coef,
    e_loss,
    port_cell,
    port_node,
    port_gain,
    diag_blocks,
    inv_blocks,
    off_blocks,
    off_cols,
    volts_init,
):
    n_gz, n_gy = lax.axis_size("gz"), lax.axis_size("gy")
    grids = (e_field, h_field, e_coef, e_loss)
    volts = volts_init.reshape(1, NODE_DEV)
    front = strip_of(True, grids, volts)
    before = shifted(front, "gy", 1)
    back = strip_of(False, grids, front)
    after = shifted(back, "gy", -1)
    up = slab_of(True, grids, back)
    lower = shifted(up, "gz", 1)
    down = slab_of(False, grids, up)
    upper = shifted(down, "gz", -1)
    out = begin(n_gy, port_cell, port_node, port_gain, e_field, volts, down)
    arrived = exchange(out)
    front_ends, back_ends = corners(lower, upper, out)
    before_ends = shifted(front_ends, "gy", 1)
    after_ends = shifted(back_ends, "gy", -1)
    arrived, front_ends, back_ends = lax.optimization_barrier((arrived, front_ends, back_ends))
    sides = (before, after, before_ends, after_ends)
    mats = matrices(diag_blocks, inv_blocks, off_blocks)

    table, columns = plan(n_gz, n_gy, arrived, port_node, port_gain)

    e_xy, e_z, h, media, sample, coef = halo(table, columns, lower, upper, sides, *grids)
    for step in range(1, STEPS + 1):
        if step > 1:
            arrived = exchange(out)
            arrived, e_z = lax.optimization_barrier((arrived, e_z))
        e_xy, e_z, h = field(step, media, e_xy, e_z, h)
        shared = (table, off_cols, arrived, columns, sample, coef, volts, mats)
        if step < STEPS:
            e_z, out, volts, sample = circuit(*shared, e_z)
        else:
            e_end, h_end, volts = finish(*shared, e_xy, e_z, h)
    return e_end, h_end, volts.reshape(-1)


def solution(mesh):
    placed = (
        P(None, "gz", "gy", None),
        P(None, "gz", "gy", None),
        P("gz", "gy", None),
        P("gz", "gy", None),
        P(("gz", "gy")),
        P(),
        P(),
        P(("gz", "gy"), None, None),
        P(("gz", "gy"), None, None),
        P(("gz", "gy"), None, None, None),
        P(("gz", "gy"), None),
        P(("gz", "gy")),
    )
    return jax.shard_map(
        body,
        mesh=mesh,
        in_specs=placed,
        out_specs=(P(None, "gz", "gy", None), P(None, "gz", "gy", None), P(("gz", "gy"))),
        check_vma=False,
    )
```

```python
import functools

import jax
import jax.numpy as jnp
from jax import lax
from jax.experimental import pallas as pl
from jax.experimental.pallas import tpu as pltpu
from jax.sharding import PartitionSpec as P

STEPS = 5
NEWTON = 2
BS = 64
NB_DEV = 2
OFF = 4
PORT_DEV = 32
ND = 128
NODE_DEV = NB_DEV * BS
DEPTH = 5
CZ, CY, NX = 32, 16, 256
LAYERS = CZ + 2 * DEPTH
PAD = 8
TALL = CY + 2 * PAD
PARTS = 8
STRIP = PARTS * DEPTH
SIDES = ((0, 0), (-1, 0), (1, 0), (0, -1), (-1, -1), (1, -1), (0, 1), (-1, 1), (1, 1))
REACH = len(SIDES) * PORT_DEV
NODES, COUNT = REACH, 2 * REACH

time_step = 0.55
charge_scale = 4.0
diode_weight = 0.5

f32 = jnp.float32
VM = pl.BlockSpec(memory_space=pltpu.VMEM)
SM = pl.BlockSpec(memory_space=pltpu.SMEM)
HBM = pl.BlockSpec(memory_space=pltpu.HBM)
ANY = pl.BlockSpec(memory_space=pl.ANY)
DMA = pltpu.SemaphoreType.DMA
CUBE = (LAYERS, TALL, NX)


def onchip(shape):
    return pltpu.VMEM(shape, f32)


def keep(value):
    return pltpu.with_memory_space_constraint(value, pltpu.VMEM)


def away(value):
    return pltpu.with_memory_space_constraint(value, pltpu.HBM)


def params():
    return pltpu.CompilerParams(vmem_limit_bytes=12 << 20)


def lanes_of(count, width):
    return lax.broadcasted_iota(jnp.int32, (count, width), 1)


def pick(rows, lane):
    hit = lanes_of(rows.shape[0], rows.shape[1]) == lane
    return jnp.sum(jnp.where(hit, rows, 0.0), axis=1, keepdims=True)


def spread(column, lane, width):
    hit = lanes_of(column.shape[0], width) == lane
    return jnp.where(hit, column, 0.0)


def columns_at(columns, part):
    block = columns[part, :]
    return block[:, 2:3], block[:, 3:4].astype(jnp.int32), block[:, 4:5].astype(jnp.int32)


def row_kind(shape, stride):
    return lax.broadcasted_iota(jnp.int32, shape, 0) % stride


def add_rows(out, stride, devices, rows_ref):
    for port, device in enumerate(devices):
        spot = pl.ds(device * stride + 1, 1)
        out[spot, :] = out[spot, :] + rows_ref[port : port + 1, :]


def copier(sems):
    copies = []

    def copy(source, target):
        job = pltpu.make_async_copy(source, target, sems.at[len(copies)])
        job.start()
        copies.append(job)

    return copies, copy


def sources_of(e_in, h_in, coef_in, loss_in):
    return [e_in.at[k] for k in range(3)] + [h_in.at[k] for k in range(3)] + [coef_in, loss_in]


def strip_kernel(top, e_in, h_in, coef_in, loss_in, after, strip, fields, sems):
    copies, copy = copier(sems)
    rows = pl.ds(CY - 8 if top else 0, 8)
    for part, source in enumerate(sources_of(e_in, h_in, coef_in, loss_in)):
        copy(source.at[:, rows], fields.at[part])
    for job in copies:
        job.wait()
    given = slice(8 - DEPTH, 8) if top else slice(0, DEPTH)

    @pl.loop(0, CZ)
    def _(layer):
        for part in range(PARTS):
            strip[layer, part * DEPTH : (part + 1) * DEPTH, :] = fields[part, layer, given, :]


def strip_of(top, grids, after):
    return pl.pallas_call(
        functools.partial(strip_kernel, top),
        name="strip",
        out_shape=jax.ShapeDtypeStruct((CZ, STRIP, NX), f32),
        in_specs=[HBM] * 4 + [ANY],
        out_specs=VM,
        scratch_shapes=[pltpu.VMEM((PARTS, CZ, 8, NX), f32), DMA((PARTS,))],
        compiler_params=params(),
    )(*map(away, grids), after)


def slab_kernel(top, e_in, h_in, coef_in, loss_in, after, slab, sems):
    copies, copy = copier(sems)
    layers = pl.ds(CZ - DEPTH if top else 0, DEPTH)
    for part, source in enumerate(sources_of(e_in, h_in, coef_in, loss_in)):
        copy(source.at[layers], slab.at[pl.ds(part * DEPTH, DEPTH)])
    for job in copies:
        job.wait()


def slab_of(top, grids, after):
    return pl.pallas_call(
        functools.partial(slab_kernel, top),
        name="slab",
        out_shape=jax.ShapeDtypeStruct((PARTS * DEPTH, CY, NX), f32),
        in_specs=[HBM] * 4 + [ANY],
        out_specs=VM,
        scratch_shapes=[DMA((PARTS,))],
        compiler_params=params(),
    )(*map(away, grids), after)


def begin_kernel(
    n_gy, cells, nodes, gains, e_in, cell_row, volts, after, out, e_z, picked, hits, rows_ref, sem,
):
    load = pltpu.make_async_copy(e_in.at[2], e_z, sem)
    load.start()
    first = (lax.axis_index("gz") * n_gy + lax.axis_index("gy")) * PORT_DEV
    wide, narrow = lanes_of(1, NX), lanes_of(1, NODE_DEV)
    own_nodes = [nodes[first + port] for port in range(PORT_DEV)]
    for port, node in enumerate(own_nodes):
        hits[port : port + 1, :] = jnp.where(narrow == node % NODE_DEV, 1.0, 0.0)
    kind = row_kind(out.shape, 4)
    rows_ref[0:1, :] = jnp.zeros((1, NODE_DEV), f32)
    rows_ref[0:1, 0:PORT_DEV] = cell_row[...].astype(f32)
    out[...] = jnp.where(kind == 0, volts[...], jnp.where(kind == 2, rows_ref[0:1, :], 0.0))

    load.wait()
    for port in range(PORT_DEV):
        cell = cells[port]
        line = cell // NX
        value = e_z[line // CY, pl.ds(line % CY, 1), :] * gains[first + port]
        picked[port : port + 1, :] = jnp.where(wide == cell % NX, value, 0.0)
    rows_ref[...] = hits[...] * jnp.sum(picked[...], axis=1, keepdims=True)
    add_rows(out, 4, [node // NODE_DEV for node in own_nodes], rows_ref)


def begin(n_gy, cells, nodes, gains, e_in, volts, after):
    return pl.pallas_call(
        functools.partial(begin_kernel, n_gy),
        name="begin",
        out_shape=jax.ShapeDtypeStruct((4 * ND, NODE_DEV), f32),
        in_specs=[SM, SM, SM, HBM, VM, VM, ANY],
        out_specs=VM,
        scratch_shapes=[
            pltpu.VMEM((CZ, CY, NX), f32),
            pltpu.VMEM((PORT_DEV, NX), f32),
            pltpu.VMEM((PORT_DEV, NODE_DEV), f32),
            pltpu.VMEM((PORT_DEV, NODE_DEV), f32),
            DMA,
        ],
        compiler_params=params(),
    )(cells, nodes, gains, away(e_in), cells.reshape(1, -1), volts, after)


def matrices_kernel(diag, inv, off, m_off, m_diag, m_inv):
    m_diag[...] = jnp.zeros_like(m_diag)
    m_inv[...] = jnp.zeros_like(m_inv)
    for j in range(NB_DEV):
        part = slice(j * BS, (j + 1) * BS)
        m_diag[part, part] = diag[j]
        m_inv[part, part] = inv[j].T
        for k in range(OFF):
            m_off[part, k * BS : (k + 1) * BS] = off[j, k]


def matrices(diag, inv, off):
    square = onchip((NODE_DEV, NODE_DEV))
    return pl.pallas_call(
        matrices_kernel,
        name="matrices",
        out_shape=(onchip((NODE_DEV, OFF * BS)), square, square),
        in_specs=[VM, VM, VM],
        out_specs=(VM, VM, VM),
        compiler_params=params(),
    )(diag, inv, off)


def corners_kernel(lower, upper, after, front, back):
    for side, source in enumerate((lower, upper)):
        for layer in range(DEPTH):
            for part in range(PARTS):
                to = slice(part * DEPTH, (part + 1) * DEPTH)
                given = part * DEPTH + layer
                front[side * DEPTH + layer, to, :] = source[given, CY - DEPTH : CY, :]
                back[side * DEPTH + layer, to, :] = source[given, 0:DEPTH, :]


def corners(lower, upper, after):
    shape = jax.ShapeDtypeStruct((2 * DEPTH, STRIP, NX), f32)
    return pl.pallas_call(
        corners_kernel,
        name="corners",
        out_shape=(shape, shape),
        in_specs=[VM, VM, ANY],
        out_specs=(VM, VM),
        compiler_params=params(),
    )(lower, upper, after)


def plan_kernel(n_gz, n_gy, arrived, nodes, gains, found, columns, facts):
    gz, gy = lax.axis_index("gz"), lax.axis_index("gy")
    lane = lanes_of(1, NODE_DEV)
    width = NODE_DEV // PORT_DEV
    facts[...] = jnp.zeros_like(facts)
    for group, (side_z, side_y) in enumerate(SIDES):
        at_z, at_y = gz + side_z, gy + side_y
        exists = (at_z >= 0) & (at_z < n_gz) & (at_y >= 0) & (at_y < n_gy)
        device = jnp.where(exists, at_z * n_gy + at_y, 0)
        slot = group % width
        turn = (slot - device % width + width) % width * PORT_DEV
        row = pl.ds(device // width, 1)
        node, gain = pltpu.roll(nodes[row, :], turn, 1), pltpu.roll(gains[row, :], turn, 1)
        cell = pltpu.roll(arrived[pl.ds(4 * device + 2, 1), :], slot * PORT_DEV, 1).astype(jnp.int32)
        layer = cell // (CY * NX) + (side_z * CZ + DEPTH)
        line = (cell // NX) % CY + (side_y * CY + PAD)
        valid = (layer >= 1) & (layer < LAYERS - 1)
        valid &= (line > PAD - DEPTH) & (line < PAD + CY + DEPTH - 1)
        valid &= (lane // PORT_DEV == slot) & (jnp.where(exists, 1, 0) > 0)
        values = (layer * TALL + line, node // NODE_DEV, gain, cell % NX, node % NODE_DEV, 1)
        part = slice(group // width * NODE_DEV, (group // width + 1) * NODE_DEV)
        for kind, value in enumerate(values):
            fact = jnp.where(valid, jnp.asarray(value).astype(f32), 0.0)
            facts[kind : kind + 1, part] = facts[kind : kind + 1, part] + fact

    used = facts[5:6, :]
    total = used.shape[1]
    upper = lax.broadcasted_iota(jnp.int32, (total, total), 0) <= lanes_of(total, total)
    ones = jnp.broadcast_to(used, (8, total))
    order = jnp.dot(ones, upper.astype(f32), preferred_element_type=f32)[0:1, :] - 1.0
    spot = lax.broadcasted_iota(jnp.int32, (REACH, total), 0)
    chosen = jnp.where((spot == order.astype(jnp.int32)) & (used > 0.0), 1.0, 0.0)
    across = (((1,), (1,)), ((), ()))
    columns[...] = lax.dot_general(
        chosen, facts[...], across, precision=lax.Precision.HIGHEST, preferred_element_type=f32
    )
    rows = lax.dot_general(
        facts[...], chosen, across, precision=lax.Precision.HIGHEST, preferred_element_type=f32
    )
    count = jnp.sum(used, axis=1, keepdims=True)
    groups = ((count + (PORT_DEV - 1)) / PORT_DEV).astype(jnp.int32)
    kind = lax.broadcasted_iota(jnp.int32, rows.shape, 0)
    unused = (kind == 0) & (lanes_of(8, REACH) >= count.astype(jnp.int32))
    whole = jnp.where(unused, PAD, (rows + 0.5).astype(jnp.int32))
    found[...] = jnp.where(kind == 7, groups, whole)


def plan(n_gz, n_gy, arrived, nodes, gains):
    lanes = -(-REACH // NODE_DEV) * NODE_DEV
    return pl.pallas_call(
        functools.partial(plan_kernel, n_gz, n_gy),
        name="plan",
        out_shape=(
            jax.ShapeDtypeStruct((8, REACH), jnp.int32),
            jax.ShapeDtypeStruct((REACH, 8), f32),
        ),
        in_specs=[VM, VM, VM],
        out_specs=(VM, VM),
        scratch_shapes=[pltpu.VMEM((8, lanes), f32)],
        compiler_params=params(),
    )(arrived, nodes.reshape(-1, NODE_DEV), gains.reshape(-1, NODE_DEV))


def halo_kernel(
    found, columns, lower, upper, before, after, before_ends, after_ends,
    e_in, h_in, coef_in, loss_in, e_xy, e_z, h, media, sample, coef, picked, sems,
):
    copies, copy = copier(sems)
    targets = [
        e_xy.at[0], e_xy.at[1], e_z, h.at[0], h.at[1], h.at[2], media.at[0], media.at[1],
    ]
    sources = [e_in.at[k] for k in range(3)] + [h_in.at[k] for k in range(3)] + [coef_in, loss_in]
    middle = pl.ds(PAD, CY)
    for part, (source, target) in enumerate(zip(sources, targets)):
        given = pl.ds(part * DEPTH, DEPTH)
        copy(source, target.at[pl.ds(DEPTH, CZ), middle])
        copy(lower.at[given], target.at[pl.ds(0, DEPTH), middle])
        copy(upper.at[given], target.at[pl.ds(DEPTH + CZ, DEPTH), middle])

    def unpack(ahead, behind, at, layer):
        for part, target in enumerate(targets):
            rows = slice(part * DEPTH, (part + 1) * DEPTH)
            target[layer, PAD - DEPTH : PAD, :] = ahead[at, rows, :]
            target[layer, PAD + CY : PAD + CY + DEPTH, :] = behind[at, rows, :]

    @pl.loop(0, CZ)
    def _(layer):
        unpack(before, after, layer, layer + DEPTH)

    @pl.loop(0, 2 * DEPTH)
    def _(end):
        unpack(before_ends, after_ends, end, jnp.where(end < DEPTH, end, end + CZ))

    for job in copies:
        job.wait()

    @pl.loop(0, LAYERS)
    def _(layer):
        media[1, layer] = 1.0 - media[1, layer]

    @pl.loop(0, found[COUNT])
    def _(group):
        part = pl.ds(pl.multiple_of(group * PORT_DEV, PORT_DEV), PORT_DEV)
        _, place, _ = columns_at(columns, part)
        sample[part, :] = gather_cells(e_z, found, group, place, picked)
        coef[part, :] = gather_cells(media.at[0], found, group, place, picked)


def gather_cells(source, found, group, place, picked):
    for port in range(PORT_DEV):
        spot = found[group * PORT_DEV + port]
        picked[port : port + 1, :] = source[spot // TALL, pl.ds(spot % TALL, 1), :]
    return pick(picked[...], place)


def halo(found, columns, lower, upper, sides, e_in, h_in, coef, loss):
    return pl.pallas_call(
        halo_kernel,
        name="halo",
        out_shape=(
            onchip((2,) + CUBE),
            onchip(CUBE),
            onchip((3,) + CUBE),
            onchip((2,) + CUBE),
            onchip((REACH, 1)),
            onchip((REACH, 1)),
        ),
        in_specs=[SM, VM, HBM, HBM, VM, VM, VM, VM] + [HBM] * 4,
        out_specs=(VM,) * 6,
        scratch_shapes=[pltpu.VMEM((PORT_DEV, NX), f32), DMA((24,))],
        compiler_params=params(),
    )(found, columns, away(lower), away(upper), *sides, *map(away, (e_in, h_in, coef, loss)))


def field_kernel(step, media, e_xy, e_z, h, to_xy, to_z, to_h):
    low_z = jnp.where(lax.axis_index("gz") > 0, 1.0, 0.0)
    low_y = jnp.where(lax.axis_index("gy") > 0, time_step, 0.0)
    lane = lanes_of(TALL, NX)
    last_lane, first_lane = lane == NX - 1, lane == 0
    row = lax.broadcasted_iota(jnp.int32, (TALL, NX), 0)
    rate_rows = jnp.where(row < PAD, low_y, time_step)

    def next_x(value):
        return jnp.where(last_lane, 0.0, pltpu.roll(value, NX - 1, 1))

    def prior_x(value):
        return jnp.where(first_lane, 0.0, pltpu.roll(value, 1, 1))

    def next_y(value):
        return pltpu.roll(value, TALL - 1, 0)

    def prior_y(value):
        return pltpu.roll(value, 1, 0)

    def magnetic(layer):
        e_x, e_y, e_zz = e_xy[0, layer], e_xy[1, layer], e_z[layer]
        rate = rate_rows * jnp.where(layer < DEPTH, low_z, 1.0)
        curl_x = (next_y(e_zz) - e_zz) - (e_xy[1, layer + 1] - e_y)
        curl_y = (e_xy[0, layer + 1] - e_x) - (next_x(e_zz) - e_zz)
        curl_z = (next_x(e_y) - e_y) - (next_y(e_x) - e_x)
        return (h[0, layer] - rate * curl_x, h[1, layer] - rate * curl_y, h[2, layer] - rate * curl_z)

    def electric(layer):
        h_x, h_y, h_z = to_h[0, layer], to_h[1, layer], to_h[2, layer]
        coef, kept = media[0, layer], media[1, layer]
        back_x = (h_z - prior_y(h_z)) - (h_y - to_h[1, layer - 1])
        back_y = (h_x - to_h[0, layer - 1]) - (h_z - prior_x(h_z))
        back_z = (h_y - prior_x(h_y)) - (h_x - prior_y(h_x))
        return (
            kept * e_xy[0, layer] + coef * back_x,
            kept * e_xy[1, layer] + coef * back_y,
            kept * e_z[layer] + coef * back_z,
        )

    def put_h(layer, values):
        to_h[0, layer], to_h[1, layer], to_h[2, layer] = values

    def put_e(layer, values):
        to_xy[0, layer], to_xy[1, layer], to_z[layer] = values

    put_h(step - 1, magnetic(step - 1))
    put_h(step, magnetic(step))
    last = LAYERS - step - 1

    @pl.loop(step, last)
    def _(layer):
        electric_values = electric(layer)
        magnetic_values = magnetic(layer + 1)
        put_e(layer, electric_values)
        put_h(layer + 1, magnetic_values)

    put_e(last, electric(last))


def field(step, media, e_xy, e_z, h):
    return pl.pallas_call(
        functools.partial(field_kernel, step),
        name="field",
        out_shape=(onchip((2,) + CUBE), onchip(CUBE), onchip((3,) + CUBE)),
        in_specs=[VM] * 4,
        out_specs=(VM,) * 3,
        compiler_params=params(),
    )(keep(media), keep(e_xy), keep(e_z), keep(h))


def solve(stride, arrived, off_cols, volts, m_off, m_diag, m_inv):
    lane = lanes_of(1, NODE_DEV)
    halves = []
    for j in range(NB_DEV):
        pieces = []
        for half in range(OFF // 2):
            total = None
            for side in range(2):
                column = off_cols[j, half * 2 + side]
                row = arrived[pl.ds(column // NB_DEV * stride, 1), :]
                row = jnp.where(column % NB_DEV == side, row, pltpu.roll(row, BS, 1))
                row = jnp.where((lane < BS) == (side == 0), row, 0.0)
                total = row if total is None else total + row
            pieces.append(jnp.broadcast_to(total, (BS, NODE_DEV)))
        halves.append(pieces)
    first = jnp.concatenate([halves[0][0], halves[1][0]], axis=0)
    second = jnp.concatenate([halves[0][1], halves[1][1]], axis=0)
    product = m_off[:, 0:NODE_DEV] * first + m_off[:, NODE_DEV : 2 * NODE_DEV] * second
    offsum = jnp.sum(product, axis=1, keepdims=True)
    kind = row_kind(arrived.shape, stride)
    inject = jnp.sum(jnp.where(kind == 1, arrived[...], 0.0), axis=0, keepdims=True)
    start = volts[...]
    target = charge_scale * start + inject
    diagonal = lax.broadcasted_iota(jnp.int32, (NODE_DEV, NODE_DEV), 0) == lanes_of(NODE_DEV, NODE_DEV)
    iterate = start
    for newton_round in range(NEWTON):
        local = diode_weight * jnp.tanh(iterate) - target
        terms = m_diag[...] * iterate + jnp.where(diagonal, local, 0.0)
        resid = jnp.sum(terms, axis=1, keepdims=True) + offsum
        iterate = iterate - jnp.sum(m_inv[...] * resid, axis=0, keepdims=True)
    return iterate


def apply_ports(stride, table, arrived, columns, sample, coef, e_z, near_rows, deltas):
    @pl.loop(0, table[COUNT])
    def _(group):
        first = group * PORT_DEV
        part = pl.ds(pl.multiple_of(first, PORT_DEV), PORT_DEV)
        for port in range(PORT_DEV):
            near_at = table[NODES + first + port] * stride
            near_rows[port : port + 1, :] = arrived[pl.ds(near_at, 1), :]
        gain, place, lane = columns_at(columns, part)
        current = gain * (sample[part, :] - pick(near_rows[...], lane))
        deltas[...] = spread(-coef[part, :] * current, place, NX)
        for port in range(PORT_DEV):
            spot = table[first + port]
            layer, row = spot // TALL, pl.ds(spot % TALL, 1)
            e_z[layer, row, :] = e_z[layer, row, :] + deltas[port : port + 1, :]


def circuit_kernel(
    stride, table, off_cols, arrived, columns, sample, coef, volts, m_off, m_diag, m_inv, e_in,
    e_z, out, volts_out, sample_out, near_rows, deltas, picked, spread_rows,
):
    e_z[...] = e_in[...]
    apply_ports(stride, table, arrived, columns, sample, coef, e_z, near_rows, deltas)

    @pl.loop(0, table[COUNT])
    def _(group):
        part = pl.ds(pl.multiple_of(group * PORT_DEV, PORT_DEV), PORT_DEV)
        _, place, _ = columns_at(columns, part)
        sample_out[part, :] = gather_cells(e_z, table, group, place, picked)

    solved = solve(stride, arrived, off_cols, volts, m_off, m_diag, m_inv)
    volts_out[...] = solved
    own = slice(0, PORT_DEV)
    gain, _, lane = columns_at(columns, own)
    spread_rows[...] = spread(gain * sample_out[own, :], lane, NODE_DEV)
    out[...] = jnp.where(row_kind(out.shape, 2) == 0, solved, 0.0)
    add_rows(out, 2, [table[NODES + port] for port in range(PORT_DEV)], spread_rows)


def circuit(table, off_cols, arrived, columns, sample, coef, volts, mats, e_z):
    return pl.pallas_call(
        functools.partial(circuit_kernel, arrived.shape[0] // ND),
        name="circuit",
        out_shape=(
            onchip(CUBE),
            onchip((2 * ND, NODE_DEV)),
            onchip((1, NODE_DEV)),
            onchip((REACH, 1)),
        ),
        in_specs=[SM, SM] + [VM] * 9,
        out_specs=(VM,) * 4,
        scratch_shapes=[
            pltpu.VMEM((PORT_DEV, NODE_DEV), f32),
            pltpu.VMEM((PORT_DEV, NX), f32),
            pltpu.VMEM((PORT_DEV, NX), f32),
            pltpu.VMEM((PORT_DEV, NODE_DEV), f32),
        ],
        compiler_params=params(),
    )(
        table, off_cols, arrived, columns, keep(sample), keep(coef), volts,
        *[keep(mat) for mat in mats], keep(e_z),
    )


def finish_kernel(
    stride, table, off_cols, arrived, columns, sample, coef, volts, m_off, m_diag, m_inv, e_xy, e_in, h,
    e_out, h_out, volts_out, e_z, near_rows, deltas, sems,
):
    copies, copy = copier(sems)
    layers, rows = pl.ds(DEPTH, CZ), pl.ds(PAD, CY)
    for k in range(3):
        copy(h.at[k, layers, rows], h_out.at[k])
    for k in range(2):
        copy(e_xy.at[k, layers, rows], e_out.at[k])
    e_z[...] = e_in[...]
    apply_ports(stride, table, arrived, columns, sample, coef, e_z, near_rows, deltas)
    copy(e_z.at[layers, rows], e_out.at[2])
    volts_out[...] = solve(stride, arrived, off_cols, volts, m_off, m_diag, m_inv)
    for job in copies:
        job.wait()


def finish(table, off_cols, arrived, columns, sample, coef, volts, mats, e_xy, e_z, h):
    return pl.pallas_call(
        functools.partial(finish_kernel, arrived.shape[0] // ND),
        name="finish",
        out_shape=(
            jax.ShapeDtypeStruct((3, CZ, CY, NX), f32),
            jax.ShapeDtypeStruct((3, CZ, CY, NX), f32),
            jax.ShapeDtypeStruct((1, NODE_DEV), f32),
        ),
        in_specs=[SM, SM] + [VM] * 11,
        out_specs=(HBM, HBM, VM),
        scratch_shapes=[
            pltpu.VMEM(CUBE, f32),
            pltpu.VMEM((PORT_DEV, NODE_DEV), f32),
            pltpu.VMEM((PORT_DEV, NX), f32),
            DMA((6,)),
        ],
        compiler_params=params(),
    )(
        table, off_cols, arrived, columns, keep(sample), keep(coef), volts,
        *[keep(mat) for mat in mats], keep(e_xy), keep(e_z), keep(h),
    )


def shifted(value, axis, steps):
    count = lax.axis_size(axis)
    first, last = (max(0, -steps), min(count, count - steps))
    return lax.ppermute(value, axis, [(source, source + steps) for source in range(first, last)])


def exchange(value):
    return lax.all_to_all(value, ("gz", "gy"), 0, 0, tiled=True)


def body(
    e_field,
    h_field,
    e_coef,
    e_loss,
    port_cell,
    port_node,
    port_gain,
    diag_blocks,
    inv_blocks,
    off_blocks,
    off_cols,
    volts_init,
):
    n_gz, n_gy = lax.axis_size("gz"), lax.axis_size("gy")
    grids = (e_field, h_field, e_coef, e_loss)
    volts = volts_init.reshape(1, NODE_DEV)
    up = slab_of(True, grids, volts)
    lower = shifted(up, "gz", 1)
    down = slab_of(False, grids, up)
    upper = shifted(down, "gz", -1)
    front = strip_of(True, grids, down)
    before = shifted(front, "gy", 1)
    back = strip_of(False, grids, front)
    after = shifted(back, "gy", -1)
    out = begin(n_gy, port_cell, port_node, port_gain, e_field, volts, back)
    arrived = exchange(out)
    front_ends, back_ends = corners(lower, upper, out)
    before_ends = shifted(front_ends, "gy", 1)
    after_ends = shifted(back_ends, "gy", -1)
    arrived, front_ends, back_ends = lax.optimization_barrier((arrived, front_ends, back_ends))
    sides = (before, after, before_ends, after_ends)
    mats = matrices(diag_blocks, inv_blocks, off_blocks)

    found, columns = plan(n_gz, n_gy, arrived, port_node, port_gain)
    table = jnp.concatenate([found[0], found[1], found[7, 0:1]])

    e_xy, e_z, h, media, sample, coef = halo(table, columns, lower, upper, sides, *grids)
    for step in range(1, STEPS + 1):
        if step > 1:
            arrived = exchange(out)
            arrived, e_z = lax.optimization_barrier((arrived, e_z))
        e_xy, e_z, h = field(step, media, e_xy, e_z, h)
        shared = (table, off_cols, arrived, columns, sample, coef, volts, mats)
        if step < STEPS:
            e_z, out, volts, sample = circuit(*shared, e_z)
        else:
            e_end, h_end, volts = finish(*shared, e_xy, e_z, h)
    return e_end, h_end, volts.reshape(-1)


def solution(mesh):
    placed = (
        P(None, "gz", "gy", None),
        P(None, "gz", "gy", None),
        P("gz", "gy", None),
        P("gz", "gy", None),
        P(("gz", "gy")),
        P(),
        P(),
        P(("gz", "gy"), None, None),
        P(("gz", "gy"), None, None),
        P(("gz", "gy"), None, None, None),
        P(("gz", "gy"), None),
        P(("gz", "gy")),
    )
    return jax.shard_map(
        body,
        mesh=mesh,
        in_specs=placed,
        out_specs=(P(None, "gz", "gy", None), P(None, "gz", "gy", None), P(("gz", "gy"))),
        check_vma=False,
    )
```

```python
import functools

import jax
import jax.numpy as jnp
from jax import lax
from jax.experimental import pallas as pl
from jax.experimental.pallas import tpu as pltpu
from jax.sharding import PartitionSpec as P

STEPS = 5
NEWTON = 2
BS = 64
NB_DEV = 2
OFF = 4
PORT_DEV = 32
GROUP = 16
ND = 128
NODE_DEV = NB_DEV * BS
DEPTH = 5
CZ, CY, NX = 32, 16, 256
LAYERS = CZ + 2 * DEPTH
PAD = 8
TALL = CY + 2 * PAD
PARTS = 8
STRIP = PARTS * DEPTH
SIDES = ((0, 0), (-1, 0), (1, 0), (0, -1), (-1, -1), (1, -1), (0, 1), (-1, 1), (1, 1))
REACH = len(SIDES) * PORT_DEV
NODES, COUNT = REACH, 2 * REACH

time_step = 0.55
charge_scale = 4.0
diode_weight = 0.5

f32 = jnp.float32
VM = pl.BlockSpec(memory_space=pltpu.VMEM)
SM = pl.BlockSpec(memory_space=pltpu.SMEM)
HBM = pl.BlockSpec(memory_space=pltpu.HBM)
ANY = pl.BlockSpec(memory_space=pl.ANY)
DMA = pltpu.SemaphoreType.DMA
CUBE = (LAYERS, TALL, NX)


def onchip(shape):
    return pltpu.VMEM(shape, f32)


def keep(value):
    return pltpu.with_memory_space_constraint(value, pltpu.VMEM)


def away(value):
    return pltpu.with_memory_space_constraint(value, pltpu.HBM)


def params():
    return pltpu.CompilerParams(vmem_limit_bytes=12 << 20)


def lanes_of(count, width):
    return lax.broadcasted_iota(jnp.int32, (count, width), 1)


def pick(rows, lane):
    hit = lanes_of(rows.shape[0], rows.shape[1]) == lane
    return jnp.sum(jnp.where(hit, rows, 0.0), axis=1, keepdims=True)


def spread(column, lane, width):
    hit = lanes_of(column.shape[0], width) == lane
    return jnp.where(hit, column, 0.0)


def columns_at(columns, part):
    block = columns[part, :]
    return block[:, 2:3], block[:, 3:4].astype(jnp.int32), block[:, 4:5].astype(jnp.int32)


def row_kind(shape, stride):
    return lax.broadcasted_iota(jnp.int32, shape, 0) % stride


def add_rows(out, stride, devices, rows_ref):
    for port, device in enumerate(devices):
        spot = pl.ds(device * stride + 1, 1)
        out[spot, :] = out[spot, :] + rows_ref[port : port + 1, :]


def copier(sems):
    copies = []

    def copy(source, target):
        job = pltpu.make_async_copy(source, target, sems.at[len(copies)])
        job.start()
        copies.append(job)

    return copies, copy


def sources_of(e_in, h_in, coef_in, loss_in):
    return [e_in.at[k] for k in range(3)] + [h_in.at[k] for k in range(3)] + [coef_in, loss_in]


def strip_kernel(top, e_in, h_in, coef_in, loss_in, lower, upper, after, strip, fields, sems):
    copies, copy = copier(sems)
    rows = pl.ds(CY - 8 if top else 0, 8)
    for part, source in enumerate(sources_of(e_in, h_in, coef_in, loss_in)):
        slab = pl.ds(part * DEPTH, DEPTH)
        copy(source.at[:, rows], fields.at[part, pl.ds(DEPTH, CZ)])
        copy(lower.at[slab, rows], fields.at[part, pl.ds(0, DEPTH)])
        copy(upper.at[slab, rows], fields.at[part, pl.ds(DEPTH + CZ, DEPTH)])
    for job in copies:
        job.wait()
    given = slice(8 - DEPTH, 8) if top else slice(0, DEPTH)

    @pl.loop(0, LAYERS)
    def _(layer):
        for part in range(PARTS):
            strip[layer, part * DEPTH : (part + 1) * DEPTH, :] = fields[part, layer, given, :]


def strip_of(top, grids, lower, upper, after):
    return pl.pallas_call(
        functools.partial(strip_kernel, top),
        name="strip",
        out_shape=jax.ShapeDtypeStruct((LAYERS, STRIP, NX), f32),
        in_specs=[HBM] * 6 + [ANY],
        out_specs=VM,
        scratch_shapes=[pltpu.VMEM((PARTS, LAYERS, 8, NX), f32), DMA((3 * PARTS,))],
        compiler_params=params(),
    )(*map(away, (*grids, lower, upper)), after)


def slab_kernel(top, e_in, h_in, coef_in, loss_in, after, slab, sems):
    copies, copy = copier(sems)
    layers = pl.ds(CZ - DEPTH if top else 0, DEPTH)
    for part, source in enumerate(sources_of(e_in, h_in, coef_in, loss_in)):
        copy(source.at[layers], slab.at[pl.ds(part * DEPTH, DEPTH)])
    for job in copies:
        job.wait()


def slab_of(top, grids, after):
    return pl.pallas_call(
        functools.partial(slab_kernel, top),
        name="slab",
        out_shape=jax.ShapeDtypeStruct((PARTS * DEPTH, CY, NX), f32),
        in_specs=[HBM] * 4 + [ANY],
        out_specs=VM,
        scratch_shapes=[DMA((PARTS,))],
        compiler_params=params(),
    )(*map(away, grids), after)


def begin_kernel(
    n_gy, cells, nodes, gains, e_in, cell_row, volts, after, out, e_z, picked, hits, rows_ref, sem,
):
    load = pltpu.make_async_copy(e_in.at[2], e_z, sem)
    load.start()
    first = (lax.axis_index("gz") * n_gy + lax.axis_index("gy")) * PORT_DEV
    wide, narrow = lanes_of(1, NX), lanes_of(1, NODE_DEV)
    own_nodes = [nodes[first + port] for port in range(PORT_DEV)]
    for port, node in enumerate(own_nodes):
        hits[port : port + 1, :] = jnp.where(narrow == node % NODE_DEV, 1.0, 0.0)
    kind = row_kind(out.shape, 4)
    rows_ref[0:1, :] = jnp.zeros((1, NODE_DEV), f32)
    rows_ref[0:1, 0:PORT_DEV] = cell_row[...].astype(f32)
    out[...] = jnp.where(kind == 0, volts[...], jnp.where(kind == 2, rows_ref[0:1, :], 0.0))

    load.wait()
    for port in range(PORT_DEV):
        cell = cells[port]
        line = cell // NX
        value = e_z[line // CY, pl.ds(line % CY, 1), :] * gains[first + port]
        picked[port : port + 1, :] = jnp.where(wide == cell % NX, value, 0.0)
    rows_ref[...] = hits[...] * jnp.sum(picked[...], axis=1, keepdims=True)
    add_rows(out, 4, [node // NODE_DEV for node in own_nodes], rows_ref)


def begin(n_gy, cells, nodes, gains, e_in, volts, after):
    return pl.pallas_call(
        functools.partial(begin_kernel, n_gy),
        name="begin",
        out_shape=jax.ShapeDtypeStruct((4 * ND, NODE_DEV), f32),
        in_specs=[SM, SM, SM, HBM, VM, VM, ANY],
        out_specs=VM,
        scratch_shapes=[
            pltpu.VMEM((CZ, CY, NX), f32),
            pltpu.VMEM((PORT_DEV, NX), f32),
            pltpu.VMEM((PORT_DEV, NODE_DEV), f32),
            pltpu.VMEM((PORT_DEV, NODE_DEV), f32),
            DMA,
        ],
        compiler_params=params(),
    )(cells, nodes, gains, away(e_in), cells.reshape(1, -1), volts, after)


def matrices_kernel(diag, inv, off, m_off, m_diag, m_inv):
    m_diag[...] = jnp.zeros_like(m_diag)
    m_inv[...] = jnp.zeros_like(m_inv)
    for j in range(NB_DEV):
        part = slice(j * BS, (j + 1) * BS)
        m_diag[part, part] = diag[j]
        m_inv[part, part] = inv[j].T
        for k in range(OFF):
            m_off[part, k * BS : (k + 1) * BS] = off[j, k]


def matrices(diag, inv, off):
    square = onchip((NODE_DEV, NODE_DEV))
    return pl.pallas_call(
        matrices_kernel,
        name="matrices",
        out_shape=(onchip((NODE_DEV, OFF * BS)), square, square),
        in_specs=[VM, VM, VM],
        out_specs=(VM, VM, VM),
        compiler_params=params(),
    )(diag, inv, off)


def plan_kernel(n_gz, n_gy, arrived, nodes, gains, found, columns, facts):
    gz, gy = lax.axis_index("gz"), lax.axis_index("gy")
    lane = lanes_of(1, NODE_DEV)
    width = NODE_DEV // PORT_DEV
    facts[...] = jnp.zeros_like(facts)
    for group, (side_z, side_y) in enumerate(SIDES):
        at_z, at_y = gz + side_z, gy + side_y
        exists = (at_z >= 0) & (at_z < n_gz) & (at_y >= 0) & (at_y < n_gy)
        device = jnp.where(exists, at_z * n_gy + at_y, 0)
        slot = group % width
        turn = (slot - device % width + width) % width * PORT_DEV
        row = pl.ds(device // width, 1)
        node, gain = pltpu.roll(nodes[row, :], turn, 1), pltpu.roll(gains[row, :], turn, 1)
        cell = pltpu.roll(arrived[pl.ds(4 * device + 2, 1), :], slot * PORT_DEV, 1).astype(jnp.int32)
        layer = cell // (CY * NX) + (side_z * CZ + DEPTH)
        line = (cell // NX) % CY + (side_y * CY + PAD)
        valid = (layer >= 1) & (layer < LAYERS - 1)
        valid &= (line > PAD - DEPTH) & (line < PAD + CY + DEPTH - 1)
        valid &= (lane // PORT_DEV == slot) & (jnp.where(exists, 1, 0) > 0)
        values = (layer * TALL + line, node // NODE_DEV, gain, cell % NX, node % NODE_DEV, 1)
        part = slice(group // width * NODE_DEV, (group // width + 1) * NODE_DEV)
        for kind, value in enumerate(values):
            fact = jnp.where(valid, jnp.asarray(value).astype(f32), 0.0)
            facts[kind : kind + 1, part] = facts[kind : kind + 1, part] + fact

    used = facts[5:6, :]
    total = used.shape[1]
    upper = lax.broadcasted_iota(jnp.int32, (total, total), 0) <= lanes_of(total, total)
    ones = jnp.broadcast_to(used, (8, total))
    order = jnp.dot(ones, upper.astype(f32), preferred_element_type=f32)[0:1, :] - 1.0
    spot = lax.broadcasted_iota(jnp.int32, (REACH, total), 0)
    chosen = jnp.where((spot == order.astype(jnp.int32)) & (used > 0.0), 1.0, 0.0)
    across = (((1,), (1,)), ((), ()))
    columns[...] = lax.dot_general(
        chosen, facts[...], across, precision=lax.Precision.HIGHEST, preferred_element_type=f32
    )
    rows = lax.dot_general(
        facts[...], chosen, across, precision=lax.Precision.HIGHEST, preferred_element_type=f32
    )
    count = jnp.sum(used, axis=1, keepdims=True)
    groups = ((count + (GROUP - 1)) * (1.0 / GROUP)).astype(jnp.int32)
    kind = lax.broadcasted_iota(jnp.int32, rows.shape, 0)
    unused = (kind == 0) & (lanes_of(8, REACH) >= count.astype(jnp.int32))
    whole = jnp.where(unused, PAD, (rows + 0.5).astype(jnp.int32))
    found[...] = jnp.where(kind == 7, groups, whole)


def plan(n_gz, n_gy, arrived, nodes, gains):
    lanes = -(-REACH // NODE_DEV) * NODE_DEV
    return pl.pallas_call(
        functools.partial(plan_kernel, n_gz, n_gy),
        name="plan",
        out_shape=(
            jax.ShapeDtypeStruct((8, REACH), jnp.int32),
            jax.ShapeDtypeStruct((REACH, 8), f32),
        ),
        in_specs=[VM, VM, VM],
        out_specs=(VM, VM),
        scratch_shapes=[pltpu.VMEM((8, lanes), f32)],
        compiler_params=params(),
    )(arrived, nodes.reshape(-1, NODE_DEV), gains.reshape(-1, NODE_DEV))


def halo_kernel(
    found, columns, lower, upper, before, after,
    e_in, h_in, coef_in, loss_in, e_xy, e_z, h, media, sample, coef, picked, sems,
):
    copies, copy = copier(sems)
    targets = [
        e_xy.at[0], e_xy.at[1], e_z, h.at[0], h.at[1], h.at[2], media.at[0], media.at[1],
    ]
    sources = [e_in.at[k] for k in range(3)] + [h_in.at[k] for k in range(3)] + [coef_in, loss_in]
    middle = pl.ds(PAD, CY)
    for part, (source, target) in enumerate(zip(sources, targets)):
        given = pl.ds(part * DEPTH, DEPTH)
        copy(source, target.at[pl.ds(DEPTH, CZ), middle])
        copy(lower.at[given], target.at[pl.ds(0, DEPTH), middle])
        copy(upper.at[given], target.at[pl.ds(DEPTH + CZ, DEPTH), middle])

    @pl.loop(0, LAYERS)
    def _(layer):
        for part, target in enumerate(targets):
            rows = slice(part * DEPTH, (part + 1) * DEPTH)
            target[layer, PAD - DEPTH : PAD, :] = before[layer, rows, :]
            target[layer, PAD + CY : PAD + CY + DEPTH, :] = after[layer, rows, :]

    for job in copies:
        job.wait()

    @pl.loop(0, LAYERS)
    def _(layer):
        media[1, layer] = 1.0 - media[1, layer]

    @pl.loop(0, found[COUNT])
    def _(group):
        part = pl.ds(pl.multiple_of(group * GROUP, GROUP), GROUP)
        _, place, _ = columns_at(columns, part)
        sample[part, :] = gather_cells(e_z, found, group, place, picked)
        coef[part, :] = gather_cells(media.at[0], found, group, place, picked)


def gather_cells(source, found, group, place, picked):
    for port in range(GROUP):
        spot = found[group * GROUP + port]
        picked[port : port + 1, :] = source[spot // TALL, pl.ds(spot % TALL, 1), :]
    return pick(picked[...], place)


def halo(found, columns, lower, upper, before, after, e_in, h_in, coef, loss):
    return pl.pallas_call(
        halo_kernel,
        name="halo",
        out_shape=(
            onchip((2,) + CUBE),
            onchip(CUBE),
            onchip((3,) + CUBE),
            onchip((2,) + CUBE),
            onchip((REACH, 1)),
            onchip((REACH, 1)),
        ),
        in_specs=[SM, VM, HBM, HBM, VM, VM] + [HBM] * 4,
        out_specs=(VM,) * 6,
        scratch_shapes=[pltpu.VMEM((GROUP, NX), f32), DMA((24,))],
        compiler_params=params(),
    )(found, columns, away(lower), away(upper), before, after, *map(away, (e_in, h_in, coef, loss)))


def field_kernel(step, media, e_xy, e_z, h, to_xy, to_z, to_h):
    low_z = jnp.where(lax.axis_index("gz") > 0, 1.0, 0.0)
    low_y = jnp.where(lax.axis_index("gy") > 0, time_step, 0.0)
    lane = lanes_of(TALL, NX)
    last_lane, first_lane = lane == NX - 1, lane == 0
    row = lax.broadcasted_iota(jnp.int32, (TALL, NX), 0)
    rate_rows = jnp.where(row < PAD, low_y, time_step)

    def next_x(value):
        return jnp.where(last_lane, 0.0, pltpu.roll(value, NX - 1, 1))

    def prior_x(value):
        return jnp.where(first_lane, 0.0, pltpu.roll(value, 1, 1))

    def next_y(value):
        return pltpu.roll(value, TALL - 1, 0)

    def prior_y(value):
        return pltpu.roll(value, 1, 0)

    def magnetic(layer):
        e_x, e_y, e_zz = e_xy[0, layer], e_xy[1, layer], e_z[layer]
        rate = rate_rows * jnp.where(layer < DEPTH, low_z, 1.0)
        curl_x = (next_y(e_zz) - e_zz) - (e_xy[1, layer + 1] - e_y)
        curl_y = (e_xy[0, layer + 1] - e_x) - (next_x(e_zz) - e_zz)
        curl_z = (next_x(e_y) - e_y) - (next_y(e_x) - e_x)
        return (h[0, layer] - rate * curl_x, h[1, layer] - rate * curl_y, h[2, layer] - rate * curl_z)

    def electric(layer):
        h_x, h_y, h_z = to_h[0, layer], to_h[1, layer], to_h[2, layer]
        coef, kept = media[0, layer], media[1, layer]
        back_x = (h_z - prior_y(h_z)) - (h_y - to_h[1, layer - 1])
        back_y = (h_x - to_h[0, layer - 1]) - (h_z - prior_x(h_z))
        back_z = (h_y - prior_x(h_y)) - (h_x - prior_y(h_x))
        return (
            kept * e_xy[0, layer] + coef * back_x,
            kept * e_xy[1, layer] + coef * back_y,
            kept * e_z[layer] + coef * back_z,
        )

    def put_h(layer, values):
        to_h[0, layer], to_h[1, layer], to_h[2, layer] = values

    def put_e(layer, values):
        to_xy[0, layer], to_xy[1, layer], to_z[layer] = values

    put_h(step - 1, magnetic(step - 1))
    put_h(step, magnetic(step))
    last = LAYERS - step - 1

    @pl.loop(step, last)
    def _(layer):
        electric_values = electric(layer)
        magnetic_values = magnetic(layer + 1)
        put_e(layer, electric_values)
        put_h(layer + 1, magnetic_values)

    put_e(last, electric(last))


def field(step, media, e_xy, e_z, h):
    return pl.pallas_call(
        functools.partial(field_kernel, step),
        name="field",
        out_shape=(onchip((2,) + CUBE), onchip(CUBE), onchip((3,) + CUBE)),
        in_specs=[VM] * 4,
        out_specs=(VM,) * 3,
        compiler_params=params(),
    )(keep(media), keep(e_xy), keep(e_z), keep(h))


def solve(stride, arrived, off_cols, volts, m_off, m_diag, m_inv):
    lane = lanes_of(1, NODE_DEV)
    halves = []
    for j in range(NB_DEV):
        pieces = []
        for half in range(OFF // 2):
            total = None
            for side in range(2):
                column = off_cols[j, half * 2 + side]
                row = arrived[pl.ds(column // NB_DEV * stride, 1), :]
                row = jnp.where(column % NB_DEV == side, row, pltpu.roll(row, BS, 1))
                row = jnp.where((lane < BS) == (side == 0), row, 0.0)
                total = row if total is None else total + row
            pieces.append(jnp.broadcast_to(total, (BS, NODE_DEV)))
        halves.append(pieces)
    first = jnp.concatenate([halves[0][0], halves[1][0]], axis=0)
    second = jnp.concatenate([halves[0][1], halves[1][1]], axis=0)
    product = m_off[:, 0:NODE_DEV] * first + m_off[:, NODE_DEV : 2 * NODE_DEV] * second
    offsum = jnp.sum(product, axis=1, keepdims=True)
    kind = row_kind(arrived.shape, stride)
    inject = jnp.sum(jnp.where(kind == 1, arrived[...], 0.0), axis=0, keepdims=True)
    start = volts[...]
    target = charge_scale * start + inject
    diagonal = lax.broadcasted_iota(jnp.int32, (NODE_DEV, NODE_DEV), 0) == lanes_of(NODE_DEV, NODE_DEV)
    iterate = start
    for newton_round in range(NEWTON):
        local = diode_weight * jnp.tanh(iterate) - target
        terms = m_diag[...] * iterate + jnp.where(diagonal, local, 0.0)
        resid = jnp.sum(terms, axis=1, keepdims=True) + offsum
        iterate = iterate - jnp.sum(m_inv[...] * resid, axis=0, keepdims=True)
    return iterate


def apply_ports(stride, table, arrived, columns, sample, coef, e_z, near_rows, deltas):
    @pl.loop(0, table[COUNT])
    def _(group):
        first = group * GROUP
        part = pl.ds(pl.multiple_of(first, GROUP), GROUP)
        for port in range(GROUP):
            near_at = table[NODES + first + port] * stride
            near_rows[port : port + 1, :] = arrived[pl.ds(near_at, 1), :]
        gain, place, lane = columns_at(columns, part)
        current = gain * (sample[part, :] - pick(near_rows[...], lane))
        deltas[...] = spread(-coef[part, :] * current, place, NX)
        for port in range(GROUP):
            spot = table[first + port]
            layer, row = spot // TALL, pl.ds(spot % TALL, 1)
            e_z[layer, row, :] = e_z[layer, row, :] + deltas[port : port + 1, :]


def circuit_kernel(
    stride, table, off_cols, arrived, columns, sample, coef, volts, m_off, m_diag, m_inv, e_in,
    e_z, out, volts_out, sample_out, near_rows, deltas, picked, spread_rows,
):
    e_z[...] = e_in[...]
    apply_ports(stride, table, arrived, columns, sample, coef, e_z, near_rows, deltas)

    @pl.loop(0, table[COUNT])
    def _(group):
        part = pl.ds(pl.multiple_of(group * GROUP, GROUP), GROUP)
        _, place, _ = columns_at(columns, part)
        sample_out[part, :] = gather_cells(e_z, table, group, place, picked)

    solved = solve(stride, arrived, off_cols, volts, m_off, m_diag, m_inv)
    volts_out[...] = solved
    own = slice(0, PORT_DEV)
    gain, _, lane = columns_at(columns, own)
    spread_rows[...] = spread(gain * sample_out[own, :], lane, NODE_DEV)
    out[...] = jnp.where(row_kind(out.shape, 2) == 0, solved, 0.0)
    add_rows(out, 2, [table[NODES + port] for port in range(PORT_DEV)], spread_rows)


def circuit(table, off_cols, arrived, columns, sample, coef, volts, mats, e_z):
    return pl.pallas_call(
        functools.partial(circuit_kernel, arrived.shape[0] // ND),
        name="circuit",
        out_shape=(
            onchip(CUBE),
            onchip((2 * ND, NODE_DEV)),
            onchip((1, NODE_DEV)),
            onchip((REACH, 1)),
        ),
        in_specs=[SM, SM] + [VM] * 9,
        out_specs=(VM,) * 4,
        scratch_shapes=[
            pltpu.VMEM((GROUP, NODE_DEV), f32),
            pltpu.VMEM((GROUP, NX), f32),
            pltpu.VMEM((GROUP, NX), f32),
            pltpu.VMEM((PORT_DEV, NODE_DEV), f32),
        ],
        compiler_params=params(),
    )(
        table, off_cols, arrived, columns, keep(sample), keep(coef), volts,
        *[keep(mat) for mat in mats], keep(e_z),
    )


def finish_kernel(
    stride, table, off_cols, arrived, columns, sample, coef, volts, m_off, m_diag, m_inv, e_xy, e_in, h,
    e_out, h_out, volts_out, e_z, near_rows, deltas, sems,
):
    copies, copy = copier(sems)
    layers, rows = pl.ds(DEPTH, CZ), pl.ds(PAD, CY)
    for k in range(3):
        copy(h.at[k, layers, rows], h_out.at[k])
    for k in range(2):
        copy(e_xy.at[k, layers, rows], e_out.at[k])
    e_z[...] = e_in[...]
    apply_ports(stride, table, arrived, columns, sample, coef, e_z, near_rows, deltas)
    copy(e_z.at[layers, rows], e_out.at[2])
    volts_out[...] = solve(stride, arrived, off_cols, volts, m_off, m_diag, m_inv)
    for job in copies:
        job.wait()


def finish(table, off_cols, arrived, columns, sample, coef, volts, mats, e_xy, e_z, h):
    return pl.pallas_call(
        functools.partial(finish_kernel, arrived.shape[0] // ND),
        name="finish",
        out_shape=(
            jax.ShapeDtypeStruct((3, CZ, CY, NX), f32),
            jax.ShapeDtypeStruct((3, CZ, CY, NX), f32),
            jax.ShapeDtypeStruct((1, NODE_DEV), f32),
        ),
        in_specs=[SM, SM] + [VM] * 11,
        out_specs=(HBM, HBM, VM),
        scratch_shapes=[
            pltpu.VMEM(CUBE, f32),
            pltpu.VMEM((GROUP, NODE_DEV), f32),
            pltpu.VMEM((GROUP, NX), f32),
            DMA((6,)),
        ],
        compiler_params=params(),
    )(
        table, off_cols, arrived, columns, keep(sample), keep(coef), volts,
        *[keep(mat) for mat in mats], keep(e_xy), keep(e_z), keep(h),
    )


def shifted(value, axis, steps):
    count = lax.axis_size(axis)
    first, last = (max(0, -steps), min(count, count - steps))
    return lax.ppermute(value, axis, [(source, source + steps) for source in range(first, last)])


def exchange(value):
    return lax.all_to_all(value, ("gz", "gy"), 0, 0, tiled=True)


def body(
    e_field,
    h_field,
    e_coef,
    e_loss,
    port_cell,
    port_node,
    port_gain,
    diag_blocks,
    inv_blocks,
    off_blocks,
    off_cols,
    volts_init,
):
    n_gz, n_gy = lax.axis_size("gz"), lax.axis_size("gy")
    grids = (e_field, h_field, e_coef, e_loss)
    volts = volts_init.reshape(1, NODE_DEV)
    up = slab_of(True, grids, volts)
    lower = shifted(up, "gz", 1)
    down = slab_of(False, grids, up)
    upper = shifted(down, "gz", -1)
    out = begin(n_gy, port_cell, port_node, port_gain, e_field, volts, down)
    arrived = exchange(out)
    front = strip_of(True, grids, lower, upper, out)
    before = shifted(front, "gy", 1)
    back = strip_of(False, grids, lower, upper, front)
    after = shifted(back, "gy", -1)
    arrived, front, back = lax.optimization_barrier((arrived, front, back))
    mats = matrices(diag_blocks, inv_blocks, off_blocks)

    found, columns = plan(n_gz, n_gy, arrived, port_node, port_gain)
    table = jnp.concatenate([found[0], found[1], found[7, 0:1]])

    e_xy, e_z, h, media, sample, coef = halo(table, columns, lower, upper, before, after, *grids)
    for step in range(1, STEPS + 1):
        if step > 1:
            arrived = exchange(out)
            arrived, e_z = lax.optimization_barrier((arrived, e_z))
        e_xy, e_z, h = field(step, media, e_xy, e_z, h)
        shared = (table, off_cols, arrived, columns, sample, coef, volts, mats)
        if step < STEPS:
            e_z, out, volts, sample = circuit(*shared, e_z)
        else:
            e_end, h_end, volts = finish(*shared, e_xy, e_z, h)
    return e_end, h_end, volts.reshape(-1)


def solution(mesh):
    placed = (
        P(None, "gz", "gy", None),
        P(None, "gz", "gy", None),
        P("gz", "gy", None),
        P("gz", "gy", None),
        P(("gz", "gy")),
        P(),
        P(),
        P(("gz", "gy"), None, None),
        P(("gz", "gy"), None, None),
        P(("gz", "gy"), None, None, None),
        P(("gz", "gy"), None),
        P(("gz", "gy")),
    )
    return jax.shard_map(
        body,
        mesh=mesh,
        in_specs=placed,
        out_specs=(P(None, "gz", "gy", None), P(None, "gz", "gy", None), P(("gz", "gy"))),
        check_vma=False,
    )
```

```python
import functools

import jax
import jax.numpy as jnp
from jax import lax
from jax.experimental import pallas as pl
from jax.experimental.pallas import tpu as pltpu
from jax.sharding import PartitionSpec as P

STEPS = 5
NEWTON = 2
BS = 64
NB_DEV = 2
OFF = 4
PORT_DEV = 32
GROUP = 16
ND = 128
NODE_DEV = NB_DEV * BS
DEPTH = 5
CZ, CY, NX = 32, 16, 256
LAYERS = CZ + 2 * DEPTH
PAD = 0
TALL = CY
STACK = 48
PARTS = 8
SIDES = ((0, 0), (-1, 0), (1, 0))
REACH = len(SIDES) * PORT_DEV
NODES, COUNT = REACH, 2 * REACH

time_step = 0.55
charge_scale = 4.0
diode_weight = 0.5

f32 = jnp.float32
VM = pl.BlockSpec(memory_space=pltpu.VMEM)
SM = pl.BlockSpec(memory_space=pltpu.SMEM)
HBM = pl.BlockSpec(memory_space=pltpu.HBM)
ANY = pl.BlockSpec(memory_space=pl.ANY)
DMA = pltpu.SemaphoreType.DMA
CUBE = (LAYERS, TALL, NX)


def onchip(shape):
    return pltpu.VMEM(shape, f32)


def keep(value):
    return pltpu.with_memory_space_constraint(value, pltpu.VMEM)


def away(value):
    return pltpu.with_memory_space_constraint(value, pltpu.HBM)


def params():
    return pltpu.CompilerParams(vmem_limit_bytes=12 << 20)


def lanes_of(count, width):
    return lax.broadcasted_iota(jnp.int32, (count, width), 1)


def pick(rows, lane):
    hit = lanes_of(rows.shape[0], rows.shape[1]) == lane
    return jnp.sum(jnp.where(hit, rows, 0.0), axis=1, keepdims=True)


def spread(column, lane, width):
    hit = lanes_of(column.shape[0], width) == lane
    return jnp.where(hit, column, 0.0)


def columns_at(columns, part):
    block = columns[part, :]
    return block[:, 2:3], block[:, 3:4].astype(jnp.int32), block[:, 4:5].astype(jnp.int32)


def row_kind(shape, stride):
    return lax.broadcasted_iota(jnp.int32, shape, 0) % stride


def add_rows(out, stride, devices, rows_ref):
    for port, device in enumerate(devices):
        spot = pl.ds(device * stride + 1, 1)
        out[spot, :] = out[spot, :] + rows_ref[port : port + 1, :]


def copier(sems):
    copies = []

    def copy(source, target):
        job = pltpu.make_async_copy(source, target, sems.at[len(copies)])
        job.start()
        copies.append(job)

    return copies, copy


def sources_of(e_in, h_in, coef_in, loss_in):
    return [e_in.at[k] for k in range(3)] + [h_in.at[k] for k in range(3)] + [coef_in, loss_in]


def write_rows(stack, sources, row):
    for slot, source in enumerate(sources):
        for layer in range(LAYERS):
            stack[slot, layer : layer + 1, :] = source[layer, row : row + 1, :]
        stack[slot, LAYERS:STACK, :] = jnp.zeros((STACK - LAYERS, NX), f32)


def stack_of(count):
    return jax.ShapeDtypeStruct((count, STACK, NX), f32)


def slab_kernel(top, e_in, h_in, coef_in, loss_in, after, slab, sems):
    copies, copy = copier(sems)
    layers = pl.ds(CZ - DEPTH if top else 0, DEPTH)
    for part, source in enumerate(sources_of(e_in, h_in, coef_in, loss_in)):
        copy(source.at[layers], slab.at[pl.ds(part * DEPTH, DEPTH)])
    for job in copies:
        job.wait()


def slab_of(top, grids, after):
    return pl.pallas_call(
        functools.partial(slab_kernel, top),
        name="slab",
        out_shape=jax.ShapeDtypeStruct((PARTS * DEPTH, CY, NX), f32),
        in_specs=[HBM] * 4 + [ANY],
        out_specs=VM,
        scratch_shapes=[DMA((PARTS,))],
        compiler_params=params(),
    )(*map(away, grids), after)


def begin_kernel(
    n_gy, cells, nodes, gains, e_in, cell_row, volts, after, out, e_z, picked, hits, rows_ref, sem,
):
    load = pltpu.make_async_copy(e_in.at[2], e_z, sem)
    load.start()
    first = (lax.axis_index("gz") * n_gy + lax.axis_index("gy")) * PORT_DEV
    wide, narrow = lanes_of(1, NX), lanes_of(1, NODE_DEV)
    own_nodes = [nodes[first + port] for port in range(PORT_DEV)]
    for port, node in enumerate(own_nodes):
        hits[port : port + 1, :] = jnp.where(narrow == node % NODE_DEV, 1.0, 0.0)
    kind = row_kind(out.shape, 4)
    rows_ref[0:1, :] = jnp.zeros((1, NODE_DEV), f32)
    rows_ref[0:1, 0:PORT_DEV] = cell_row[...].astype(f32)
    out[...] = jnp.where(kind == 0, volts[...], jnp.where(kind == 2, rows_ref[0:1, :], 0.0))

    load.wait()
    for port in range(PORT_DEV):
        cell = cells[port]
        line = cell // NX
        value = e_z[line // CY, pl.ds(line % CY, 1), :] * gains[first + port]
        picked[port : port + 1, :] = jnp.where(wide == cell % NX, value, 0.0)
    rows_ref[...] = hits[...] * jnp.sum(picked[...], axis=1, keepdims=True)
    add_rows(out, 4, [node // NODE_DEV for node in own_nodes], rows_ref)


def begin(n_gy, cells, nodes, gains, e_in, volts, after):
    return pl.pallas_call(
        functools.partial(begin_kernel, n_gy),
        name="begin",
        out_shape=jax.ShapeDtypeStruct((4 * ND, NODE_DEV), f32),
        in_specs=[SM, SM, SM, HBM, VM, VM, ANY],
        out_specs=VM,
        scratch_shapes=[
            pltpu.VMEM((CZ, CY, NX), f32),
            pltpu.VMEM((PORT_DEV, NX), f32),
            pltpu.VMEM((PORT_DEV, NODE_DEV), f32),
            pltpu.VMEM((PORT_DEV, NODE_DEV), f32),
            DMA,
        ],
        compiler_params=params(),
    )(cells, nodes, gains, away(e_in), cells.reshape(1, -1), volts, after)


def matrices_kernel(diag, inv, off, m_off, m_diag, m_inv):
    m_diag[...] = jnp.zeros_like(m_diag)
    m_inv[...] = jnp.zeros_like(m_inv)
    for j in range(NB_DEV):
        part = slice(j * BS, (j + 1) * BS)
        m_diag[part, part] = diag[j]
        m_inv[part, part] = inv[j].T
        for k in range(OFF):
            m_off[part, k * BS : (k + 1) * BS] = off[j, k]


def matrices(diag, inv, off):
    square = onchip((NODE_DEV, NODE_DEV))
    return pl.pallas_call(
        matrices_kernel,
        name="matrices",
        out_shape=(onchip((NODE_DEV, OFF * BS)), square, square),
        in_specs=[VM, VM, VM],
        out_specs=(VM, VM, VM),
        compiler_params=params(),
    )(diag, inv, off)


def plan_kernel(n_gz, n_gy, arrived, nodes, gains, found, columns, facts):
    gz, gy = lax.axis_index("gz"), lax.axis_index("gy")
    lane = lanes_of(1, NODE_DEV)
    width = NODE_DEV // PORT_DEV
    facts[...] = jnp.zeros_like(facts)
    for group, (side_z, side_y) in enumerate(SIDES):
        at_z, at_y = gz + side_z, gy + side_y
        exists = (at_z >= 0) & (at_z < n_gz) & (at_y >= 0) & (at_y < n_gy)
        device = jnp.where(exists, at_z * n_gy + at_y, 0)
        slot = group % width
        turn = (slot - device % width + width) % width * PORT_DEV
        row = pl.ds(device // width, 1)
        node, gain = pltpu.roll(nodes[row, :], turn, 1), pltpu.roll(gains[row, :], turn, 1)
        cell = pltpu.roll(arrived[pl.ds(4 * device + 2, 1), :], slot * PORT_DEV, 1).astype(jnp.int32)
        layer = cell // (CY * NX) + (side_z * CZ + DEPTH)
        line = (cell // NX) % CY + (side_y * CY + PAD)
        valid = (layer >= 1) & (layer < LAYERS - 1)
        valid &= (line > PAD - DEPTH) & (line < PAD + CY + DEPTH - 1)
        valid &= (lane // PORT_DEV == slot) & (jnp.where(exists, 1, 0) > 0)
        values = (layer * TALL + line, node // NODE_DEV, gain, cell % NX, node % NODE_DEV, 1)
        part = slice(group // width * NODE_DEV, (group // width + 1) * NODE_DEV)
        for kind, value in enumerate(values):
            fact = jnp.where(valid, jnp.asarray(value).astype(f32), 0.0)
            facts[kind : kind + 1, part] = facts[kind : kind + 1, part] + fact

    used = facts[5:6, :]
    total = used.shape[1]
    upper = lax.broadcasted_iota(jnp.int32, (total, total), 0) <= lanes_of(total, total)
    ones = jnp.broadcast_to(used, (8, total))
    order = jnp.dot(ones, upper.astype(f32), preferred_element_type=f32)[0:1, :] - 1.0
    spot = lax.broadcasted_iota(jnp.int32, (REACH, total), 0)
    chosen = jnp.where((spot == order.astype(jnp.int32)) & (used > 0.0), 1.0, 0.0)
    across = (((1,), (1,)), ((), ()))
    columns[...] = lax.dot_general(
        chosen, facts[...], across, precision=lax.Precision.HIGHEST, preferred_element_type=f32
    )
    rows = lax.dot_general(
        facts[...], chosen, across, precision=lax.Precision.HIGHEST, preferred_element_type=f32
    )
    count = jnp.sum(used, axis=1, keepdims=True)
    groups = ((count + (GROUP - 1)) * (1.0 / GROUP)).astype(jnp.int32)
    kind = lax.broadcasted_iota(jnp.int32, rows.shape, 0)
    unused = (kind == 0) & (lanes_of(8, REACH) >= count.astype(jnp.int32))
    whole = jnp.where(unused, PAD, (rows + 0.5).astype(jnp.int32))
    found[...] = jnp.where(kind == 7, groups, whole)


def plan(n_gz, n_gy, arrived, nodes, gains):
    lanes = -(-REACH // NODE_DEV) * NODE_DEV
    return pl.pallas_call(
        functools.partial(plan_kernel, n_gz, n_gy),
        name="plan",
        out_shape=(
            jax.ShapeDtypeStruct((8, REACH), jnp.int32),
            jax.ShapeDtypeStruct((REACH, 8), f32),
        ),
        in_specs=[VM, VM, VM],
        out_specs=(VM, VM),
        scratch_shapes=[pltpu.VMEM((8, lanes), f32)],
        compiler_params=params(),
    )(arrived, nodes.reshape(-1, NODE_DEV), gains.reshape(-1, NODE_DEV))


def halo_kernel(
    found, columns, lower, upper, e_in, h_in, coef_in, loss_in,
    e_xy, e_z, h, media, sample, coef, up, down, picked, sems,
):
    copies, copy = copier(sems)
    targets = [
        e_xy.at[0], e_xy.at[1], e_z, h.at[0], h.at[1], h.at[2], media.at[0], media.at[1],
    ]
    for part, source in enumerate(sources_of(e_in, h_in, coef_in, loss_in)):
        given = pl.ds(part * DEPTH, DEPTH)
        copy(source, targets[part].at[pl.ds(DEPTH, CZ)])
        copy(lower.at[given], targets[part].at[pl.ds(0, DEPTH)])
        copy(upper.at[given], targets[part].at[pl.ds(DEPTH + CZ, DEPTH)])
    for job in copies:
        job.wait()
    write_rows(up, targets[:4] + [targets[5]], CY - 1)
    write_rows(down, (targets[0], targets[2]), 0)

    @pl.loop(0, LAYERS)
    def _(layer):
        media[1, layer] = 1.0 - media[1, layer]

    @pl.loop(0, found[COUNT])
    def _(group):
        part = pl.ds(pl.multiple_of(group * GROUP, GROUP), GROUP)
        _, place, _ = columns_at(columns, part)
        sample[part, :] = gather_cells(e_z, found, group, place, picked)
        coef[part, :] = gather_cells(media.at[0], found, group, place, picked)


def gather_cells(source, found, group, place, picked):
    for port in range(GROUP):
        spot = found[group * GROUP + port]
        picked[port : port + 1, :] = source[spot // TALL, pl.ds(spot % TALL, 1), :]
    return pick(picked[...], place)


def halo(found, columns, lower, upper, e_in, h_in, coef, loss):
    return pl.pallas_call(
        halo_kernel,
        name="halo",
        out_shape=(
            onchip((2,) + CUBE),
            onchip(CUBE),
            onchip((3,) + CUBE),
            onchip((2,) + CUBE),
            onchip((REACH, 1)),
            onchip((REACH, 1)),
            stack_of(5),
            stack_of(2),
        ),
        in_specs=[SM, VM, HBM, HBM] + [HBM] * 4,
        out_specs=(VM,) * 8,
        scratch_shapes=[pltpu.VMEM((GROUP, NX), f32), DMA((24,))],
        compiler_params=params(),
    )(found, columns, *map(away, (lower, upper, e_in, h_in, coef, loss)))


def field_kernel(
    step, base, front, back, near, edge_in, media, e_xy, e_z, h, to_xy, to_z, to_h, edge
):
    low_z = jnp.where(lax.axis_index("gz") > 0, time_step, 0.0)
    low_y = jnp.where(lax.axis_index("gy") > 0, time_step, 0.0)
    lane = lanes_of(TALL, NX)
    last_lane, first_lane = lane == NX - 1, lane == 0
    row = lax.broadcasted_iota(jnp.int32, (TALL, NX), 0)
    last_row, first_row = row == TALL - 1, row == 0

    def next_x(value):
        return jnp.where(last_lane, 0.0, pltpu.roll(value, NX - 1, 1))

    def prior_x(value):
        return jnp.where(first_lane, 0.0, pltpu.roll(value, 1, 1))

    def next_y(value, beyond):
        return jnp.where(last_row, beyond, pltpu.roll(value, TALL - 1, 0))

    def prior_y(value, beyond):
        return jnp.where(first_row, beyond, pltpu.roll(value, 1, 0))

    span = pl.ds(0, LAYERS)
    out_x, out_y, out_z = front[0, span, :], front[1, span, :], front[2, span, :]
    out_y_above = front[1, pl.ds(1, LAYERS), :]
    tall_lane = lanes_of(LAYERS, NX)
    out_y_next = jnp.where(tall_lane == NX - 1, 0.0, pltpu.roll(out_y, NX - 1, 1))
    near_x, near_z = near[0, span, :], near[1, span, :]
    edge_x, edge_z = edge_in[base, span, :], edge_in[base + 1, span, :]
    edge[0, span, :] = edge_x - low_y * ((near_z - out_z) - (out_y_above - out_y))
    edge[1, span, :] = edge_z - low_y * ((out_y_next - out_y) - (near_x - out_x))

    def magnetic(layer):
        e_x, e_y, e_zz = e_xy[0, layer], e_xy[1, layer], e_z[layer]
        rate = jnp.where(layer < DEPTH, low_z, time_step)
        beyond = pl.ds(layer, 1)
        curl_x = (next_y(e_zz, back[1, beyond, :]) - e_zz) - (e_xy[1, layer + 1] - e_y)
        curl_y = (e_xy[0, layer + 1] - e_x) - (next_x(e_zz) - e_zz)
        curl_z = (next_x(e_y) - e_y) - (next_y(e_x, back[0, beyond, :]) - e_x)
        return (h[0, layer] - rate * curl_x, h[1, layer] - rate * curl_y, h[2, layer] - rate * curl_z)

    def electric(layer):
        h_x, h_y, h_z = to_h[0, layer], to_h[1, layer], to_h[2, layer]
        coef, kept = media[0, layer], media[1, layer]
        beyond = pl.ds(layer, 1)
        back_x = (h_z - prior_y(h_z, edge[1, beyond, :])) - (h_y - to_h[1, layer - 1])
        back_y = (h_x - to_h[0, layer - 1]) - (h_z - prior_x(h_z))
        back_z = (h_y - prior_x(h_y)) - (h_x - prior_y(h_x, edge[0, beyond, :]))
        return (
            kept * e_xy[0, layer] + coef * back_x,
            kept * e_xy[1, layer] + coef * back_y,
            kept * e_z[layer] + coef * back_z,
        )

    def put_h(layer, values):
        to_h[0, layer], to_h[1, layer], to_h[2, layer] = values

    def put_e(layer, values):
        to_xy[0, layer], to_xy[1, layer], to_z[layer] = values

    put_h(step - 1, magnetic(step - 1))
    put_h(step, magnetic(step))
    last = LAYERS - step - 1

    @pl.loop(step, last)
    def _(layer):
        electric_values = electric(layer)
        magnetic_values = magnetic(layer + 1)
        put_e(layer, electric_values)
        put_h(layer + 1, magnetic_values)

    put_e(last, electric(last))


def field(step, front, back, near, edge, media, e_xy, e_z, h):
    first = edge is None
    return pl.pallas_call(
        functools.partial(field_kernel, step, 3 if first else 0),
        name="field",
        out_shape=(onchip((2,) + CUBE), onchip(CUBE), onchip((3,) + CUBE), onchip((2, STACK, NX))),
        in_specs=[VM] * 8,
        out_specs=(VM,) * 4,
        compiler_params=params(),
    )(
        front, back, near, front if first else keep(edge),
        keep(media), keep(e_xy), keep(e_z), keep(h),
    )


def solve(stride, arrived, off_cols, volts, m_off, m_diag, m_inv):
    lane = lanes_of(1, NODE_DEV)
    halves = []
    for j in range(NB_DEV):
        pieces = []
        for half in range(OFF // 2):
            total = None
            for side in range(2):
                column = off_cols[j, half * 2 + side]
                row = arrived[pl.ds(column // NB_DEV * stride, 1), :]
                row = jnp.where(column % NB_DEV == side, row, pltpu.roll(row, BS, 1))
                row = jnp.where((lane < BS) == (side == 0), row, 0.0)
                total = row if total is None else total + row
            pieces.append(jnp.broadcast_to(total, (BS, NODE_DEV)))
        halves.append(pieces)
    first = jnp.concatenate([halves[0][0], halves[1][0]], axis=0)
    second = jnp.concatenate([halves[0][1], halves[1][1]], axis=0)
    product = m_off[:, 0:NODE_DEV] * first + m_off[:, NODE_DEV : 2 * NODE_DEV] * second
    offsum = jnp.sum(product, axis=1, keepdims=True)
    kind = row_kind(arrived.shape, stride)
    inject = jnp.sum(jnp.where(kind == 1, arrived[...], 0.0), axis=0, keepdims=True)
    start = volts[...]
    target = charge_scale * start + inject
    diagonal = lax.broadcasted_iota(jnp.int32, (NODE_DEV, NODE_DEV), 0) == lanes_of(NODE_DEV, NODE_DEV)
    iterate = start
    for newton_round in range(NEWTON):
        local = diode_weight * jnp.tanh(iterate) - target
        terms = m_diag[...] * iterate + jnp.where(diagonal, local, 0.0)
        resid = jnp.sum(terms, axis=1, keepdims=True) + offsum
        iterate = iterate - jnp.sum(m_inv[...] * resid, axis=0, keepdims=True)
    return iterate


def apply_ports(stride, table, arrived, columns, sample, coef, e_z, near_rows, deltas):
    @pl.loop(0, table[COUNT])
    def _(group):
        first = group * GROUP
        part = pl.ds(pl.multiple_of(first, GROUP), GROUP)
        for port in range(GROUP):
            near_at = table[NODES + first + port] * stride
            near_rows[port : port + 1, :] = arrived[pl.ds(near_at, 1), :]
        gain, place, lane = columns_at(columns, part)
        current = gain * (sample[part, :] - pick(near_rows[...], lane))
        deltas[...] = spread(-coef[part, :] * current, place, NX)
        for port in range(GROUP):
            spot = table[first + port]
            layer, row = spot // TALL, pl.ds(spot % TALL, 1)
            e_z[layer, row, :] = e_z[layer, row, :] + deltas[port : port + 1, :]


def ports_kernel(
    stride, table, arrived, columns, sample, coef, e_xy, e_in, e_z, up, near_rows, deltas,
):
    e_z[...] = e_in[...]
    apply_ports(stride, table, arrived, columns, sample, coef, e_z, near_rows, deltas)
    write_rows(up, (e_xy.at[0], e_xy.at[1], e_z), CY - 1)


def ports(table, arrived, columns, sample, coef, e_xy, e_z):
    return pl.pallas_call(
        functools.partial(ports_kernel, arrived.shape[0] // ND),
        name="ports",
        out_shape=(onchip(CUBE), stack_of(3)),
        in_specs=[SM] + [VM] * 6,
        out_specs=(VM, VM),
        scratch_shapes=[pltpu.VMEM((GROUP, NODE_DEV), f32), pltpu.VMEM((GROUP, NX), f32)],
        compiler_params=params(),
    )(table, arrived, columns, keep(sample), keep(coef), keep(e_xy), keep(e_z))


def base_kernel(e_xy, e_z, after, down):
    write_rows(down, (e_xy.at[0], e_z), 0)


def base_rows(e_xy, e_z, after):
    return pl.pallas_call(
        base_kernel,
        name="base",
        out_shape=stack_of(2),
        in_specs=[VM, VM, ANY],
        out_specs=VM,
        compiler_params=params(),
    )(keep(e_xy), keep(e_z), after)


def circuit_kernel(
    stride, table, off_cols, arrived, columns, volts, m_off, m_diag, m_inv, e_z, after,
    out, volts_out, sample_out, picked, spread_rows,
):
    @pl.loop(0, table[COUNT])
    def _(group):
        part = pl.ds(pl.multiple_of(group * GROUP, GROUP), GROUP)
        _, place, _ = columns_at(columns, part)
        sample_out[part, :] = gather_cells(e_z, table, group, place, picked)

    solved = solve(stride, arrived, off_cols, volts, m_off, m_diag, m_inv)
    volts_out[...] = solved
    own = slice(0, PORT_DEV)
    gain, _, lane = columns_at(columns, own)
    spread_rows[...] = spread(gain * sample_out[own, :], lane, NODE_DEV)
    out[...] = jnp.where(row_kind(out.shape, 2) == 0, solved, 0.0)
    add_rows(out, 2, [table[NODES + port] for port in range(PORT_DEV)], spread_rows)


def circuit(table, off_cols, arrived, columns, volts, mats, e_z, after):
    return pl.pallas_call(
        functools.partial(circuit_kernel, arrived.shape[0] // ND),
        name="circuit",
        out_shape=(onchip((2 * ND, NODE_DEV)), onchip((1, NODE_DEV)), onchip((REACH, 1))),
        in_specs=[SM, SM] + [VM] * 7 + [ANY],
        out_specs=(VM,) * 3,
        scratch_shapes=[pltpu.VMEM((GROUP, NX), f32), pltpu.VMEM((PORT_DEV, NODE_DEV), f32)],
        compiler_params=params(),
    )(table, off_cols, arrived, columns, volts, *[keep(mat) for mat in mats], keep(e_z), after)


def finish_kernel(
    stride, table, off_cols, arrived, columns, sample, coef, volts, m_off, m_diag, m_inv, e_xy, e_in, h,
    e_out, h_out, volts_out, e_z, near_rows, deltas, sems,
):
    copies, copy = copier(sems)
    layers = pl.ds(DEPTH, CZ)
    for k in range(3):
        copy(h.at[k, layers], h_out.at[k])
    for k in range(2):
        copy(e_xy.at[k, layers], e_out.at[k])
    e_z[...] = e_in[...]
    apply_ports(stride, table, arrived, columns, sample, coef, e_z, near_rows, deltas)
    copy(e_z.at[layers], e_out.at[2])
    volts_out[...] = solve(stride, arrived, off_cols, volts, m_off, m_diag, m_inv)
    for job in copies:
        job.wait()


def finish(table, off_cols, arrived, columns, sample, coef, volts, mats, e_xy, e_z, h):
    return pl.pallas_call(
        functools.partial(finish_kernel, arrived.shape[0] // ND),
        name="finish",
        out_shape=(
            jax.ShapeDtypeStruct((3, CZ, CY, NX), f32),
            jax.ShapeDtypeStruct((3, CZ, CY, NX), f32),
            jax.ShapeDtypeStruct((1, NODE_DEV), f32),
        ),
        in_specs=[SM, SM] + [VM] * 11,
        out_specs=(HBM, HBM, VM),
        scratch_shapes=[
            pltpu.VMEM(CUBE, f32),
            pltpu.VMEM((GROUP, NODE_DEV), f32),
            pltpu.VMEM((GROUP, NX), f32),
            DMA((6,)),
        ],
        compiler_params=params(),
    )(
        table, off_cols, arrived, columns, keep(sample), keep(coef), volts,
        *[keep(mat) for mat in mats], keep(e_xy), keep(e_z), keep(h),
    )


def shifted(value, axis, steps):
    count = lax.axis_size(axis)
    first, last = (max(0, -steps), min(count, count - steps))
    return lax.ppermute(value, axis, [(source, source + steps) for source in range(first, last)])


def exchange(value):
    return lax.all_to_all(value, ("gz", "gy"), 0, 0, tiled=True)


def body(
    e_field,
    h_field,
    e_coef,
    e_loss,
    port_cell,
    port_node,
    port_gain,
    diag_blocks,
    inv_blocks,
    off_blocks,
    off_cols,
    volts_init,
):
    n_gz, n_gy = lax.axis_size("gz"), lax.axis_size("gy")
    grids = (e_field, h_field, e_coef, e_loss)
    volts = volts_init.reshape(1, NODE_DEV)
    up = slab_of(True, grids, volts)
    lower = shifted(up, "gz", 1)
    down = slab_of(False, grids, up)
    upper = shifted(down, "gz", -1)
    out = begin(n_gy, port_cell, port_node, port_gain, e_field, volts, down)
    arrived = exchange(out)
    mats = matrices(diag_blocks, inv_blocks, off_blocks)

    found, columns = plan(n_gz, n_gy, arrived, port_node, port_gain)
    table = jnp.concatenate([found[0], found[1], found[7, 0:1]])

    e_xy, e_z, h, media, sample, coef, up, down = halo(table, columns, lower, upper, *grids)
    edge = None
    for step in range(1, STEPS + 1):
        front = shifted(up, "gy", 1)
        back = shifted(down, "gy", -1)
        if step > 1:
            out, volts, sample = circuit(table, off_cols, arrived, columns, volts, mats, e_z, down)
            out, back = lax.optimization_barrier((out, back))
            arrived = exchange(out)
            arrived, e_z = lax.optimization_barrier((arrived, e_z))
        e_xy, e_z, h, edge = field(step, front, back, down, edge, media, e_xy, e_z, h)
        if step < STEPS:
            e_z, up = ports(table, arrived, columns, sample, coef, e_xy, e_z)
            down = base_rows(e_xy, e_z, up)
        else:
            e_end, h_end, volts = finish(
                table, off_cols, arrived, columns, sample, coef, volts, mats, e_xy, e_z, h
            )
    return e_end, h_end, volts.reshape(-1)


def solution(mesh):
    placed = (
        P(None, "gz", "gy", None),
        P(None, "gz", "gy", None),
        P("gz", "gy", None),
        P("gz", "gy", None),
        P(("gz", "gy")),
        P(),
        P(),
        P(("gz", "gy"), None, None),
        P(("gz", "gy"), None, None),
        P(("gz", "gy"), None, None, None),
        P(("gz", "gy"), None),
        P(("gz", "gy")),
    )
    return jax.shard_map(
        body,
        mesh=mesh,
        in_specs=placed,
        out_specs=(P(None, "gz", "gy", None), P(None, "gz", "gy", None), P(("gz", "gy"))),
        check_vma=False,
    )
```

```python
import functools

import jax
import jax.numpy as jnp
from jax import lax
from jax.experimental import pallas as pl
from jax.experimental.pallas import tpu as pltpu
from jax.sharding import PartitionSpec as P

STEPS = 5
NEWTON = 2
BS = 64
NB_DEV = 2
OFF = 4
PORT_DEV = 32
GROUP = 16
ND = 128
NODE_DEV = NB_DEV * BS
DEPTH = 5
CZ, CY, NX = 32, 16, 256
LAYERS = CZ + 2 * DEPTH
PAD = 0
TALL = CY
STACK = 48
SPARE = 3
PARTS = 8
SIDES = ((0, 0), (-1, 0), (1, 0))
REACH = len(SIDES) * PORT_DEV
NODES, COUNT = REACH, 2 * REACH

time_step = 0.55
charge_scale = 4.0
diode_weight = 0.5

f32 = jnp.float32
VM = pl.BlockSpec(memory_space=pltpu.VMEM)
SM = pl.BlockSpec(memory_space=pltpu.SMEM)
HBM = pl.BlockSpec(memory_space=pltpu.HBM)
ANY = pl.BlockSpec(memory_space=pl.ANY)
DMA = pltpu.SemaphoreType.DMA
CUBE = (LAYERS, TALL, NX)


def onchip(shape):
    return pltpu.VMEM(shape, f32)


def keep(value):
    return pltpu.with_memory_space_constraint(value, pltpu.VMEM)


def away(value):
    return pltpu.with_memory_space_constraint(value, pltpu.HBM)


def params():
    return pltpu.CompilerParams(vmem_limit_bytes=12 << 20)


def lanes_of(count, width):
    return lax.broadcasted_iota(jnp.int32, (count, width), 1)


def pick(rows, lane):
    hit = lanes_of(rows.shape[0], rows.shape[1]) == lane
    return jnp.sum(jnp.where(hit, rows, 0.0), axis=1, keepdims=True)


def spread(column, lane, width):
    hit = lanes_of(column.shape[0], width) == lane
    return jnp.where(hit, column, 0.0)


def columns_at(columns, part):
    block = columns[part, :]
    return block[:, 2:3], block[:, 3:4].astype(jnp.int32), block[:, 4:5].astype(jnp.int32)


def row_kind(shape, stride):
    return lax.broadcasted_iota(jnp.int32, shape, 0) % stride


def add_rows(out, stride, devices, rows_ref):
    for port, device in enumerate(devices):
        spot = pl.ds(device * stride + 1, 1)
        out[spot, :] = out[spot, :] + rows_ref[port : port + 1, :]


def copier(sems):
    copies = []

    def copy(source, target):
        job = pltpu.make_async_copy(source, target, sems.at[len(copies)])
        job.start()
        copies.append(job)

    return copies, copy


def sources_of(e_in, h_in, coef_in, loss_in):
    return [e_in.at[k] for k in range(3)] + [h_in.at[k] for k in range(3)] + [coef_in, loss_in]


def write_rows(stack, sources, row):
    for slot, source in enumerate(sources):
        for layer in range(LAYERS):
            stack[slot, layer : layer + 1, :] = source[layer, row : row + 1, :]
        stack[slot, LAYERS:STACK, :] = jnp.zeros((STACK - LAYERS, NX), f32)


def stack_of(count):
    return jax.ShapeDtypeStruct((count, STACK, NX), f32)


def slab_kernel(top, e_in, h_in, coef_in, loss_in, after, slab, sems):
    copies, copy = copier(sems)
    layers = pl.ds(CZ - DEPTH if top else 0, DEPTH)
    for part, source in enumerate(sources_of(e_in, h_in, coef_in, loss_in)):
        copy(source.at[layers], slab.at[pl.ds(part * DEPTH, DEPTH)])
    for job in copies:
        job.wait()


def slab_of(top, grids, after):
    return pl.pallas_call(
        functools.partial(slab_kernel, top),
        name="slab",
        out_shape=jax.ShapeDtypeStruct((PARTS * DEPTH, CY, NX), f32),
        in_specs=[HBM] * 4 + [ANY],
        out_specs=VM,
        scratch_shapes=[DMA((PARTS,))],
        compiler_params=params(),
    )(*map(away, grids), after)


def begin_kernel(
    n_gy, cells, nodes, gains, e_in, cell_row, volts, after, out, e_z, picked, hits, rows_ref, sem,
):
    load = pltpu.make_async_copy(e_in.at[2], e_z, sem)
    load.start()
    first = (lax.axis_index("gz") * n_gy + lax.axis_index("gy")) * PORT_DEV
    wide, narrow = lanes_of(1, NX), lanes_of(1, NODE_DEV)
    own_nodes = [nodes[first + port] for port in range(PORT_DEV)]
    for port, node in enumerate(own_nodes):
        hits[port : port + 1, :] = jnp.where(narrow == node % NODE_DEV, 1.0, 0.0)
    kind = row_kind(out.shape, 4)
    rows_ref[0:1, :] = jnp.zeros((1, NODE_DEV), f32)
    rows_ref[0:1, 0:PORT_DEV] = cell_row[...].astype(f32)
    out[...] = jnp.where(kind == 0, volts[...], jnp.where(kind == 2, rows_ref[0:1, :], 0.0))

    load.wait()
    for port in range(PORT_DEV):
        cell = cells[port]
        line = cell // NX
        value = e_z[line // CY, pl.ds(line % CY, 1), :] * gains[first + port]
        picked[port : port + 1, :] = jnp.where(wide == cell % NX, value, 0.0)
    rows_ref[...] = hits[...] * jnp.sum(picked[...], axis=1, keepdims=True)
    add_rows(out, 4, [node // NODE_DEV for node in own_nodes], rows_ref)


def begin(n_gy, cells, nodes, gains, e_in, volts, after):
    return pl.pallas_call(
        functools.partial(begin_kernel, n_gy),
        name="begin",
        out_shape=jax.ShapeDtypeStruct((4 * ND, NODE_DEV), f32),
        in_specs=[SM, SM, SM, HBM, VM, VM, ANY],
        out_specs=VM,
        scratch_shapes=[
            pltpu.VMEM((CZ, CY, NX), f32),
            pltpu.VMEM((PORT_DEV, NX), f32),
            pltpu.VMEM((PORT_DEV, NODE_DEV), f32),
            pltpu.VMEM((PORT_DEV, NODE_DEV), f32),
            DMA,
        ],
        compiler_params=params(),
    )(cells, nodes, gains, away(e_in), cells.reshape(1, -1), volts, after)


def matrices_kernel(diag, inv, off, m_off, m_diag, m_inv):
    m_diag[...] = jnp.zeros_like(m_diag)
    m_inv[...] = jnp.zeros_like(m_inv)
    for j in range(NB_DEV):
        part = slice(j * BS, (j + 1) * BS)
        m_diag[part, part] = diag[j]
        m_inv[part, part] = inv[j].T
        for k in range(OFF):
            m_off[part, k * BS : (k + 1) * BS] = off[j, k]


def matrices(diag, inv, off):
    square = onchip((NODE_DEV, NODE_DEV))
    return pl.pallas_call(
        matrices_kernel,
        name="matrices",
        out_shape=(onchip((NODE_DEV, OFF * BS)), square, square),
        in_specs=[VM, VM, VM],
        out_specs=(VM, VM, VM),
        compiler_params=params(),
    )(diag, inv, off)


def plan_kernel(n_gz, n_gy, arrived, nodes, gains, found, columns, facts):
    gz, gy = lax.axis_index("gz"), lax.axis_index("gy")
    lane = lanes_of(1, NODE_DEV)
    width = NODE_DEV // PORT_DEV
    facts[...] = jnp.zeros_like(facts)
    for group, (side_z, side_y) in enumerate(SIDES):
        at_z, at_y = gz + side_z, gy + side_y
        exists = (at_z >= 0) & (at_z < n_gz) & (at_y >= 0) & (at_y < n_gy)
        device = jnp.where(exists, at_z * n_gy + at_y, 0)
        slot = group % width
        turn = (slot - device % width + width) % width * PORT_DEV
        row = pl.ds(device // width, 1)
        node, gain = pltpu.roll(nodes[row, :], turn, 1), pltpu.roll(gains[row, :], turn, 1)
        cell = pltpu.roll(arrived[pl.ds(4 * device + 2, 1), :], slot * PORT_DEV, 1).astype(jnp.int32)
        layer = cell // (CY * NX) + (side_z * CZ + DEPTH)
        line = (cell // NX) % CY + (side_y * CY + PAD)
        valid = (layer >= 1) & (layer < LAYERS - 1)
        valid &= (line > PAD - DEPTH) & (line < PAD + CY + DEPTH - 1)
        valid &= (lane // PORT_DEV == slot) & (jnp.where(exists, 1, 0) > 0)
        values = (layer * TALL + line, node // NODE_DEV, gain, cell % NX, node % NODE_DEV, 1)
        part = slice(group // width * NODE_DEV, (group // width + 1) * NODE_DEV)
        for kind, value in enumerate(values):
            fact = jnp.where(valid, jnp.asarray(value).astype(f32), 0.0)
            facts[kind : kind + 1, part] = facts[kind : kind + 1, part] + fact

    used = facts[5:6, :]
    total = used.shape[1]
    upper = lax.broadcasted_iota(jnp.int32, (total, total), 0) <= lanes_of(total, total)
    ones = jnp.broadcast_to(used, (8, total))
    order = jnp.dot(ones, upper.astype(f32), preferred_element_type=f32)[0:1, :] - 1.0
    spot = lax.broadcasted_iota(jnp.int32, (REACH, total), 0)
    chosen = jnp.where((spot == order.astype(jnp.int32)) & (used > 0.0), 1.0, 0.0)
    across = (((1,), (1,)), ((), ()))
    columns[...] = lax.dot_general(
        chosen, facts[...], across, precision=lax.Precision.HIGHEST, preferred_element_type=f32
    )
    rows = lax.dot_general(
        facts[...], chosen, across, precision=lax.Precision.HIGHEST, preferred_element_type=f32
    )
    count = jnp.sum(used, axis=1, keepdims=True)
    groups = ((count + (GROUP - 1)) * (1.0 / GROUP)).astype(jnp.int32)
    kind = lax.broadcasted_iota(jnp.int32, rows.shape, 0)
    unused = (kind == 0) & (lanes_of(8, REACH) >= count.astype(jnp.int32))
    whole = jnp.where(unused, PAD, (rows + 0.5).astype(jnp.int32))
    found[...] = jnp.where(kind == 7, groups, whole)


def plan(n_gz, n_gy, arrived, nodes, gains):
    lanes = -(-REACH // NODE_DEV) * NODE_DEV
    return pl.pallas_call(
        functools.partial(plan_kernel, n_gz, n_gy),
        name="plan",
        out_shape=(
            jax.ShapeDtypeStruct((8, REACH), jnp.int32),
            jax.ShapeDtypeStruct((REACH, 8), f32),
        ),
        in_specs=[VM, VM, VM],
        out_specs=(VM, VM),
        scratch_shapes=[pltpu.VMEM((8, lanes), f32)],
        compiler_params=params(),
    )(arrived, nodes.reshape(-1, NODE_DEV), gains.reshape(-1, NODE_DEV))


def halo_kernel(
    lower, upper, e_in, h_in, coef_in, loss_in, e_xy, e_z, h, media, up, down, sems,
):
    copies, copy = copier(sems)
    targets = [
        e_xy.at[0], e_xy.at[1], e_z, h.at[0], h.at[1], h.at[2], media.at[0], media.at[1],
    ]
    for part, source in enumerate(sources_of(e_in, h_in, coef_in, loss_in)):
        given = pl.ds(part * DEPTH, DEPTH)
        copy(source, targets[part].at[pl.ds(DEPTH, CZ)])
        copy(lower.at[given], targets[part].at[pl.ds(0, DEPTH)])
        copy(upper.at[given], targets[part].at[pl.ds(DEPTH + CZ, DEPTH)])
    for job in copies:
        job.wait()
    write_rows(up, targets[:4] + [targets[5]], CY - 1)
    write_rows(down, (targets[0], targets[2]), 0)

    @pl.loop(0, LAYERS)
    def _(layer):
        media[1, layer] = 1.0 - media[1, layer]


def samples_kernel(found, columns, e_z, media, sample, coef, picked):
    @pl.loop(0, found[COUNT])
    def _(group):
        part = pl.ds(pl.multiple_of(group * GROUP, GROUP), GROUP)
        _, place, _ = columns_at(columns, part)
        sample[part, :] = gather_cells(e_z, found, group, place, picked)
        coef[part, :] = gather_cells(media.at[0], found, group, place, picked)


def gather_cells(source, found, group, place, picked):
    for port in range(GROUP):
        spot = found[group * GROUP + port]
        picked[port : port + 1, :] = source[spot // TALL, pl.ds(spot % TALL, 1), :]
    return pick(picked[...], place)


def halo(lower, upper, e_in, h_in, coef, loss):
    return pl.pallas_call(
        halo_kernel,
        name="halo",
        out_shape=(
            onchip((2,) + CUBE),
            onchip(CUBE),
            onchip((3,) + CUBE),
            onchip((2,) + CUBE),
            stack_of(5),
            stack_of(2),
        ),
        in_specs=[HBM] * 6,
        out_specs=(VM,) * 6,
        scratch_shapes=[DMA((24,))],
        compiler_params=params(),
    )(*map(away, (lower, upper, e_in, h_in, coef, loss)))


def samples(found, columns, e_z, media):
    return pl.pallas_call(
        samples_kernel,
        name="samples",
        out_shape=(onchip((REACH, 1)), onchip((REACH, 1))),
        in_specs=[SM, VM, VM, VM],
        out_specs=(VM, VM),
        scratch_shapes=[pltpu.VMEM((GROUP, NX), f32)],
        compiler_params=params(),
    )(found, columns, keep(e_z), keep(media))


def field_kernel(
    step, base, front, back, near, edge_in, media, e_xy, e_z, h, to_xy, to_z, to_h, edge
):
    low_z = jnp.where(lax.axis_index("gz") > 0, time_step, 0.0)
    low_y = jnp.where(lax.axis_index("gy") > 0, time_step, 0.0)
    lane = lanes_of(TALL, NX)
    last_lane, first_lane = lane == NX - 1, lane == 0
    row = lax.broadcasted_iota(jnp.int32, (TALL, NX), 0)
    last_row, first_row = row == TALL - 1, row == 0

    def next_x(value):
        return jnp.where(last_lane, 0.0, pltpu.roll(value, NX - 1, 1))

    def prior_x(value):
        return jnp.where(first_lane, 0.0, pltpu.roll(value, 1, 1))

    def next_y(value, beyond):
        return jnp.where(last_row, beyond, pltpu.roll(value, TALL - 1, 0))

    def prior_y(value, beyond):
        return jnp.where(first_row, beyond, pltpu.roll(value, 1, 0))

    span = pl.ds(0, LAYERS)
    out_x, out_y, out_z = front[0, span, :], front[1, span, :], front[2, span, :]
    out_y_above = front[1, pl.ds(1, LAYERS), :]
    tall_lane = lanes_of(LAYERS, NX)
    out_y_next = jnp.where(tall_lane == NX - 1, 0.0, pltpu.roll(out_y, NX - 1, 1))
    near_x, near_z = near[0, span, :], near[1, span, :]
    edge_x, edge_z = edge_in[base, span, :], edge_in[base + 1, span, :]
    edge[0, span, :] = edge_x - low_y * ((near_z - out_z) - (out_y_above - out_y))
    edge[1, span, :] = edge_z - low_y * ((out_y_next - out_y) - (near_x - out_x))

    def magnetic(layer):
        e_x, e_y, e_zz = e_xy[0, layer], e_xy[1, layer], e_z[layer]
        rate = jnp.where(layer < DEPTH, low_z, time_step)
        beyond = pl.ds(layer, 1)
        curl_x = (next_y(e_zz, back[1, beyond, :]) - e_zz) - (e_xy[1, layer + 1] - e_y)
        curl_y = (e_xy[0, layer + 1] - e_x) - (next_x(e_zz) - e_zz)
        curl_z = (next_x(e_y) - e_y) - (next_y(e_x, back[0, beyond, :]) - e_x)
        return (h[0, layer] - rate * curl_x, h[1, layer] - rate * curl_y, h[2, layer] - rate * curl_z)

    def electric(layer):
        h_x, h_y, h_z = to_h[0, layer], to_h[1, layer], to_h[2, layer]
        coef, kept = media[0, layer], media[1, layer]
        beyond = pl.ds(layer, 1)
        back_x = (h_z - prior_y(h_z, edge[1, beyond, :])) - (h_y - to_h[1, layer - 1])
        back_y = (h_x - to_h[0, layer - 1]) - (h_z - prior_x(h_z))
        back_z = (h_y - prior_x(h_y)) - (h_x - prior_y(h_x, edge[0, beyond, :]))
        return (
            kept * e_xy[0, layer] + coef * back_x,
            kept * e_xy[1, layer] + coef * back_y,
            kept * e_z[layer] + coef * back_z,
        )

    def put_h(layer, values):
        to_h[0, layer], to_h[1, layer], to_h[2, layer] = values

    def put_e(layer, values):
        to_xy[0, layer], to_xy[1, layer], to_z[layer] = values

    put_h(step - 1, magnetic(step - 1))
    put_h(step, magnetic(step))
    last = LAYERS - step - 1

    electric_values = electric(step)
    put_h(step + 1, magnetic(step + 1))
    put_e(step, electric_values)

    @pl.loop(step + 1, last, step=2)
    def _(layer):
        electric_values = electric(layer)
        magnetic_values = magnetic(layer + 1)
        magnetic_above = magnetic(layer + 2)
        put_e(layer, electric_values)
        put_h(layer + 1, magnetic_values)
        electric_above = electric(layer + 1)
        put_h(layer + 2, magnetic_above)
        put_e(layer + 1, electric_above)

    put_e(last, electric(last))


def field(step, front, back, near, edge, media, e_xy, e_z, h):
    first = edge is None
    return pl.pallas_call(
        functools.partial(field_kernel, step, 3 if first else 0),
        name="field",
        out_shape=(onchip((2,) + CUBE), onchip(CUBE), onchip((3,) + CUBE), onchip((2, STACK, NX))),
        in_specs=[VM] * 8,
        out_specs=(VM,) * 4,
        compiler_params=params(),
    )(
        front, back, near, front if first else keep(edge),
        keep(media), keep(e_xy), keep(e_z), keep(h),
    )


def solve(stride, arrived, off_cols, volts, m_off, m_diag, m_inv):
    lane = lanes_of(1, NODE_DEV)
    halves = []
    for j in range(NB_DEV):
        pieces = []
        for half in range(OFF // 2):
            total = None
            for side in range(2):
                column = off_cols[j, half * 2 + side]
                row = arrived[pl.ds(column // NB_DEV * stride, 1), :]
                row = jnp.where(column % NB_DEV == side, row, pltpu.roll(row, BS, 1))
                row = jnp.where((lane < BS) == (side == 0), row, 0.0)
                total = row if total is None else total + row
            pieces.append(jnp.broadcast_to(total, (BS, NODE_DEV)))
        halves.append(pieces)
    first = jnp.concatenate([halves[0][0], halves[1][0]], axis=0)
    second = jnp.concatenate([halves[0][1], halves[1][1]], axis=0)
    product = m_off[:, 0:NODE_DEV] * first + m_off[:, NODE_DEV : 2 * NODE_DEV] * second
    offsum = jnp.sum(product, axis=1, keepdims=True)
    kind = row_kind(arrived.shape, stride)
    inject = jnp.sum(jnp.where(kind == 1, arrived[...], 0.0), axis=0, keepdims=True)
    start = volts[...]
    target = charge_scale * start + inject
    diagonal = lax.broadcasted_iota(jnp.int32, (NODE_DEV, NODE_DEV), 0) == lanes_of(NODE_DEV, NODE_DEV)
    iterate = start
    for newton_round in range(NEWTON):
        local = diode_weight * jnp.tanh(iterate) - target
        terms = m_diag[...] * iterate + jnp.where(diagonal, local, 0.0)
        resid = jnp.sum(terms, axis=1, keepdims=True) + offsum
        iterate = iterate - jnp.sum(m_inv[...] * resid, axis=0, keepdims=True)
    return iterate


def apply_ports(stride, table, arrived, columns, sample, coef, e_z, near_rows, deltas):
    @pl.loop(0, table[COUNT])
    def _(group):
        first = group * GROUP
        part = pl.ds(pl.multiple_of(first, GROUP), GROUP)
        for port in range(GROUP):
            near_at = table[NODES + first + port] * stride
            near_rows[port : port + 1, :] = arrived[pl.ds(near_at, 1), :]
        gain, place, lane = columns_at(columns, part)
        current = gain * (sample[part, :] - pick(near_rows[...], lane))
        deltas[...] = spread(-coef[part, :] * current, place, NX)
        for port in range(GROUP):
            spot = table[first + port]
            layer, row = spot // TALL, pl.ds(spot % TALL, 1)
            e_z[layer, row, :] = e_z[layer, row, :] + deltas[port : port + 1, :]


def ports_kernel(
    stride, table, arrived, columns, sample, coef, e_xy, e_in, e_z, up, near_rows, deltas,
):
    e_z[...] = e_in[...]
    apply_ports(stride, table, arrived, columns, sample, coef, e_z, near_rows, deltas)
    write_rows(up, (e_xy.at[0], e_xy.at[1], e_z), CY - 1)


def ports(table, arrived, columns, sample, coef, e_xy, e_z):
    return pl.pallas_call(
        functools.partial(ports_kernel, arrived.shape[0] // ND),
        name="ports",
        out_shape=(onchip(CUBE), stack_of(3)),
        in_specs=[SM] + [VM] * 6,
        out_specs=(VM, VM),
        scratch_shapes=[pltpu.VMEM((GROUP, NODE_DEV), f32), pltpu.VMEM((GROUP, NX), f32)],
        compiler_params=params(),
    )(table, arrived, columns, keep(sample), keep(coef), keep(e_xy), keep(e_z))


def base_kernel(e_xy, e_z, after, down):
    write_rows(down, (e_xy.at[0], e_z), 0)
    for slot in range(2, SPARE):
        down[slot] = jnp.zeros((STACK, NX), f32)


def base_rows(e_xy, e_z, after):
    return pl.pallas_call(
        base_kernel,
        name="base",
        out_shape=stack_of(SPARE),
        in_specs=[VM, VM, ANY],
        out_specs=VM,
        compiler_params=params(),
    )(keep(e_xy), keep(e_z), after)


def circuit_kernel(
    stride, table, off_cols, arrived, columns, volts, m_off, m_diag, m_inv, e_z, after,
    out, volts_out, sample_out, picked, spread_rows,
):
    @pl.loop(0, table[COUNT])
    def _(group):
        part = pl.ds(pl.multiple_of(group * GROUP, GROUP), GROUP)
        _, place, _ = columns_at(columns, part)
        sample_out[part, :] = gather_cells(e_z, table, group, place, picked)

    solved = solve(stride, arrived, off_cols, volts, m_off, m_diag, m_inv)
    volts_out[...] = solved
    own = slice(0, PORT_DEV)
    gain, _, lane = columns_at(columns, own)
    spread_rows[...] = spread(gain * sample_out[own, :], lane, NODE_DEV)
    out[...] = jnp.where(row_kind(out.shape, 2) == 0, solved, 0.0)
    add_rows(out, 2, [table[NODES + port] for port in range(PORT_DEV)], spread_rows)


def circuit(table, off_cols, arrived, columns, volts, mats, e_z, after):
    return pl.pallas_call(
        functools.partial(circuit_kernel, arrived.shape[0] // ND),
        name="circuit",
        out_shape=(onchip((2 * ND, NODE_DEV)), onchip((1, NODE_DEV)), onchip((REACH, 1))),
        in_specs=[SM, SM] + [VM] * 7 + [ANY],
        out_specs=(VM,) * 3,
        scratch_shapes=[pltpu.VMEM((GROUP, NX), f32), pltpu.VMEM((PORT_DEV, NODE_DEV), f32)],
        compiler_params=params(),
    )(table, off_cols, arrived, columns, volts, *[keep(mat) for mat in mats], keep(e_z), after)


def finish_kernel(
    stride, table, off_cols, arrived, columns, sample, coef, volts, m_off, m_diag, m_inv, e_xy, e_in, h,
    e_out, h_out, volts_out, e_z, near_rows, deltas, sems,
):
    copies, copy = copier(sems)
    layers = pl.ds(DEPTH, CZ)
    for k in range(3):
        copy(h.at[k, layers], h_out.at[k])
    for k in range(2):
        copy(e_xy.at[k, layers], e_out.at[k])
    e_z[...] = e_in[...]
    apply_ports(stride, table, arrived, columns, sample, coef, e_z, near_rows, deltas)
    copy(e_z.at[layers], e_out.at[2])
    volts_out[...] = solve(stride, arrived, off_cols, volts, m_off, m_diag, m_inv)
    for job in copies:
        job.wait()


def finish(table, off_cols, arrived, columns, sample, coef, volts, mats, e_xy, e_z, h):
    return pl.pallas_call(
        functools.partial(finish_kernel, arrived.shape[0] // ND),
        name="finish",
        out_shape=(
            jax.ShapeDtypeStruct((3, CZ, CY, NX), f32),
            jax.ShapeDtypeStruct((3, CZ, CY, NX), f32),
            jax.ShapeDtypeStruct((1, NODE_DEV), f32),
        ),
        in_specs=[SM, SM] + [VM] * 11,
        out_specs=(HBM, HBM, VM),
        scratch_shapes=[
            pltpu.VMEM(CUBE, f32),
            pltpu.VMEM((GROUP, NODE_DEV), f32),
            pltpu.VMEM((GROUP, NX), f32),
            DMA((6,)),
        ],
        compiler_params=params(),
    )(
        table, off_cols, arrived, columns, keep(sample), keep(coef), volts,
        *[keep(mat) for mat in mats], keep(e_xy), keep(e_z), keep(h),
    )


def shifted(value, axis, steps):
    count = lax.axis_size(axis)
    first, last = (max(0, -steps), min(count, count - steps))
    return lax.ppermute(value, axis, [(source, source + steps) for source in range(first, last)])


def exchange(value):
    return lax.all_to_all(value, ("gz", "gy"), 0, 0, tiled=True)


def body(
    e_field,
    h_field,
    e_coef,
    e_loss,
    port_cell,
    port_node,
    port_gain,
    diag_blocks,
    inv_blocks,
    off_blocks,
    off_cols,
    volts_init,
):
    n_gz, n_gy = lax.axis_size("gz"), lax.axis_size("gy")
    grids = (e_field, h_field, e_coef, e_loss)
    volts = volts_init.reshape(1, NODE_DEV)
    up = slab_of(True, grids, volts)
    lower = shifted(up, "gz", 1)
    down = slab_of(False, grids, up)
    upper = shifted(down, "gz", -1)
    out = begin(n_gy, port_cell, port_node, port_gain, e_field, volts, down)
    arrived = exchange(out)
    lower, upper, arrived = lax.optimization_barrier((lower, upper, arrived))
    mats = matrices(diag_blocks, inv_blocks, off_blocks)
    e_xy, e_z, h, media, up, down = halo(lower, upper, *grids)
    found, columns = plan(n_gz, n_gy, arrived, port_node, port_gain)
    table = jnp.concatenate([found[0], found[1], found[7, 0:1]])
    sample, coef = samples(table, columns, e_z, media)
    edge = None
    for step in range(1, STEPS + 1):
        front = shifted(up, "gy", 1)
        if step > 1:
            out, volts, sample = circuit(table, off_cols, arrived, columns, volts, mats, e_z, up)
            down = base_rows(e_xy, e_z, out)
        back = shifted(down, "gy", -1)
        if step > 1:
            out, front = lax.optimization_barrier((out, front))
            arrived = exchange(out)
            arrived, e_z = lax.optimization_barrier((arrived, e_z))
        e_xy, e_z, h, edge = field(step, front, back, down, edge, media, e_xy, e_z, h)
        if step < STEPS:
            e_z, up = ports(table, arrived, columns, sample, coef, e_xy, e_z)
        else:
            e_end, h_end, volts = finish(
                table, off_cols, arrived, columns, sample, coef, volts, mats, e_xy, e_z, h
            )
    return e_end, h_end, volts.reshape(-1)


def solution(mesh):
    placed = (
        P(None, "gz", "gy", None),
        P(None, "gz", "gy", None),
        P("gz", "gy", None),
        P("gz", "gy", None),
        P(("gz", "gy")),
        P(),
        P(),
        P(("gz", "gy"), None, None),
        P(("gz", "gy"), None, None),
        P(("gz", "gy"), None, None, None),
        P(("gz", "gy"), None),
        P(("gz", "gy")),
    )
    return jax.shard_map(
        body,
        mesh=mesh,
        in_specs=placed,
        out_specs=(P(None, "gz", "gy", None), P(None, "gz", "gy", None), P(("gz", "gy"))),
        check_vma=False,
    )
```

```python
import functools

import jax
import jax.numpy as jnp
from jax import lax
from jax.experimental import pallas as pl
from jax.experimental.pallas import tpu as pltpu
from jax.sharding import PartitionSpec as P

STEPS = 5
NEWTON = 2
BS = 64
NB_DEV = 2
OFF = 4
PORT_DEV = 32
GROUP = 16
ND = 128
NODE_DEV = NB_DEV * BS
DEPTH = 5
CZ, CY, NX = 32, 16, 256
LAYERS = CZ + 2 * DEPTH
PAD = 0
TALL = CY
STACK = 48
PARTS = 8
SIDES = ((0, 0), (-1, 0), (1, 0))
REACH = len(SIDES) * PORT_DEV
NODES, COUNT = REACH, 2 * REACH

time_step = 0.55
charge_scale = 4.0
diode_weight = 0.5

f32 = jnp.float32
VM = pl.BlockSpec(memory_space=pltpu.VMEM)
SM = pl.BlockSpec(memory_space=pltpu.SMEM)
HBM = pl.BlockSpec(memory_space=pltpu.HBM)
ANY = pl.BlockSpec(memory_space=pl.ANY)
DMA = pltpu.SemaphoreType.DMA
CUBE = (LAYERS, TALL, NX)


def onchip(shape):
    return pltpu.VMEM(shape, f32)


def keep(value):
    return pltpu.with_memory_space_constraint(value, pltpu.VMEM)


def away(value):
    return pltpu.with_memory_space_constraint(value, pltpu.HBM)


def params():
    return pltpu.CompilerParams(vmem_limit_bytes=12 << 20)


def lanes_of(count, width):
    return lax.broadcasted_iota(jnp.int32, (count, width), 1)


def pick(rows, lane):
    hit = lanes_of(rows.shape[0], rows.shape[1]) == lane
    return jnp.sum(jnp.where(hit, rows, 0.0), axis=1, keepdims=True)


def spread(column, lane, width):
    hit = lanes_of(column.shape[0], width) == lane
    return jnp.where(hit, column, 0.0)


def columns_at(columns, part):
    block = columns[part, :]
    return block[:, 2:3], block[:, 3:4].astype(jnp.int32), block[:, 4:5].astype(jnp.int32)


def row_kind(shape, stride):
    return lax.broadcasted_iota(jnp.int32, shape, 0) % stride


def add_rows(out, stride, devices, rows_ref):
    for port, device in enumerate(devices):
        spot = pl.ds(device * stride + 1, 1)
        out[spot, :] = out[spot, :] + rows_ref[port : port + 1, :]


def copier(sems):
    copies = []

    def copy(source, target):
        job = pltpu.make_async_copy(source, target, sems.at[len(copies)])
        job.start()
        copies.append(job)

    return copies, copy


def sources_of(e_in, h_in, coef_in, loss_in):
    return [e_in.at[k] for k in range(3)] + [h_in.at[k] for k in range(3)] + [coef_in, loss_in]


def write_rows(stack, sources, swap):
    even = lax.axis_index("gy") % 2 == 0
    row = jnp.where(even, CY - 1, 0) if swap == 0 else jnp.where(even, 0, CY - 1)
    for slot, source in enumerate(sources):
        for layer in range(LAYERS):
            stack[slot, layer : layer + 1, :] = source[layer, pl.ds(row, 1), :]
        stack[slot, LAYERS:STACK, :] = jnp.zeros((STACK - LAYERS, NX), f32)


def stack_of(count):
    return jax.ShapeDtypeStruct((count, STACK, NX), f32)


def slab_kernel(top, e_in, h_in, coef_in, loss_in, after, slab, sems):
    copies, copy = copier(sems)
    layers = pl.ds(CZ - DEPTH if top else 0, DEPTH)
    for part, source in enumerate(sources_of(e_in, h_in, coef_in, loss_in)):
        copy(source.at[layers], slab.at[pl.ds(part * DEPTH, DEPTH)])
    for job in copies:
        job.wait()


def slab_of(top, grids, after):
    return pl.pallas_call(
        functools.partial(slab_kernel, top),
        name="slab",
        out_shape=jax.ShapeDtypeStruct((PARTS * DEPTH, CY, NX), f32),
        in_specs=[HBM] * 4 + [ANY],
        out_specs=VM,
        scratch_shapes=[DMA((PARTS,))],
        compiler_params=params(),
    )(*map(away, grids), after)


def begin_kernel(
    n_gy, cells, nodes, gains, e_in, cell_row, volts, after, out, e_z, picked, hits, rows_ref, sem,
):
    load = pltpu.make_async_copy(e_in.at[2], e_z, sem)
    load.start()
    first = (lax.axis_index("gz") * n_gy + lax.axis_index("gy")) * PORT_DEV
    wide, narrow = lanes_of(1, NX), lanes_of(1, NODE_DEV)
    own_nodes = [nodes[first + port] for port in range(PORT_DEV)]
    for port, node in enumerate(own_nodes):
        hits[port : port + 1, :] = jnp.where(narrow == node % NODE_DEV, 1.0, 0.0)
    kind = row_kind(out.shape, 4)
    rows_ref[0:1, :] = jnp.zeros((1, NODE_DEV), f32)
    rows_ref[0:1, 0:PORT_DEV] = cell_row[...].astype(f32)
    out[...] = jnp.where(kind == 0, volts[...], jnp.where(kind == 2, rows_ref[0:1, :], 0.0))

    load.wait()
    for port in range(PORT_DEV):
        cell = cells[port]
        line = cell // NX
        value = e_z[line // CY, pl.ds(line % CY, 1), :] * gains[first + port]
        picked[port : port + 1, :] = jnp.where(wide == cell % NX, value, 0.0)
    rows_ref[...] = hits[...] * jnp.sum(picked[...], axis=1, keepdims=True)
    add_rows(out, 4, [node // NODE_DEV for node in own_nodes], rows_ref)


def begin(n_gy, cells, nodes, gains, e_in, volts, after):
    return pl.pallas_call(
        functools.partial(begin_kernel, n_gy),
        name="begin",
        out_shape=jax.ShapeDtypeStruct((4 * ND, NODE_DEV), f32),
        in_specs=[SM, SM, SM, HBM, VM, VM, ANY],
        out_specs=VM,
        scratch_shapes=[
            pltpu.VMEM((CZ, CY, NX), f32),
            pltpu.VMEM((PORT_DEV, NX), f32),
            pltpu.VMEM((PORT_DEV, NODE_DEV), f32),
            pltpu.VMEM((PORT_DEV, NODE_DEV), f32),
            DMA,
        ],
        compiler_params=params(),
    )(cells, nodes, gains, away(e_in), cells.reshape(1, -1), volts, after)


def matrices_kernel(diag, inv, off, m_off, m_diag, m_inv):
    m_diag[...] = jnp.zeros_like(m_diag)
    m_inv[...] = jnp.zeros_like(m_inv)
    for j in range(NB_DEV):
        part = slice(j * BS, (j + 1) * BS)
        m_diag[part, part] = diag[j]
        m_inv[part, part] = inv[j].T
        for k in range(OFF):
            m_off[part, k * BS : (k + 1) * BS] = off[j, k]


def matrices(diag, inv, off):
    square = onchip((NODE_DEV, NODE_DEV))
    return pl.pallas_call(
        matrices_kernel,
        name="matrices",
        out_shape=(onchip((NODE_DEV, OFF * BS)), square, square),
        in_specs=[VM, VM, VM],
        out_specs=(VM, VM, VM),
        compiler_params=params(),
    )(diag, inv, off)


def plan_kernel(n_gz, n_gy, arrived, nodes, gains, found, columns, facts):
    gz, gy = lax.axis_index("gz"), lax.axis_index("gy")
    lane = lanes_of(1, NODE_DEV)
    width = NODE_DEV // PORT_DEV
    facts[...] = jnp.zeros_like(facts)
    for group, (side_z, side_y) in enumerate(SIDES):
        at_z, at_y = gz + side_z, gy + side_y
        exists = (at_z >= 0) & (at_z < n_gz) & (at_y >= 0) & (at_y < n_gy)
        device = jnp.where(exists, at_z * n_gy + at_y, 0)
        slot = group % width
        turn = (slot - device % width + width) % width * PORT_DEV
        row = pl.ds(device // width, 1)
        node, gain = pltpu.roll(nodes[row, :], turn, 1), pltpu.roll(gains[row, :], turn, 1)
        cell = pltpu.roll(arrived[pl.ds(4 * device + 2, 1), :], slot * PORT_DEV, 1).astype(jnp.int32)
        layer = cell // (CY * NX) + (side_z * CZ + DEPTH)
        line = (cell // NX) % CY + (side_y * CY + PAD)
        valid = (layer >= 1) & (layer < LAYERS - 1)
        valid &= (line > PAD - DEPTH) & (line < PAD + CY + DEPTH - 1)
        valid &= (lane // PORT_DEV == slot) & (jnp.where(exists, 1, 0) > 0)
        values = (layer * TALL + line, node // NODE_DEV, gain, cell % NX, node % NODE_DEV, 1)
        part = slice(group // width * NODE_DEV, (group // width + 1) * NODE_DEV)
        for kind, value in enumerate(values):
            fact = jnp.where(valid, jnp.asarray(value).astype(f32), 0.0)
            facts[kind : kind + 1, part] = facts[kind : kind + 1, part] + fact

    used = facts[5:6, :]
    total = used.shape[1]
    upper = lax.broadcasted_iota(jnp.int32, (total, total), 0) <= lanes_of(total, total)
    ones = jnp.broadcast_to(used, (8, total))
    order = jnp.dot(ones, upper.astype(f32), preferred_element_type=f32)[0:1, :] - 1.0
    spot = lax.broadcasted_iota(jnp.int32, (REACH, total), 0)
    chosen = jnp.where((spot == order.astype(jnp.int32)) & (used > 0.0), 1.0, 0.0)
    across = (((1,), (1,)), ((), ()))
    columns[...] = lax.dot_general(
        chosen, facts[...], across, precision=lax.Precision.HIGHEST, preferred_element_type=f32
    )
    rows = lax.dot_general(
        facts[...], chosen, across, precision=lax.Precision.HIGHEST, preferred_element_type=f32
    )
    count = jnp.sum(used, axis=1, keepdims=True)
    groups = ((count + (GROUP - 1)) * (1.0 / GROUP)).astype(jnp.int32)
    kind = lax.broadcasted_iota(jnp.int32, rows.shape, 0)
    unused = (kind == 0) & (lanes_of(8, REACH) >= count.astype(jnp.int32))
    whole = jnp.where(unused, PAD, (rows + 0.5).astype(jnp.int32))
    found[...] = jnp.where(kind == 7, groups, whole)


def plan(n_gz, n_gy, arrived, nodes, gains):
    lanes = -(-REACH // NODE_DEV) * NODE_DEV
    return pl.pallas_call(
        functools.partial(plan_kernel, n_gz, n_gy),
        name="plan",
        out_shape=(
            jax.ShapeDtypeStruct((8, REACH), jnp.int32),
            jax.ShapeDtypeStruct((REACH, 8), f32),
        ),
        in_specs=[VM, VM, VM],
        out_specs=(VM, VM),
        scratch_shapes=[pltpu.VMEM((8, lanes), f32)],
        compiler_params=params(),
    )(arrived, nodes.reshape(-1, NODE_DEV), gains.reshape(-1, NODE_DEV))


def halo_kernel(
    lower, upper, e_in, h_in, coef_in, loss_in, e_xy, e_z, h, media, first, second, sems,
):
    copies, copy = copier(sems)
    targets = [
        e_xy.at[0], e_xy.at[1], e_z, h.at[0], h.at[1], h.at[2], media.at[0], media.at[1],
    ]
    for part, source in enumerate(sources_of(e_in, h_in, coef_in, loss_in)):
        given = pl.ds(part * DEPTH, DEPTH)
        copy(source, targets[part].at[pl.ds(DEPTH, CZ)])
        copy(lower.at[given], targets[part].at[pl.ds(0, DEPTH)])
        copy(upper.at[given], targets[part].at[pl.ds(DEPTH + CZ, DEPTH)])
    for job in copies:
        job.wait()
    for swap, stack in enumerate((first, second)):
        write_rows(stack, targets[:4] + [targets[5]], swap)

    @pl.loop(0, LAYERS)
    def _(layer):
        media[1, layer] = 1.0 - media[1, layer]


def samples_kernel(found, columns, e_z, media, sample, coef, picked):
    @pl.loop(0, found[COUNT])
    def _(group):
        part = pl.ds(pl.multiple_of(group * GROUP, GROUP), GROUP)
        _, place, _ = columns_at(columns, part)
        sample[part, :] = gather_cells(e_z, found, group, place, picked)
        coef[part, :] = gather_cells(media.at[0], found, group, place, picked)


def gather_cells(source, found, group, place, picked):
    for port in range(GROUP):
        spot = found[group * GROUP + port]
        picked[port : port + 1, :] = source[spot // TALL, pl.ds(spot % TALL, 1), :]
    return pick(picked[...], place)


def halo(lower, upper, e_in, h_in, coef, loss):
    return pl.pallas_call(
        halo_kernel,
        name="halo",
        out_shape=(
            onchip((2,) + CUBE),
            onchip(CUBE),
            onchip((3,) + CUBE),
            onchip((2,) + CUBE),
            stack_of(5),
            stack_of(5),
        ),
        in_specs=[HBM] * 6,
        out_specs=(VM,) * 6,
        scratch_shapes=[DMA((24,))],
        compiler_params=params(),
    )(*map(away, (lower, upper, e_in, h_in, coef, loss)))


def samples(found, columns, e_z, media):
    return pl.pallas_call(
        samples_kernel,
        name="samples",
        out_shape=(onchip((REACH, 1)), onchip((REACH, 1))),
        in_specs=[SM, VM, VM, VM],
        out_specs=(VM, VM),
        scratch_shapes=[pltpu.VMEM((GROUP, NX), f32)],
        compiler_params=params(),
    )(found, columns, keep(e_z), keep(media))


def field_kernel(
    step, base, *refs
):
    first, second, sent_first, sent_second = refs[:4]
    edge_in, media, e_xy, e_z, h, to_xy, to_z, to_h, edge, beyond_rows = refs[4:]
    even = lax.axis_index("gy") % 2 == 0
    low_z = jnp.where(lax.axis_index("gz") > 0, time_step, 0.0)
    low_y = jnp.where(lax.axis_index("gy") > 0, time_step, 0.0)
    lane = lanes_of(TALL, NX)
    last_lane, first_lane = lane == NX - 1, lane == 0
    row = lax.broadcasted_iota(jnp.int32, (TALL, NX), 0)
    last_row, first_row = row == TALL - 1, row == 0

    def next_x(value):
        return jnp.where(last_lane, 0.0, pltpu.roll(value, NX - 1, 1))

    def prior_x(value):
        return jnp.where(first_lane, 0.0, pltpu.roll(value, 1, 1))

    def next_y(value, beyond):
        return jnp.where(last_row, beyond, pltpu.roll(value, TALL - 1, 0))

    def prior_y(value, beyond):
        return jnp.where(first_row, beyond, pltpu.roll(value, 1, 0))

    span = pl.ds(0, LAYERS)

    def behind(slot, part=span):
        return jnp.where(even, second[slot, part, :], first[slot, part, :])

    for slot, kind in enumerate((0, 2)):
        beyond_rows[slot, span, :] = jnp.where(even, first[kind, span, :], second[kind, span, :])
    near_x, near_z = (
        jnp.where(even, sent_second[kind, span, :], sent_first[kind, span, :]) for kind in (0, 2)
    )
    out_x, out_y, out_z = behind(0), behind(1), behind(2)
    out_y_above = behind(1, pl.ds(1, LAYERS))
    tall_lane = lanes_of(LAYERS, NX)
    out_y_next = jnp.where(tall_lane == NX - 1, 0.0, pltpu.roll(out_y, NX - 1, 1))
    if base:
        edge_x, edge_z = behind(base), behind(base + 1)
    else:
        edge_x, edge_z = edge_in[0, span, :], edge_in[1, span, :]
    edge[0, span, :] = edge_x - low_y * ((near_z - out_z) - (out_y_above - out_y))
    edge[1, span, :] = edge_z - low_y * ((out_y_next - out_y) - (near_x - out_x))

    def magnetic(layer):
        e_x, e_y, e_zz = e_xy[0, layer], e_xy[1, layer], e_z[layer]
        rate = jnp.where(layer < DEPTH, low_z, time_step)
        beyond = pl.ds(layer, 1)
        curl_x = (next_y(e_zz, beyond_rows[1, beyond, :]) - e_zz) - (e_xy[1, layer + 1] - e_y)
        curl_y = (e_xy[0, layer + 1] - e_x) - (next_x(e_zz) - e_zz)
        curl_z = (next_x(e_y) - e_y) - (next_y(e_x, beyond_rows[0, beyond, :]) - e_x)
        return (h[0, layer] - rate * curl_x, h[1, layer] - rate * curl_y, h[2, layer] - rate * curl_z)

    def electric(layer):
        h_x, h_y, h_z = to_h[0, layer], to_h[1, layer], to_h[2, layer]
        coef, kept = media[0, layer], media[1, layer]
        beyond = pl.ds(layer, 1)
        back_x = (h_z - prior_y(h_z, edge[1, beyond, :])) - (h_y - to_h[1, layer - 1])
        back_y = (h_x - to_h[0, layer - 1]) - (h_z - prior_x(h_z))
        back_z = (h_y - prior_x(h_y)) - (h_x - prior_y(h_x, edge[0, beyond, :]))
        return (
            kept * e_xy[0, layer] + coef * back_x,
            kept * e_xy[1, layer] + coef * back_y,
            kept * e_z[layer] + coef * back_z,
        )

    def put_h(layer, values):
        to_h[0, layer], to_h[1, layer], to_h[2, layer] = values

    def put_e(layer, values):
        to_xy[0, layer], to_xy[1, layer], to_z[layer] = values

    put_h(step - 1, magnetic(step - 1))
    put_h(step, magnetic(step))
    last = LAYERS - step - 1

    electric_values = electric(step)
    put_h(step + 1, magnetic(step + 1))
    put_e(step, electric_values)

    @pl.loop(step + 1, last, step=2)
    def _(layer):
        electric_values = electric(layer)
        magnetic_values = magnetic(layer + 1)
        magnetic_above = magnetic(layer + 2)
        put_e(layer, electric_values)
        put_h(layer + 1, magnetic_values)
        electric_above = electric(layer + 1)
        put_h(layer + 2, magnetic_above)
        put_e(layer + 1, electric_above)

    put_e(last, electric(last))


def field(step, came, sent, edge, media, e_xy, e_z, h):
    first = edge is None
    return pl.pallas_call(
        functools.partial(field_kernel, step, 3 if first else 0),
        name="field",
        out_shape=(onchip((2,) + CUBE), onchip(CUBE), onchip((3,) + CUBE), onchip((2, STACK, NX))),
        in_specs=[VM] * 9,
        out_specs=(VM,) * 4,
        scratch_shapes=[pltpu.VMEM((2, STACK, NX), f32)],
        compiler_params=params(),
    )(
        *came, *sent, came[0] if first else keep(edge),
        keep(media), keep(e_xy), keep(e_z), keep(h),
    )


def solve(stride, arrived, off_cols, volts, m_off, m_diag, m_inv):
    lane = lanes_of(1, NODE_DEV)
    halves = []
    for j in range(NB_DEV):
        pieces = []
        for half in range(OFF // 2):
            total = None
            for side in range(2):
                column = off_cols[j, half * 2 + side]
                row = arrived[pl.ds(column // NB_DEV * stride, 1), :]
                row = jnp.where(column % NB_DEV == side, row, pltpu.roll(row, BS, 1))
                row = jnp.where((lane < BS) == (side == 0), row, 0.0)
                total = row if total is None else total + row
            pieces.append(jnp.broadcast_to(total, (BS, NODE_DEV)))
        halves.append(pieces)
    first = jnp.concatenate([halves[0][0], halves[1][0]], axis=0)
    second = jnp.concatenate([halves[0][1], halves[1][1]], axis=0)
    product = m_off[:, 0:NODE_DEV] * first + m_off[:, NODE_DEV : 2 * NODE_DEV] * second
    offsum = jnp.sum(product, axis=1, keepdims=True)
    kind = row_kind(arrived.shape, stride)
    inject = jnp.sum(jnp.where(kind == 1, arrived[...], 0.0), axis=0, keepdims=True)
    start = volts[...]
    target = charge_scale * start + inject
    diagonal = lax.broadcasted_iota(jnp.int32, (NODE_DEV, NODE_DEV), 0) == lanes_of(NODE_DEV, NODE_DEV)
    iterate = start
    for newton_round in range(NEWTON):
        local = diode_weight * jnp.tanh(iterate) - target
        terms = m_diag[...] * iterate + jnp.where(diagonal, local, 0.0)
        resid = jnp.sum(terms, axis=1, keepdims=True) + offsum
        iterate = iterate - jnp.sum(m_inv[...] * resid, axis=0, keepdims=True)
    return iterate


def apply_ports(stride, table, arrived, columns, sample, coef, e_z, near_rows, deltas):
    @pl.loop(0, table[COUNT])
    def _(group):
        first = group * GROUP
        part = pl.ds(pl.multiple_of(first, GROUP), GROUP)
        for port in range(GROUP):
            near_at = table[NODES + first + port] * stride
            near_rows[port : port + 1, :] = arrived[pl.ds(near_at, 1), :]
        gain, place, lane = columns_at(columns, part)
        current = gain * (sample[part, :] - pick(near_rows[...], lane))
        deltas[...] = spread(-coef[part, :] * current, place, NX)
        for port in range(GROUP):
            spot = table[first + port]
            layer, row = spot // TALL, pl.ds(spot % TALL, 1)
            e_z[layer, row, :] = e_z[layer, row, :] + deltas[port : port + 1, :]


def ports_kernel(
    stride, table, arrived, columns, sample, coef, e_xy, e_in, e_z, first, near_rows, deltas,
):
    e_z[...] = e_in[...]
    apply_ports(stride, table, arrived, columns, sample, coef, e_z, near_rows, deltas)
    write_rows(first, (e_xy.at[0], e_xy.at[1], e_z), 0)


def ports(table, arrived, columns, sample, coef, e_xy, e_z):
    return pl.pallas_call(
        functools.partial(ports_kernel, arrived.shape[0] // ND),
        name="ports",
        out_shape=(onchip(CUBE), stack_of(3)),
        in_specs=[SM] + [VM] * 6,
        out_specs=(VM, VM),
        scratch_shapes=[pltpu.VMEM((GROUP, NODE_DEV), f32), pltpu.VMEM((GROUP, NX), f32)],
        compiler_params=params(),
    )(table, arrived, columns, keep(sample), keep(coef), keep(e_xy), keep(e_z))


def second_kernel(e_xy, e_z, after, second):
    write_rows(second, (e_xy.at[0], e_xy.at[1], e_z), 1)


def second_rows(e_xy, e_z, after):
    return pl.pallas_call(
        second_kernel,
        name="second",
        out_shape=stack_of(3),
        in_specs=[VM, VM, ANY],
        out_specs=VM,
        compiler_params=params(),
    )(keep(e_xy), keep(e_z), after)


def circuit_kernel(
    stride, table, off_cols, arrived, columns, volts, m_off, m_diag, m_inv, e_z, after,
    out, volts_out, sample_out, picked, spread_rows,
):
    @pl.loop(0, table[COUNT])
    def _(group):
        part = pl.ds(pl.multiple_of(group * GROUP, GROUP), GROUP)
        _, place, _ = columns_at(columns, part)
        sample_out[part, :] = gather_cells(e_z, table, group, place, picked)

    solved = solve(stride, arrived, off_cols, volts, m_off, m_diag, m_inv)
    volts_out[...] = solved
    own = slice(0, PORT_DEV)
    gain, _, lane = columns_at(columns, own)
    spread_rows[...] = spread(gain * sample_out[own, :], lane, NODE_DEV)
    out[...] = jnp.where(row_kind(out.shape, 2) == 0, solved, 0.0)
    add_rows(out, 2, [table[NODES + port] for port in range(PORT_DEV)], spread_rows)


def circuit(table, off_cols, arrived, columns, volts, mats, e_z, after):
    return pl.pallas_call(
        functools.partial(circuit_kernel, arrived.shape[0] // ND),
        name="circuit",
        out_shape=(onchip((2 * ND, NODE_DEV)), onchip((1, NODE_DEV)), onchip((REACH, 1))),
        in_specs=[SM, SM] + [VM] * 7 + [ANY],
        out_specs=(VM,) * 3,
        scratch_shapes=[pltpu.VMEM((GROUP, NX), f32), pltpu.VMEM((PORT_DEV, NODE_DEV), f32)],
        compiler_params=params(),
    )(table, off_cols, arrived, columns, volts, *[keep(mat) for mat in mats], keep(e_z), after)


def finish_kernel(
    stride, table, off_cols, arrived, columns, sample, coef, volts, m_off, m_diag, m_inv, e_xy, e_in, h,
    e_out, h_out, volts_out, e_z, near_rows, deltas, sems,
):
    copies, copy = copier(sems)
    layers = pl.ds(DEPTH, CZ)
    for k in range(3):
        copy(h.at[k, layers], h_out.at[k])
    for k in range(2):
        copy(e_xy.at[k, layers], e_out.at[k])
    e_z[...] = e_in[...]
    apply_ports(stride, table, arrived, columns, sample, coef, e_z, near_rows, deltas)
    copy(e_z.at[layers], e_out.at[2])
    volts_out[...] = solve(stride, arrived, off_cols, volts, m_off, m_diag, m_inv)
    for job in copies:
        job.wait()


def finish(table, off_cols, arrived, columns, sample, coef, volts, mats, e_xy, e_z, h):
    return pl.pallas_call(
        functools.partial(finish_kernel, arrived.shape[0] // ND),
        name="finish",
        out_shape=(
            jax.ShapeDtypeStruct((3, CZ, CY, NX), f32),
            jax.ShapeDtypeStruct((3, CZ, CY, NX), f32),
            jax.ShapeDtypeStruct((1, NODE_DEV), f32),
        ),
        in_specs=[SM, SM] + [VM] * 11,
        out_specs=(HBM, HBM, VM),
        scratch_shapes=[
            pltpu.VMEM(CUBE, f32),
            pltpu.VMEM((GROUP, NODE_DEV), f32),
            pltpu.VMEM((GROUP, NX), f32),
            DMA((6,)),
        ],
        compiler_params=params(),
    )(
        table, off_cols, arrived, columns, keep(sample), keep(coef), volts,
        *[keep(mat) for mat in mats], keep(e_xy), keep(e_z), keep(h),
    )


def shifted(value, axis, steps):
    count = lax.axis_size(axis)
    first, last = (max(0, -steps), min(count, count - steps))
    return lax.ppermute(value, axis, [(source, source + steps) for source in range(first, last)])


def swapped(value, axis, start):
    count = lax.axis_size(axis)
    pairs = [(low, low + 1) for low in range(start, count - 1, 2)]
    return lax.ppermute(value, axis, pairs + [(high, low) for low, high in pairs])


def exchange(value):
    return lax.all_to_all(value, ("gz", "gy"), 0, 0, tiled=True)


def body(
    e_field,
    h_field,
    e_coef,
    e_loss,
    port_cell,
    port_node,
    port_gain,
    diag_blocks,
    inv_blocks,
    off_blocks,
    off_cols,
    volts_init,
):
    n_gz, n_gy = lax.axis_size("gz"), lax.axis_size("gy")
    grids = (e_field, h_field, e_coef, e_loss)
    volts = volts_init.reshape(1, NODE_DEV)
    up = slab_of(True, grids, volts)
    lower = shifted(up, "gz", 1)
    down = slab_of(False, grids, up)
    upper = shifted(down, "gz", -1)
    out = begin(n_gy, port_cell, port_node, port_gain, e_field, volts, down)
    arrived = exchange(out)
    lower, upper, arrived = lax.optimization_barrier((lower, upper, arrived))
    mats = matrices(diag_blocks, inv_blocks, off_blocks)
    e_xy, e_z, h, media, first, second = halo(lower, upper, *grids)
    found, columns = plan(n_gz, n_gy, arrived, port_node, port_gain)
    table = jnp.concatenate([found[0], found[1], found[7, 0:1]])
    sample, coef = samples(table, columns, e_z, media)
    edge = None
    for step in range(1, STEPS + 1):
        came_first = swapped(first, "gy", 0)
        if step > 1:
            out, volts, sample = circuit(table, off_cols, arrived, columns, volts, mats, e_z, first)
            second = second_rows(e_xy, e_z, out)
        came_second = swapped(second, "gy", 1)
        if step > 1:
            out, came_first = lax.optimization_barrier((out, came_first))
            arrived = exchange(out)
            arrived, e_z = lax.optimization_barrier((arrived, e_z))
        came, sent = (came_first, came_second), (first, second)
        e_xy, e_z, h, edge = field(step, came, sent, edge, media, e_xy, e_z, h)
        if step < STEPS:
            e_z, first = ports(table, arrived, columns, sample, coef, e_xy, e_z)
        else:
            e_end, h_end, volts = finish(
                table, off_cols, arrived, columns, sample, coef, volts, mats, e_xy, e_z, h
            )
    return e_end, h_end, volts.reshape(-1)


def solution(mesh):
    placed = (
        P(None, "gz", "gy", None),
        P(None, "gz", "gy", None),
        P("gz", "gy", None),
        P("gz", "gy", None),
        P(("gz", "gy")),
        P(),
        P(),
        P(("gz", "gy"), None, None),
        P(("gz", "gy"), None, None),
        P(("gz", "gy"), None, None, None),
        P(("gz", "gy"), None),
        P(("gz", "gy")),
    )
    return jax.shard_map(
        body,
        mesh=mesh,
        in_specs=placed,
        out_specs=(P(None, "gz", "gy", None), P(None, "gz", "gy", None), P(("gz", "gy"))),
        check_vma=False,
    )
```

```python
import functools

import jax
import jax.numpy as jnp
from jax import lax
from jax.experimental import pallas as pl
from jax.experimental.pallas import tpu as pltpu
from jax.sharding import PartitionSpec as P

STEPS = 5
NEWTON = 2
BS = 64
NB_DEV = 2
OFF = 4
PORT_DEV = 32
GROUP = 16
ND = 128
NODE_DEV = NB_DEV * BS
DEPTH = 5
CZ, CY, NX = 32, 16, 256
LAYERS = CZ + 2 * DEPTH
PAD = 0
TALL = CY
STACK = 48
PARTS = 8
SIDES = ((0, 0), (-1, 0), (1, 0))
REACH = len(SIDES) * PORT_DEV
NODES, COUNT = REACH, 2 * REACH

time_step = 0.55
charge_scale = 4.0
diode_weight = 0.5

f32 = jnp.float32
VM = pl.BlockSpec(memory_space=pltpu.VMEM)
SM = pl.BlockSpec(memory_space=pltpu.SMEM)
HBM = pl.BlockSpec(memory_space=pltpu.HBM)
ANY = pl.BlockSpec(memory_space=pl.ANY)
DMA = pltpu.SemaphoreType.DMA
CUBE = (LAYERS, TALL, NX)


def onchip(shape):
    return pltpu.VMEM(shape, f32)


def keep(value):
    return pltpu.with_memory_space_constraint(value, pltpu.VMEM)


def away(value):
    return pltpu.with_memory_space_constraint(value, pltpu.HBM)


def params():
    return pltpu.CompilerParams(vmem_limit_bytes=12 << 20)


def lanes_of(count, width):
    return lax.broadcasted_iota(jnp.int32, (count, width), 1)


def pick(rows, lane):
    hit = lanes_of(rows.shape[0], rows.shape[1]) == lane
    return jnp.sum(jnp.where(hit, rows, 0.0), axis=1, keepdims=True)


def spread(column, lane, width):
    hit = lanes_of(column.shape[0], width) == lane
    return jnp.where(hit, column, 0.0)


def columns_at(columns, part):
    block = columns[part, :]
    return block[:, 2:3], block[:, 3:4].astype(jnp.int32), block[:, 4:5].astype(jnp.int32)


def row_kind(shape, stride):
    return lax.broadcasted_iota(jnp.int32, shape, 0) % stride


def add_rows(out, stride, devices, rows_ref):
    for port, device in enumerate(devices):
        spot = pl.ds(device * stride + 1, 1)
        out[spot, :] = out[spot, :] + rows_ref[port : port + 1, :]


def copier(sems):
    copies = []

    def copy(source, target):
        job = pltpu.make_async_copy(source, target, sems.at[len(copies)])
        job.start()
        copies.append(job)

    return copies, copy


def sources_of(e_in, h_in, coef_in, loss_in):
    return [e_in.at[k] for k in range(3)] + [h_in.at[k] for k in range(3)] + [coef_in, loss_in]


def write_rows(stack, sources, swap):
    even = lax.axis_index("gy") % 2 == 0
    row = jnp.where(even, CY - 1, 0) if swap == 0 else jnp.where(even, 0, CY - 1)
    for slot, source in enumerate(sources):
        for layer in range(LAYERS):
            stack[slot, layer : layer + 1, :] = source[layer, pl.ds(row, 1), :]
        stack[slot, LAYERS:STACK, :] = jnp.zeros((STACK - LAYERS, NX), f32)


def stack_of(count):
    return jax.ShapeDtypeStruct((count, STACK, NX), f32)


def slab_kernel(swap, e_in, h_in, coef_in, loss_in, after, slab, sems):
    copies, copy = copier(sems)
    even = lax.axis_index("gz") % 2 == 0
    top, bottom = CZ - DEPTH, 0
    start = jnp.where(even, top, bottom) if swap == 0 else jnp.where(even, bottom, top)
    layers = pl.ds(start, DEPTH)
    for part, source in enumerate(sources_of(e_in, h_in, coef_in, loss_in)):
        copy(source.at[layers], slab.at[pl.ds(part * DEPTH, DEPTH)])
    for job in copies:
        job.wait()


def slab_of(swap, grids, after):
    return pl.pallas_call(
        functools.partial(slab_kernel, swap),
        name="slab",
        out_shape=jax.ShapeDtypeStruct((PARTS * DEPTH, CY, NX), f32),
        in_specs=[HBM] * 4 + [ANY],
        out_specs=VM,
        scratch_shapes=[DMA((PARTS,))],
        compiler_params=params(),
    )(*map(away, grids), after)


def begin_kernel(
    n_gy, cells, nodes, gains, e_in, cell_row, volts, after, out, e_z, picked, hits, rows_ref, sem,
):
    load = pltpu.make_async_copy(e_in.at[2], e_z, sem)
    load.start()
    first = (lax.axis_index("gz") * n_gy + lax.axis_index("gy")) * PORT_DEV
    wide, narrow = lanes_of(1, NX), lanes_of(1, NODE_DEV)
    own_nodes = [nodes[first + port] for port in range(PORT_DEV)]
    for port, node in enumerate(own_nodes):
        hits[port : port + 1, :] = jnp.where(narrow == node % NODE_DEV, 1.0, 0.0)
    kind = row_kind(out.shape, 4)
    rows_ref[0:1, :] = jnp.zeros((1, NODE_DEV), f32)
    rows_ref[0:1, 0:PORT_DEV] = cell_row[...].astype(f32)
    out[...] = jnp.where(kind == 0, volts[...], jnp.where(kind == 2, rows_ref[0:1, :], 0.0))

    load.wait()
    for port in range(PORT_DEV):
        cell = cells[port]
        line = cell // NX
        value = e_z[line // CY, pl.ds(line % CY, 1), :] * gains[first + port]
        picked[port : port + 1, :] = jnp.where(wide == cell % NX, value, 0.0)
    rows_ref[...] = hits[...] * jnp.sum(picked[...], axis=1, keepdims=True)
    add_rows(out, 4, [node // NODE_DEV for node in own_nodes], rows_ref)


def begin(n_gy, cells, nodes, gains, e_in, volts, after):
    return pl.pallas_call(
        functools.partial(begin_kernel, n_gy),
        name="begin",
        out_shape=jax.ShapeDtypeStruct((4 * ND, NODE_DEV), f32),
        in_specs=[SM, SM, SM, HBM, VM, VM, ANY],
        out_specs=VM,
        scratch_shapes=[
            pltpu.VMEM((CZ, CY, NX), f32),
            pltpu.VMEM((PORT_DEV, NX), f32),
            pltpu.VMEM((PORT_DEV, NODE_DEV), f32),
            pltpu.VMEM((PORT_DEV, NODE_DEV), f32),
            DMA,
        ],
        compiler_params=params(),
    )(cells, nodes, gains, away(e_in), cells.reshape(1, -1), volts, after)


def matrices_kernel(diag, inv, off, m_off, m_diag, m_inv):
    m_diag[...] = jnp.zeros_like(m_diag)
    m_inv[...] = jnp.zeros_like(m_inv)
    for j in range(NB_DEV):
        part = slice(j * BS, (j + 1) * BS)
        m_diag[part, part] = diag[j]
        m_inv[part, part] = inv[j].T
        for k in range(OFF):
            m_off[part, k * BS : (k + 1) * BS] = off[j, k]


def matrices(diag, inv, off):
    square = onchip((NODE_DEV, NODE_DEV))
    return pl.pallas_call(
        matrices_kernel,
        name="matrices",
        out_shape=(onchip((NODE_DEV, OFF * BS)), square, square),
        in_specs=[VM, VM, VM],
        out_specs=(VM, VM, VM),
        compiler_params=params(),
    )(diag, inv, off)


def plan_kernel(n_gz, n_gy, arrived, nodes, gains, found, columns, facts):
    gz, gy = lax.axis_index("gz"), lax.axis_index("gy")
    lane = lanes_of(1, NODE_DEV)
    width = NODE_DEV // PORT_DEV
    facts[...] = jnp.zeros_like(facts)
    for group, (side_z, side_y) in enumerate(SIDES):
        at_z, at_y = gz + side_z, gy + side_y
        exists = (at_z >= 0) & (at_z < n_gz) & (at_y >= 0) & (at_y < n_gy)
        device = jnp.where(exists, at_z * n_gy + at_y, 0)
        slot = group % width
        turn = (slot - device % width + width) % width * PORT_DEV
        row = pl.ds(device // width, 1)
        node, gain = pltpu.roll(nodes[row, :], turn, 1), pltpu.roll(gains[row, :], turn, 1)
        cell = pltpu.roll(arrived[pl.ds(4 * device + 2, 1), :], slot * PORT_DEV, 1).astype(jnp.int32)
        layer = cell // (CY * NX) + (side_z * CZ + DEPTH)
        line = (cell // NX) % CY + (side_y * CY + PAD)
        valid = (layer >= 1) & (layer < LAYERS - 1)
        valid &= (line > PAD - DEPTH) & (line < PAD + CY + DEPTH - 1)
        valid &= (lane // PORT_DEV == slot) & (jnp.where(exists, 1, 0) > 0)
        values = (layer * TALL + line, node // NODE_DEV, gain, cell % NX, node % NODE_DEV, 1)
        part = slice(group // width * NODE_DEV, (group // width + 1) * NODE_DEV)
        for kind, value in enumerate(values):
            fact = jnp.where(valid, jnp.asarray(value).astype(f32), 0.0)
            facts[kind : kind + 1, part] = facts[kind : kind + 1, part] + fact

    used = facts[5:6, :]
    total = used.shape[1]
    upper = lax.broadcasted_iota(jnp.int32, (total, total), 0) <= lanes_of(total, total)
    ones = jnp.broadcast_to(used, (8, total))
    order = jnp.dot(ones, upper.astype(f32), preferred_element_type=f32)[0:1, :] - 1.0
    spot = lax.broadcasted_iota(jnp.int32, (REACH, total), 0)
    chosen = jnp.where((spot == order.astype(jnp.int32)) & (used > 0.0), 1.0, 0.0)
    across = (((1,), (1,)), ((), ()))
    columns[...] = lax.dot_general(
        chosen, facts[...], across, precision=lax.Precision.HIGHEST, preferred_element_type=f32
    )
    rows = lax.dot_general(
        facts[...], chosen, across, precision=lax.Precision.HIGHEST, preferred_element_type=f32
    )
    count = jnp.sum(used, axis=1, keepdims=True)
    groups = ((count + (GROUP - 1)) * (1.0 / GROUP)).astype(jnp.int32)
    kind = lax.broadcasted_iota(jnp.int32, rows.shape, 0)
    unused = (kind == 0) & (lanes_of(8, REACH) >= count.astype(jnp.int32))
    whole = jnp.where(unused, PAD, (rows + 0.5).astype(jnp.int32))
    found[...] = jnp.where(kind == 7, groups, whole)


def plan(n_gz, n_gy, arrived, nodes, gains):
    lanes = -(-REACH // NODE_DEV) * NODE_DEV
    return pl.pallas_call(
        functools.partial(plan_kernel, n_gz, n_gy),
        name="plan",
        out_shape=(
            jax.ShapeDtypeStruct((8, REACH), jnp.int32),
            jax.ShapeDtypeStruct((REACH, 8), f32),
        ),
        in_specs=[VM, VM, VM],
        out_specs=(VM, VM),
        scratch_shapes=[pltpu.VMEM((8, lanes), f32)],
        compiler_params=params(),
    )(arrived, nodes.reshape(-1, NODE_DEV), gains.reshape(-1, NODE_DEV))


def halo_kernel(
    came_first, came_second, e_in, h_in, coef_in, loss_in,
    e_xy, e_z, h, media, first, second, sems,
):
    copies, copy = copier(sems)
    even, high = lax.axis_index("gz") % 2 == 0, DEPTH + CZ
    targets = [
        e_xy.at[0], e_xy.at[1], e_z, h.at[0], h.at[1], h.at[2], media.at[0], media.at[1],
    ]
    for part, source in enumerate(sources_of(e_in, h_in, coef_in, loss_in)):
        given = pl.ds(part * DEPTH, DEPTH)
        copy(source, targets[part].at[pl.ds(DEPTH, CZ)])
        copy(came_first.at[given], targets[part].at[pl.ds(jnp.where(even, high, 0), DEPTH)])
        copy(came_second.at[given], targets[part].at[pl.ds(jnp.where(even, 0, high), DEPTH)])
    for job in copies:
        job.wait()
    for swap, stack in enumerate((first, second)):
        write_rows(stack, targets[:4] + [targets[5]], swap)

    @pl.loop(0, LAYERS)
    def _(layer):
        media[1, layer] = 1.0 - media[1, layer]


def samples_kernel(found, columns, e_z, media, sample, coef, picked):
    @pl.loop(0, found[COUNT])
    def _(group):
        part = pl.ds(pl.multiple_of(group * GROUP, GROUP), GROUP)
        _, place, _ = columns_at(columns, part)
        sample[part, :] = gather_cells(e_z, found, group, place, picked)
        coef[part, :] = gather_cells(media.at[0], found, group, place, picked)


def gather_cells(source, found, group, place, picked):
    for port in range(GROUP):
        spot = found[group * GROUP + port]
        picked[port : port + 1, :] = source[spot // TALL, pl.ds(spot % TALL, 1), :]
    return pick(picked[...], place)


def halo(lower, upper, e_in, h_in, coef, loss):
    return pl.pallas_call(
        halo_kernel,
        name="halo",
        out_shape=(
            onchip((2,) + CUBE),
            onchip(CUBE),
            onchip((3,) + CUBE),
            onchip((2,) + CUBE),
            stack_of(5),
            stack_of(5),
        ),
        in_specs=[HBM] * 6,
        out_specs=(VM,) * 6,
        scratch_shapes=[DMA((24,))],
        compiler_params=params(),
    )(*map(away, (lower, upper, e_in, h_in, coef, loss)))


def samples(found, columns, e_z, media):
    return pl.pallas_call(
        samples_kernel,
        name="samples",
        out_shape=(onchip((REACH, 1)), onchip((REACH, 1))),
        in_specs=[SM, VM, VM, VM],
        out_specs=(VM, VM),
        scratch_shapes=[pltpu.VMEM((GROUP, NX), f32)],
        compiler_params=params(),
    )(found, columns, keep(e_z), keep(media))


def field_kernel(
    step, base, *refs
):
    first, second, sent_first, sent_second = refs[:4]
    edge_in, media, e_xy, e_z, h, to_xy, to_z, to_h, edge, beyond_rows = refs[4:]
    even = lax.axis_index("gy") % 2 == 0
    low_z = jnp.where(lax.axis_index("gz") > 0, time_step, 0.0)
    low_y = jnp.where(lax.axis_index("gy") > 0, time_step, 0.0)
    lane = lanes_of(TALL, NX)
    last_lane, first_lane = lane == NX - 1, lane == 0
    row = lax.broadcasted_iota(jnp.int32, (TALL, NX), 0)
    last_row, first_row = row == TALL - 1, row == 0

    def next_x(value):
        return jnp.where(last_lane, 0.0, pltpu.roll(value, NX - 1, 1))

    def prior_x(value):
        return jnp.where(first_lane, 0.0, pltpu.roll(value, 1, 1))

    def next_y(value, beyond):
        return jnp.where(last_row, beyond, pltpu.roll(value, TALL - 1, 0))

    def prior_y(value, beyond):
        return jnp.where(first_row, beyond, pltpu.roll(value, 1, 0))

    span = pl.ds(0, LAYERS)

    def behind(slot, part=span):
        return jnp.where(even, second[slot, part, :], first[slot, part, :])

    for slot, kind in enumerate((0, 2)):
        beyond_rows[slot, span, :] = jnp.where(even, first[kind, span, :], second[kind, span, :])
    near_x, near_z = (
        jnp.where(even, sent_second[kind, span, :], sent_first[kind, span, :]) for kind in (0, 2)
    )
    out_x, out_y, out_z = behind(0), behind(1), behind(2)
    out_y_above = behind(1, pl.ds(1, LAYERS))
    tall_lane = lanes_of(LAYERS, NX)
    out_y_next = jnp.where(tall_lane == NX - 1, 0.0, pltpu.roll(out_y, NX - 1, 1))
    if base:
        edge_x, edge_z = behind(base), behind(base + 1)
    else:
        edge_x, edge_z = edge_in[0, span, :], edge_in[1, span, :]
    edge[0, span, :] = edge_x - low_y * ((near_z - out_z) - (out_y_above - out_y))
    edge[1, span, :] = edge_z - low_y * ((out_y_next - out_y) - (near_x - out_x))

    def magnetic(layer):
        e_x, e_y, e_zz = e_xy[0, layer], e_xy[1, layer], e_z[layer]
        rate = jnp.where(layer < DEPTH, low_z, time_step)
        beyond = pl.ds(layer, 1)
        curl_x = (next_y(e_zz, beyond_rows[1, beyond, :]) - e_zz) - (e_xy[1, layer + 1] - e_y)
        curl_y = (e_xy[0, layer + 1] - e_x) - (next_x(e_zz) - e_zz)
        curl_z = (next_x(e_y) - e_y) - (next_y(e_x, beyond_rows[0, beyond, :]) - e_x)
        return (h[0, layer] - rate * curl_x, h[1, layer] - rate * curl_y, h[2, layer] - rate * curl_z)

    def electric(layer):
        h_x, h_y, h_z = to_h[0, layer], to_h[1, layer], to_h[2, layer]
        coef, kept = media[0, layer], media[1, layer]
        beyond = pl.ds(layer, 1)
        back_x = (h_z - prior_y(h_z, edge[1, beyond, :])) - (h_y - to_h[1, layer - 1])
        back_y = (h_x - to_h[0, layer - 1]) - (h_z - prior_x(h_z))
        back_z = (h_y - prior_x(h_y)) - (h_x - prior_y(h_x, edge[0, beyond, :]))
        return (
            kept * e_xy[0, layer] + coef * back_x,
            kept * e_xy[1, layer] + coef * back_y,
            kept * e_z[layer] + coef * back_z,
        )

    def put_h(layer, values):
        to_h[0, layer], to_h[1, layer], to_h[2, layer] = values

    def put_e(layer, values):
        to_xy[0, layer], to_xy[1, layer], to_z[layer] = values

    put_h(step - 1, magnetic(step - 1))
    put_h(step, magnetic(step))
    last = LAYERS - step - 1

    electric_values = electric(step)
    put_h(step + 1, magnetic(step + 1))
    put_e(step, electric_values)

    @pl.loop(step + 1, last, step=2)
    def _(layer):
        electric_values = electric(layer)
        magnetic_values = magnetic(layer + 1)
        magnetic_above = magnetic(layer + 2)
        put_e(layer, electric_values)
        put_h(layer + 1, magnetic_values)
        electric_above = electric(layer + 1)
        put_h(layer + 2, magnetic_above)
        put_e(layer + 1, electric_above)

    put_e(last, electric(last))


def field(step, came, sent, edge, media, e_xy, e_z, h):
    first = edge is None
    return pl.pallas_call(
        functools.partial(field_kernel, step, 3 if first else 0),
        name="field",
        out_shape=(onchip((2,) + CUBE), onchip(CUBE), onchip((3,) + CUBE), onchip((2, STACK, NX))),
        in_specs=[VM] * 9,
        out_specs=(VM,) * 4,
        scratch_shapes=[pltpu.VMEM((2, STACK, NX), f32)],
        compiler_params=params(),
    )(
        *came, *sent, came[0] if first else keep(edge),
        keep(media), keep(e_xy), keep(e_z), keep(h),
    )


def solve(stride, arrived, off_cols, volts, m_off, m_diag, m_inv):
    lane = lanes_of(1, NODE_DEV)
    halves = []
    for j in range(NB_DEV):
        pieces = []
        for half in range(OFF // 2):
            total = None
            for side in range(2):
                column = off_cols[j, half * 2 + side]
                row = arrived[pl.ds(column // NB_DEV * stride, 1), :]
                row = jnp.where(column % NB_DEV == side, row, pltpu.roll(row, BS, 1))
                row = jnp.where((lane < BS) == (side == 0), row, 0.0)
                total = row if total is None else total + row
            pieces.append(jnp.broadcast_to(total, (BS, NODE_DEV)))
        halves.append(pieces)
    first = jnp.concatenate([halves[0][0], halves[1][0]], axis=0)
    second = jnp.concatenate([halves[0][1], halves[1][1]], axis=0)
    product = m_off[:, 0:NODE_DEV] * first + m_off[:, NODE_DEV : 2 * NODE_DEV] * second
    offsum = jnp.sum(product, axis=1, keepdims=True)
    kind = row_kind(arrived.shape, stride)
    inject = jnp.sum(jnp.where(kind == 1, arrived[...], 0.0), axis=0, keepdims=True)
    start = volts[...]
    target = charge_scale * start + inject
    diagonal = lax.broadcasted_iota(jnp.int32, (NODE_DEV, NODE_DEV), 0) == lanes_of(NODE_DEV, NODE_DEV)
    iterate = start
    for newton_round in range(NEWTON):
        local = diode_weight * jnp.tanh(iterate) - target
        terms = m_diag[...] * iterate + jnp.where(diagonal, local, 0.0)
        resid = jnp.sum(terms, axis=1, keepdims=True) + offsum
        iterate = iterate - jnp.sum(m_inv[...] * resid, axis=0, keepdims=True)
    return iterate


def apply_ports(stride, table, arrived, columns, sample, coef, e_z, near_rows, deltas):
    @pl.loop(0, table[COUNT])
    def _(group):
        first = group * GROUP
        part = pl.ds(pl.multiple_of(first, GROUP), GROUP)
        for port in range(GROUP):
            near_at = table[NODES + first + port] * stride
            near_rows[port : port + 1, :] = arrived[pl.ds(near_at, 1), :]
        gain, place, lane = columns_at(columns, part)
        current = gain * (sample[part, :] - pick(near_rows[...], lane))
        deltas[...] = spread(-coef[part, :] * current, place, NX)
        for port in range(GROUP):
            spot = table[first + port]
            layer, row = spot // TALL, pl.ds(spot % TALL, 1)
            e_z[layer, row, :] = e_z[layer, row, :] + deltas[port : port + 1, :]


def ports_kernel(
    stride, table, arrived, columns, sample, coef, e_xy, e_in, e_z, first, near_rows, deltas,
):
    e_z[...] = e_in[...]
    apply_ports(stride, table, arrived, columns, sample, coef, e_z, near_rows, deltas)
    write_rows(first, (e_xy.at[0], e_xy.at[1], e_z), 0)


def ports(table, arrived, columns, sample, coef, e_xy, e_z):
    return pl.pallas_call(
        functools.partial(ports_kernel, arrived.shape[0] // ND),
        name="ports",
        out_shape=(onchip(CUBE), stack_of(3)),
        in_specs=[SM] + [VM] * 6,
        out_specs=(VM, VM),
        scratch_shapes=[pltpu.VMEM((GROUP, NODE_DEV), f32), pltpu.VMEM((GROUP, NX), f32)],
        compiler_params=params(),
    )(table, arrived, columns, keep(sample), keep(coef), keep(e_xy), keep(e_z))


def second_kernel(e_xy, e_z, after, second):
    write_rows(second, (e_xy.at[0], e_xy.at[1], e_z), 1)


def second_rows(e_xy, e_z, after):
    return pl.pallas_call(
        second_kernel,
        name="second",
        out_shape=stack_of(3),
        in_specs=[VM, VM, ANY],
        out_specs=VM,
        compiler_params=params(),
    )(keep(e_xy), keep(e_z), after)


def circuit_kernel(
    stride, table, off_cols, arrived, columns, volts, m_off, m_diag, m_inv, e_z, after,
    out, volts_out, sample_out, picked, spread_rows,
):
    @pl.loop(0, table[COUNT])
    def _(group):
        part = pl.ds(pl.multiple_of(group * GROUP, GROUP), GROUP)
        _, place, _ = columns_at(columns, part)
        sample_out[part, :] = gather_cells(e_z, table, group, place, picked)

    solved = solve(stride, arrived, off_cols, volts, m_off, m_diag, m_inv)
    volts_out[...] = solved
    own = slice(0, PORT_DEV)
    gain, _, lane = columns_at(columns, own)
    spread_rows[...] = spread(gain * sample_out[own, :], lane, NODE_DEV)
    out[...] = jnp.where(row_kind(out.shape, 2) == 0, solved, 0.0)
    add_rows(out, 2, [table[NODES + port] for port in range(PORT_DEV)], spread_rows)


def circuit(table, off_cols, arrived, columns, volts, mats, e_z, after):
    return pl.pallas_call(
        functools.partial(circuit_kernel, arrived.shape[0] // ND),
        name="circuit",
        out_shape=(onchip((2 * ND, NODE_DEV)), onchip((1, NODE_DEV)), onchip((REACH, 1))),
        in_specs=[SM, SM] + [VM] * 7 + [ANY],
        out_specs=(VM,) * 3,
        scratch_shapes=[pltpu.VMEM((GROUP, NX), f32), pltpu.VMEM((PORT_DEV, NODE_DEV), f32)],
        compiler_params=params(),
    )(table, off_cols, arrived, columns, volts, *[keep(mat) for mat in mats], keep(e_z), after)


def finish_kernel(
    stride, table, off_cols, arrived, columns, sample, coef, volts, m_off, m_diag, m_inv, e_xy, e_in, h,
    e_out, h_out, volts_out, e_z, near_rows, deltas, sems,
):
    copies, copy = copier(sems)
    layers = pl.ds(DEPTH, CZ)
    for k in range(3):
        copy(h.at[k, layers], h_out.at[k])
    for k in range(2):
        copy(e_xy.at[k, layers], e_out.at[k])
    e_z[...] = e_in[...]
    apply_ports(stride, table, arrived, columns, sample, coef, e_z, near_rows, deltas)
    copy(e_z.at[layers], e_out.at[2])
    volts_out[...] = solve(stride, arrived, off_cols, volts, m_off, m_diag, m_inv)
    for job in copies:
        job.wait()


def finish(table, off_cols, arrived, columns, sample, coef, volts, mats, e_xy, e_z, h):
    return pl.pallas_call(
        functools.partial(finish_kernel, arrived.shape[0] // ND),
        name="finish",
        out_shape=(
            jax.ShapeDtypeStruct((3, CZ, CY, NX), f32),
            jax.ShapeDtypeStruct((3, CZ, CY, NX), f32),
            jax.ShapeDtypeStruct((1, NODE_DEV), f32),
        ),
        in_specs=[SM, SM] + [VM] * 11,
        out_specs=(HBM, HBM, VM),
        scratch_shapes=[
            pltpu.VMEM(CUBE, f32),
            pltpu.VMEM((GROUP, NODE_DEV), f32),
            pltpu.VMEM((GROUP, NX), f32),
            DMA((6,)),
        ],
        compiler_params=params(),
    )(
        table, off_cols, arrived, columns, keep(sample), keep(coef), volts,
        *[keep(mat) for mat in mats], keep(e_xy), keep(e_z), keep(h),
    )


def swapped(value, axis, start):
    count = lax.axis_size(axis)
    pairs = [(low, low + 1) for low in range(start, count - 1, 2)]
    return lax.ppermute(value, axis, pairs + [(high, low) for low, high in pairs])


def exchange(value):
    return lax.all_to_all(value, ("gz", "gy"), 0, 0, tiled=True)


def body(
    e_field,
    h_field,
    e_coef,
    e_loss,
    port_cell,
    port_node,
    port_gain,
    diag_blocks,
    inv_blocks,
    off_blocks,
    off_cols,
    volts_init,
):
    n_gz, n_gy = lax.axis_size("gz"), lax.axis_size("gy")
    grids = (e_field, h_field, e_coef, e_loss)
    volts = volts_init.reshape(1, NODE_DEV)
    slab_first = slab_of(0, grids, volts)
    slab_came = swapped(slab_first, "gz", 0)
    slab_second = slab_of(1, grids, slab_first)
    slab_next = swapped(slab_second, "gz", 1)
    out = begin(n_gy, port_cell, port_node, port_gain, e_field, volts, slab_second)
    arrived = exchange(out)
    slab_came, slab_next, arrived = lax.optimization_barrier((slab_came, slab_next, arrived))
    mats = matrices(diag_blocks, inv_blocks, off_blocks)
    e_xy, e_z, h, media, first, second = halo(slab_came, slab_next, *grids)
    found, columns = plan(n_gz, n_gy, arrived, port_node, port_gain)
    table = jnp.concatenate([found[0], found[1], found[7, 0:1]])
    sample, coef = samples(table, columns, e_z, media)
    edge = None
    for step in range(1, STEPS + 1):
        came_first = swapped(first, "gy", 0)
        if step > 1:
            out, volts, sample = circuit(table, off_cols, arrived, columns, volts, mats, e_z, first)
            second = second_rows(e_xy, e_z, out)
        came_second = swapped(second, "gy", 1)
        if step > 1:
            out, came_first = lax.optimization_barrier((out, came_first))
            arrived = exchange(out)
            arrived, e_z = lax.optimization_barrier((arrived, e_z))
        came, sent = (came_first, came_second), (first, second)
        e_xy, e_z, h, edge = field(step, came, sent, edge, media, e_xy, e_z, h)
        if step < STEPS:
            e_z, first = ports(table, arrived, columns, sample, coef, e_xy, e_z)
        else:
            e_end, h_end, volts = finish(
                table, off_cols, arrived, columns, sample, coef, volts, mats, e_xy, e_z, h
            )
    return e_end, h_end, volts.reshape(-1)


def solution(mesh):
    placed = (
        P(None, "gz", "gy", None),
        P(None, "gz", "gy", None),
        P("gz", "gy", None),
        P("gz", "gy", None),
        P(("gz", "gy")),
        P(),
        P(),
        P(("gz", "gy"), None, None),
        P(("gz", "gy"), None, None),
        P(("gz", "gy"), None, None, None),
        P(("gz", "gy"), None),
        P(("gz", "gy")),
    )
    return jax.shard_map(
        body,
        mesh=mesh,
        in_specs=placed,
        out_specs=(P(None, "gz", "gy", None), P(None, "gz", "gy", None), P(("gz", "gy"))),
        check_vma=False,
    )
```
